32 devices in a mesh: dp: 8 (over y, x, core), mp: 4 (over z).
Axes of the slice: x: 2, y: 2, z: 4, core: 2. Of those that a mesh axis runs over, the one named last changes fastest.
Arguments:
- frames: bfloat16 [8192, 1024], P(('dp', 'mp')), may hold values from -6 to 6
- lengths: int32 [8, 6], P('dp'), may hold values from 1 to 682, 896 in all within a row
- w_qkv: bfloat16 [3, 1024, 1024], P(None, None, 'mp'), may hold values from -0.1875 to 0.1875
- w_attn_out: bfloat16 [1024, 1024], P('mp'), may hold values from -0.5 to 0.5
- w_in: bfloat16 [1024, 4096], P(None, 'mp'), may hold values from -0.1875 to 0.1875
- w_out: bfloat16 [4096, 1024], P('mp'), may hold values from -0.09375 to 0.09375
- gain_attn: float32 [1024], replicated, may hold values from 0.5 to 1.5
- gain_mlp: float32 [1024], replicated, may hold values from 0.5 to 1.5
- cotangent: bfloat16 [8192, 1024], P(('dp', 'mp')), may hold values from -6 to 6
Outputs:
- output: bfloat16 [8192, 1024], P(('dp', 'mp'))
- grad_frames: float32 [8192, 1024], P(('dp', 'mp'))
- grad_w_qkv: float32 [3, 1024, 1024], P(None, None, 'mp')
- grad_w_attn_out: float32 [1024, 1024], P('mp')
- grad_w_in: float32 [1024, 4096], P(None, 'mp')
- grad_w_out: float32 [4096, 1024], P('mp')
- grad_gain_attn: float32 [1024], replicated
- grad_gain_mlp: float32 [1024], replicated
The draws below stay inside these ranges and needn't reach their ends.
Inputs may be any that keep to these rules, and one draw needn't show every extreme that they name: `lengths`: each row holds the frame counts of the 6 items of one batch; they sum to 896 and the largest is exactly 682; the remaining frames of the batch are padding.
All inputs are finite; a program needn't handle non-finite values.
Results may differ from the reference program's by a relative error of at most 0.012.
Values may be sent and summed in bfloat16 or wider, within the bound.
A program may use at most 128 MiB of HBM per device.

```python
import math
import jax
import jax.numpy as jnp
import numpy as np
from jax import lax

D = 1024
HEADS = 16
HEAD = 64
FF = 4096
TOK_DEV = 1024
ITEMS = 6
MAXLEN = 682
BLOCK = 512
BATCHES = 8
TOKENS = 8192


def block_levels(own_key, shape, cuts, low, top_value):
    loudness = 1.0
    for axis_at, shards_of in cuts:
        heights = jax.random.uniform(jax.random.fold_in(jax.random.fold_in(own_key, 6), axis_at), (shards_of,), jnp.float32, low / len(cuts), top_value / len(cuts))
        loudness = loudness * jnp.repeat(jnp.exp(heights), shape[axis_at] // shards_of).reshape((-1,) + (1,) * (len(shape) - 1 - axis_at))
    return loudness


def length_profile(amount, total, most, skew):
    weights = [(1 << 20) // math.isqrt(grade ** skew) + 1 for grade in range(2, amount + 1)]
    spare, holding = total - most - (amount - 1), [1] * (amount - 1)
    while spare > 0:
        candidates = [i for i in range(amount - 1) if holding[i] < most]
        pool, remaining = sum([weights[i] for i in candidates]), spare
        for i in candidates:
            more = min(most - holding[i], max(1, remaining * weights[i] // pool), spare)
            holding[i] = holding[i] + more
            spare = spare - more
    return np.array([most] + holding)


def uneven(own_key, count, total, reach, skew):
    if count == 2:
        one = jax.random.randint(own_key, (), max(1, total - reach), min(reach, total - 1) + 1)
        return jnp.stack([one, total - one])
    sizes = jnp.asarray(length_profile(count, total, reach, skew), jnp.int32)
    couples = (count - 1) // 2
    donor, sink = sizes[1:1 + 2 * couples:2], sizes[2:2 + 2 * couples:2]
    room = jnp.minimum(donor - 1, reach - sink)
    moved = jax.random.randint(jax.random.fold_in(own_key, 1), (couples,), 0, 1 << 20) % (room + 1)
    sizes = sizes.at[1:1 + 2 * couples:2].set(donor - moved).at[2:2 + 2 * couples:2].set(sink + moved)
    return sizes[jax.random.permutation(jax.random.fold_in(own_key, 2), count)]


def gaussian(own_key, dims, width, limit, split=(), kind=jnp.bfloat16):
    drawn = width * jax.random.normal(own_key, dims, jnp.float32)
    if split:
        drawn = drawn * block_levels(own_key, dims, split, -0.22, 0.18)
    return jnp.clip(drawn, -limit, limit).astype(kind)


def setup_inputs(seed: int = 0) -> dict:
    seeds = jax.random.split(jax.random.key(seed), 10)
    return {
        "frames": gaussian(seeds[0], (TOKENS, D), 1.0, 6.0, ((0, 32),)),
        "lengths": jax.vmap(lambda own: uneven(own, ITEMS, TOK_DEV - TOK_DEV // 8, MAXLEN, 2))(jax.random.split(seeds[1], BATCHES)).reshape((BATCHES, ITEMS)).astype(jnp.int32),
        "w_qkv": gaussian(seeds[2], (3, D, D), D ** -0.5, 0.1875, ((2, 4),)),
        "w_attn_out": gaussian(seeds[3], (D, D), (D // 8) ** -0.5, 0.5, ((0, 4),)),
        "w_in": gaussian(seeds[4], (D, FF), D ** -0.5, 0.1875, ((1, 4),)),
        "w_out": gaussian(seeds[5], (FF, D), FF ** -0.5, 0.09375, ((0, 4),)),
        "gain_attn": jnp.clip(1.0 + 0.1 * jax.random.normal(seeds[6], (D,), jnp.float32), 0.5, 1.5),
        "gain_mlp": jnp.clip(1.0 + 0.1 * jax.random.normal(seeds[7], (D,), jnp.float32), 0.5, 1.5),
        "cotangent": gaussian(seeds[8], (TOKENS, D), 1.0, 6.0, ((0, 32),)),
    }


EPSILON = 1e-06
NEGATIVE = -1e+30
HIGH = lax.Precision.HIGHEST

@jax.custom_vjp
def low(v):
    return lax.optimization_barrier(v.astype(jnp.bfloat16)).astype(jnp.float32)

@jax.custom_vjp
def low_back(v):
    return v

def low_keep(v):
    return (low(v), None)

def low_pass(kept, grad):
    return (grad,)

def back_keep(v):
    return (v, None)

def back_low(kept, grad):
    return (low(grad),)
low.defvjp(low_keep, low_pass)
low_back.defvjp(back_keep, back_low)

def rms_scale(values, scaling_gain):
    return values * lax.rsqrt(lax.optimization_barrier(jnp.mean(values * values, axis=-1, keepdims=True)) + EPSILON) * scaling_gain

def item_ids(length_row, frame_count):
    item_ends = jnp.cumsum(length_row.astype(jnp.int32)).astype(jnp.int32)
    positions = jnp.arange(frame_count, dtype=jnp.int32)
    before = lax.optimization_barrier(jnp.sum((positions[:, None] >= item_ends[None, :]).astype(jnp.int32), axis=1)).astype(jnp.int32)
    return jnp.where(positions < item_ends[-1], before, before + positions + 1).astype(jnp.int32)

def attend_block(queries, positions, idents, keys_all, values_all, idents_all):
    frame_count = keys_all.shape[0]
    scaling = HEAD ** (-0.5)
    scores = low_back(jnp.einsum('bhd,khd->hbk', queries, keys_all, precision=HIGH) * scaling)
    visible = (idents[:, None] == idents_all[None, :]) & (jnp.arange(frame_count, dtype=jnp.int32)[None, :] <= positions[:, None])
    scores = jnp.where(visible[None], scores, NEGATIVE)
    row_peak = lax.optimization_barrier(jnp.max(scores, axis=-1, keepdims=True))
    weights = jnp.where(visible[None], jnp.exp(scores - row_peak), 0.0)
    probabilities = weights / lax.optimization_barrier(jnp.sum(weights, axis=-1, keepdims=True))
    return jnp.einsum('hbk,khd->bhd', low(probabilities), values_all, precision=HIGH)

def shard_forward(frames, length_row, w_qkv, w_attn_out, w_in, w_out, gain_attn, gain_mlp):
    frame_count = frames.shape[0]
    idents = item_ids(length_row, frame_count)
    positions = jnp.arange(frame_count, dtype=jnp.int32)
    normed = low(rms_scale(frames, gain_attn))
    projected = low(low_back(jnp.einsum('td,cde->cte', normed, w_qkv, precision=HIGH)))
    head_split = projected.reshape(3, frame_count, HEADS, HEAD)
    blocks = frame_count // BLOCK

    def one_block(block_data):
        return attend_block(block_data[0], block_data[1], block_data[2], head_split[1], head_split[2], idents)
    attended = lax.map(jax.checkpoint(one_block), (head_split[0].reshape(blocks, BLOCK, HEADS, HEAD), positions.reshape(blocks, BLOCK), idents.reshape(blocks, BLOCK)))
    mixed = low(low_back(attended.reshape(frame_count, D)))
    resid = frames + low_back(jnp.dot(mixed, w_attn_out, precision=HIGH))
    normed_mlp = low(rms_scale(resid, gain_mlp))
    hidden = low_back(jnp.dot(normed_mlp, w_in, precision=HIGH))
    active = low(jax.nn.gelu(hidden, approximate=True))
    return resid + low_back(jnp.dot(active, w_out, precision=HIGH))

def reference(frames, lengths, w_qkv, w_attn_out, w_in, w_out, gain_attn, gain_mlp, cotangent):

    def forward(frames_wide, qkv_wide, attn_wide, in_wide, out_wide, gain_first, gain_second):
        shards = frames_wide.reshape(BATCHES, TOK_DEV, D)

        def per_shard(block_data):
            return shard_forward(block_data[0], block_data[1], qkv_wide, attn_wide, in_wide, out_wide, gain_first, gain_second)
        stacked = lax.map(jax.checkpoint(per_shard), (shards, lengths))
        return stacked.reshape(BATCHES * TOK_DEV, D)
    result, pullback = jax.vjp(forward, frames.astype(jnp.float32), w_qkv.astype(jnp.float32), w_attn_out.astype(jnp.float32), w_in.astype(jnp.float32), w_out.astype(jnp.float32), gain_attn.astype(jnp.float32), gain_mlp.astype(jnp.float32))
    grads = pullback(cotangent.astype(jnp.float32))
    return (result.astype(jnp.bfloat16), grads[0], grads[1], grads[2], grads[3], grads[4], grads[5], grads[6])
```

```python
import jax
import jax.numpy as jnp
from jax import lax
from jax.sharding import PartitionSpec as P

HEAD = 64
BLOCK = 512


EPSILON = 1e-06
NEGATIVE = -1e30


def rms_scale(values, scaling_gain):
    return (
        values
        * lax.rsqrt(jnp.mean(values * values, axis=-1, keepdims=True) + EPSILON)
        * scaling_gain
    )


def gelu_tanh(values):
    return jax.nn.gelu(values, approximate=True)


def item_ids(length_row, frame_count):
    item_ends = jnp.cumsum(length_row)
    positions = jnp.arange(frame_count, dtype=jnp.int32)
    before = jnp.sum((positions[:, None] >= item_ends[None, :]).astype(jnp.int32), axis=1)
    return jnp.where(positions < item_ends[-1], before, before + positions + 1)


def block_scores(queries, positions, idents, keys_all, idents_all, scaling):
    scores = (
        jnp.einsum("bhd,khd->hbk", queries, keys_all, preferred_element_type=jnp.float32) * scaling
    )
    frame_count = keys_all.shape[0]
    visible = (idents[:, None] == idents_all[None, :]) & (
        jnp.arange(frame_count, dtype=jnp.int32)[None, :] <= positions[:, None]
    )
    return (scores, visible[None])


def scatter_sum(part):
    return lax.psum_scatter(
        part.astype(jnp.bfloat16), "mp", scatter_dimension=0, tiled=True
    ).astype(jnp.float32)


def batch_sum(parts):
    sent = tuple(part.astype(jnp.bfloat16) for part in parts)
    return tuple(total.astype(jnp.float32) for total in lax.psum(sent, "dp"))


def per_device(frames, lengths, w_qkv, w_attn_out, w_in, w_out, gain_attn, gain_mlp, cotangent):
    frame_count = frames.shape[0] * lax.axis_size("mp")
    heads_here = w_attn_out.shape[0] // HEAD
    scaling = HEAD ** (-0.5)
    idents = item_ids(lengths[0], frame_count)
    positions = jnp.arange(frame_count, dtype=jnp.int32)
    frames_wide = frames.astype(jnp.float32)
    normed = rms_scale(frames_wide, gain_attn).astype(jnp.bfloat16)
    normed_all = lax.all_gather(normed, "mp", axis=0, tiled=True)
    projected = jnp.einsum(
        "td,cde->cte", normed_all, w_qkv, preferred_element_type=jnp.float32
    ).astype(jnp.bfloat16)
    head_split = projected.reshape(3, frame_count, heads_here, HEAD)
    queries, keys_all, values_all = (head_split[0], head_split[1], head_split[2])
    blocks = frame_count // BLOCK
    outputs = []
    log_totals = []
    for number in range(blocks):
        window = slice(number * BLOCK, (number + 1) * BLOCK)
        scores, visible = block_scores(
            queries[window], positions[window], idents[window], keys_all, idents, scaling
        )
        masked = jnp.where(visible, scores, NEGATIVE)
        row_peak = jnp.max(masked, axis=-1, keepdims=True)
        weights = jnp.where(visible, jnp.exp(masked - row_peak), 0.0)
        row_total = jnp.sum(weights, axis=-1, keepdims=True)
        probabilities = weights / row_total
        outputs.append(
            jnp.einsum(
                "hbk,khd->bhd",
                probabilities.astype(jnp.bfloat16),
                values_all,
                preferred_element_type=jnp.float32,
            )
        )
        log_totals.append(row_peak + jnp.log(row_total))
    attended = (
        jnp.concatenate(outputs, axis=0)
        .reshape(frame_count, heads_here * HEAD)
        .astype(jnp.bfloat16)
    )
    attn_part = jnp.dot(attended, w_attn_out, preferred_element_type=jnp.float32)
    attn_own = scatter_sum(attn_part)
    resid = frames_wide + attn_own
    normed_mlp = rms_scale(resid, gain_mlp).astype(jnp.bfloat16)
    normed_mlp_all = lax.all_gather(normed_mlp, "mp", axis=0, tiled=True)
    hidden = jnp.dot(normed_mlp_all, w_in, preferred_element_type=jnp.float32)
    active = gelu_tanh(hidden).astype(jnp.bfloat16)
    mlp_own = lax.psum_scatter(
        jnp.dot(active, w_out, preferred_element_type=jnp.float32).astype(jnp.bfloat16),
        "mp",
        scatter_dimension=0,
        tiled=True,
    ).astype(jnp.float32)
    output = (resid + mlp_own).astype(jnp.bfloat16)
    grad_top = cotangent.astype(jnp.float32)
    grad_all = lax.all_gather(cotangent, "mp", axis=0, tiled=True)
    grad_w_out = jnp.einsum("tf,td->fd", active, grad_all, preferred_element_type=jnp.float32)
    grad_active = jnp.einsum("td,fd->tf", grad_all, w_out, preferred_element_type=jnp.float32)
    grad_hidden = jax.vjp(gelu_tanh, hidden)[1](grad_active)[0].astype(jnp.bfloat16)
    grad_w_in = jnp.einsum(
        "td,tf->df", normed_mlp_all, grad_hidden, preferred_element_type=jnp.float32
    )
    grad_normed_mlp = scatter_sum(
        jnp.einsum("tf,df->td", grad_hidden, w_in, preferred_element_type=jnp.float32)
    )
    resid_back, gain_mlp_part = jax.vjp(rms_scale, resid, gain_mlp)[1](grad_normed_mlp)
    grad_resid = grad_top + resid_back
    grad_resid_all = lax.all_gather(grad_resid.astype(jnp.bfloat16), "mp", axis=0, tiled=True)
    grad_w_attn_out = jnp.einsum(
        "te,td->ed", attended, grad_resid_all, preferred_element_type=jnp.float32
    )
    grad_attended = (
        jnp.einsum("td,ed->te", grad_resid_all, w_attn_out, preferred_element_type=jnp.float32)
        .astype(jnp.bfloat16)
        .reshape(frame_count, heads_here, HEAD)
    )
    grad_keys = jnp.zeros((frame_count, heads_here, HEAD), jnp.float32)
    grad_values = jnp.zeros((frame_count, heads_here, HEAD), jnp.float32)
    grad_queries = []
    for number in range(blocks):
        window = slice(number * BLOCK, (number + 1) * BLOCK)
        scores, visible = block_scores(
            queries[window], positions[window], idents[window], keys_all, idents, scaling
        )
        probabilities = jnp.where(
            visible, jnp.exp(jnp.where(visible, scores, NEGATIVE) - log_totals[number]), 0.0
        )
        grad_rows = grad_attended[window]
        grad_probs = jnp.einsum(
            "bhd,khd->hbk", grad_rows, values_all, preferred_element_type=jnp.float32
        )
        grad_values = grad_values + jnp.einsum(
            "hbk,bhd->khd",
            probabilities.astype(jnp.bfloat16),
            grad_rows,
            preferred_element_type=jnp.float32,
        )
        inner_sum = jnp.sum(probabilities * grad_probs, axis=-1, keepdims=True)
        grad_scores = (probabilities * (grad_probs - inner_sum)).astype(jnp.bfloat16)
        grad_queries.append(
            jnp.einsum("hbk,khd->bhd", grad_scores, keys_all, preferred_element_type=jnp.float32)
            * scaling
        )
        grad_keys = (
            grad_keys
            + jnp.einsum(
                "hbk,bhd->khd", grad_scores, queries[window], preferred_element_type=jnp.float32
            )
            * scaling
        )
    grad_projected = jnp.stack(
        [
            jnp.concatenate(grad_queries, axis=0).reshape(frame_count, heads_here * HEAD),
            grad_keys.reshape(frame_count, heads_here * HEAD),
            grad_values.reshape(frame_count, heads_here * HEAD),
        ]
    ).astype(jnp.bfloat16)
    grad_w_qkv = jnp.einsum(
        "td,cte->cde", normed_all, grad_projected, preferred_element_type=jnp.float32
    )
    grad_normed = scatter_sum(
        jnp.einsum("cte,cde->td", grad_projected, w_qkv, preferred_element_type=jnp.float32)
    )
    frames_back, gain_attn_part = jax.vjp(rms_scale, frames_wide, gain_attn)[1](grad_normed)
    grad_frames = grad_resid + frames_back
    grad_gain_attn, grad_gain_mlp = lax.psum((gain_attn_part, gain_mlp_part), ("dp", "mp"))
    grad_w_in, grad_w_out = batch_sum((grad_w_in, grad_w_out))
    grad_w_qkv, grad_w_attn_out = batch_sum((grad_w_qkv, grad_w_attn_out))
    return (
        output,
        grad_frames,
        grad_w_qkv,
        grad_w_attn_out,
        grad_w_in,
        grad_w_out,
        grad_gain_attn,
        grad_gain_mlp,
    )


def solution(mesh):
    in_specs = (
        P(("dp", "mp"), None),
        P("dp", None),
        P(None, None, "mp"),
        P("mp", None),
        P(None, "mp"),
        P("mp", None),
        P(),
        P(),
        P(("dp", "mp"), None),
    )
    out_specs = (
        P(("dp", "mp"), None),
        P(("dp", "mp"), None),
        P(None, None, "mp"),
        P("mp", None),
        P(None, "mp"),
        P("mp", None),
        P(),
        P(),
    )
    return jax.shard_map(
        per_device, mesh=mesh, in_specs=in_specs, out_specs=out_specs, check_vma=False
    )
```

```python
import functools
import math

import jax
import jax.numpy as jnp
from jax import lax
from jax.experimental import pallas as pl
from jax.experimental.pallas import tpu as pltpu
from jax.sharding import Mesh
from jax.sharding import PartitionSpec as P

HEAD = 64
EPSILON = 1e-06
NEGATIVE = -1e30
MEMBERS = 4
LOG2E = math.log2(math.e)
GELU_A = math.sqrt(2.0 / math.pi)
GELU_B = 0.044715
AXES = ("col", "core", "pair", "zz")
BF16 = jnp.bfloat16
F32 = jnp.float32
VMEM_LIMIT = 60 << 20
MESH_ID = pl.DeviceIdType.MESH


def dot_nn(a, b):
    return lax.dot_general(a, b, (((1,), (0,)), ((), ())), preferred_element_type=F32)


def dot_nt(a, b):
    return lax.dot_general(a, b, (((1,), (1,)), ((), ())), preferred_element_type=F32)


def dot_tn(a, b):
    return lax.dot_general(a, b, (((0,), (0,)), ((), ())), preferred_element_type=F32)


def flip(bit, amount):
    return bit + amount - 2 * bit * amount


class Place:
    def __init__(self):
        self.col = lax.axis_index("col")
        self.core = lax.axis_index("core")
        self.pair = lax.axis_index("pair")
        self.zz = lax.axis_index("zz")
        self.swapped = self.core != self.pair
        self.stays = self.core == self.pair
        self.me = self.member(0, 0)

    def member(self, other_core, other_chip):
        return 2 * flip(self.core, other_core) + flip(self.zz, other_chip)

    def sibling(self):
        return {"core": 1 - self.core}

    def across(self):
        return {"zz": 1 - self.zz}

    def trade(self):
        return {"pair": 1 - self.pair, "core": 1 - self.core}

    def column(self, bit):
        step = 1 << bit
        here = lax.rem(lax.div(self.col, step), 2)
        return {"col": self.col + step * (1 - 2 * here)}


class Wire:
    def __init__(self, send_sems, recv_sems):
        self.send_sems = send_sems
        self.recv_sems = recv_sems
        self.used = 0

    def copy(self, src, dst, target, got=None):
        number = self.used
        self.used += 1
        return Transfer(
            src, dst, target, dst if got is None else got,
            self.send_sems.at[number], self.recv_sems.at[number],
        )


class Transfer:
    def __init__(self, src, dst, target, got, send_sem, recv_sem):
        self.args = (src, dst, target, got, send_sem, recv_sem)

    def start(self):
        src, dst, target, _, send_sem, recv_sem = self.args
        pltpu.make_async_remote_copy(
            src_ref=src, dst_ref=dst, send_sem=send_sem, recv_sem=recv_sem,
            device_id=target, device_id_type=MESH_ID,
        ).start()

    def wait_send(self):
        src, dst, target, _, send_sem, recv_sem = self.args
        pltpu.make_async_remote_copy(
            src_ref=src, dst_ref=dst, send_sem=send_sem, recv_sem=recv_sem,
            device_id=target, device_id_type=MESH_ID,
        ).wait_send()

    def wait_recv(self):
        _, _, target, got, send_sem, recv_sem = self.args
        pltpu.make_async_remote_copy(
            src_ref=got, dst_ref=got, send_sem=send_sem, recv_sem=recv_sem,
            device_id=target, device_id_type=MESH_ID,
        ).wait_recv()


def meet(targets):
    barrier = pltpu.get_barrier_semaphore()
    for target in targets:
        pl.semaphore_signal(barrier, inc=1, device_id=target, device_id_type=MESH_ID)
    pl.semaphore_wait(barrier, len(targets))


class Gather:
    def __init__(self, wire, place, whole):
        me, near = place.me, place.member(1, 0)
        far, corner = place.member(0, 1), place.member(1, 1)
        self.to_near = wire.copy(whole.at[me], whole.at[me], place.sibling(), whole.at[near])
        self.to_far = wire.copy(whole.at[me], whole.at[me], place.across(), whole.at[far])
        self.relay = wire.copy(whole.at[far], whole.at[far], place.sibling(), whole.at[corner])

    def start(self):
        self.to_far.start()
        self.to_near.start()

    def take_near(self):
        self.to_near.wait_recv()

    def take_far(self):
        self.to_far.wait_recv()
        self.relay.start()

    def take_corner(self):
        self.relay.wait_recv()

    def drain(self):
        self.to_near.wait_send()
        self.to_far.wait_send()
        self.relay.wait_send()


class Scatter:
    def __init__(self, wire, place, part, near_in, joined, far_in):
        self.place, self.part = place, part
        self.near_in, self.joined, self.far_in = near_in, joined, far_in
        corner, near = place.member(1, 1), place.member(1, 0)
        self.corner = wire.copy(part.at[corner], near_in.at[0], place.sibling())
        self.near = wire.copy(part.at[near], near_in.at[1], place.sibling())
        self.far = wire.copy(joined, far_in, place.across())

    def send_corner(self):
        self.corner.start()

    def send_near(self):
        self.near.start()

    def send_far(self):
        self.corner.wait_recv()
        far = self.place.member(0, 1)

        def rows(step, carry):
            at = pl.ds(pl.multiple_of(step * 64, 64), 64)
            total = self.part[far, at].astype(F32) + self.near_in[0, at].astype(F32)
            self.joined[at] = total.astype(BF16)
            return carry

        lax.fori_loop(0, self.joined.shape[0] // 64, rows, 0)
        self.far.start()

    def wait(self):
        self.near.wait_recv()
        self.far.wait_recv()

    def total(self, at):
        return (
            self.part[self.place.me, at].astype(F32)
            + self.near_in[1, at].astype(F32)
            + self.far_in[at].astype(F32)
        )

    def drain(self):
        self.corner.wait_send()
        self.near.wait_send()
        self.far.wait_send()


def each_rows(count, size, body):
    def step(number, carry):
        body(pl.ds(pl.multiple_of(number * size, size), size))
        return carry

    lax.fori_loop(0, count // size, step, 0)


def scatter_shapes(rows, width):
    return [
        pltpu.VMEM((MEMBERS, rows, width), BF16),
        pltpu.VMEM((2, rows, width), BF16),
        pltpu.VMEM((rows, width), BF16),
        pltpu.VMEM((rows, width), BF16),
    ]


def visible_tile(first_ref, block, tile, rows):
    key_at = tile * rows + lax.broadcasted_iota(jnp.int32, (rows, rows), 0)
    query_at = block * rows + lax.broadcasted_iota(jnp.int32, (rows, rows), 1)
    first = first_ref[0:1, pl.ds(pl.multiple_of(block * rows, rows), rows)]
    return (key_at >= first) & (key_at <= query_at)


def swap_order(step):
    return lax.rem(step, 2), lax.div(step, 2)


def forward_kernel(
    items,
    x_own, dy_own, lengths, gain_attn, gain_mlp, wq, wa, wi, wo,
    heads_out, keys_t, att_t, lse, first, normed, grads, outs, resid, grad_resid, gain_part,
    wq_m, wa_m, x_keep,
    wi_m, wo_m, x_all, dy_all, values_t, first_near, scores, acc_t, normed_mlp, active, grad_hidden,
    part1, near1, joined1, far1, part3, near3, joined3, far3,
    send_sems, recv_sems, local_sems,
):
    place = Place()
    wire = Wire(send_sems, recv_sems)
    rows, width = x_own.shape
    heads = heads_out.shape[1]
    me = place.me
    frame_count = MEMBERS * rows
    hidden_units = wi.shape[1]

    near = place.member(1, 0)
    x_trade = wire.copy(x_own, x_all.at[near], place.trade(), x_all.at[me])
    dy_trade = wire.copy(dy_own, dy_all.at[near], place.trade(), dy_all.at[me])
    first_trade = wire.copy(first_near.at[0], first_near.at[1], place.sibling())

    quarter = lax.rem(place.col, MEMBERS)
    weights = []
    for source, target, axis in ((wq, wq_m, 1), (wa, wa_m, 0), (wi, wi_m, 0), (wo, wo_m, 0)):
        depth = source.shape[axis] // MEMBERS

        def cut(ref, start, size, axis=axis):
            window = pl.ds(pl.multiple_of(start, size), size)
            return ref.at[:, window] if axis == 1 else ref.at[window]

        other = quarter + 1 - 2 * lax.rem(quarter, 2)
        duo = lax.div(quarter, 2)
        mine = cut(target, quarter * depth, depth)
        steps = (
            wire.copy(cut(source, quarter * depth, depth), mine, place.trade()),
            wire.copy(mine, mine, place.column(0), cut(target, other * depth, depth)),
            wire.copy(
                cut(target, duo * 2 * depth, 2 * depth),
                cut(target, duo * 2 * depth, 2 * depth),
                place.column(1),
                cut(target, (1 - duo) * 2 * depth, 2 * depth),
            ),
        )
        local = pltpu.make_async_copy(source, target, local_sems.at[len(weights)])
        weights.append((steps, local))

    def when_swapped(action):
        pl.when(place.swapped)(action)

    def when_stays(action):
        pl.when(place.stays)(action)

    meet([place.sibling(), place.across(), place.trade(), place.column(0), place.column(1)])

    @when_swapped
    def _():
        x_trade.start()
        weights[0][0][0].start()

    @when_stays
    def _():
        x_all[me] = x_own[...]
        dy_all[me] = dy_own[...]
        for _, local in weights:
            local.start()

    position = lax.broadcasted_iota(jnp.int32, (8, frame_count), 1)
    begin = jnp.zeros((8, frame_count), jnp.int32)
    end = jnp.int32(0)
    for item in range(items):
        size = lengths[0, item]
        end = end + size
        begin = begin + jnp.where(position >= end, size, 0)
    first_near[0] = jnp.where(position >= end, position, begin)
    first_trade.start()

    @when_swapped
    def _():
        x_trade.wait_recv()

    gather_x = Gather(wire, place, x_all)
    gather_x.start()
    gain = gain_attn[...]

    def norm_block(member):
        def some(at):
            values = x_all[member, at].astype(F32)
            scale = lax.rsqrt(jnp.mean(values * values, axis=-1, keepdims=True) + EPSILON)
            normed[member, at] = (values * scale * gain).astype(BF16)

        each_rows(rows, 64, some)

    norm_block(me)
    x_keep[...] = x_all[me]
    first_trade.wait_recv()

    @when_swapped
    def _():
        first[...] = first_near[1]
        weights[0][0][0].wait_recv()
        weights[0][0][1].start()
        dy_trade.start()
        for steps, _ in weights[1:]:
            steps[0].start()

    @when_stays
    def _():
        first[...] = first_near[0]

    gather_x.take_near()
    norm_block(place.member(1, 0))

    @when_swapped
    def _():
        weights[0][0][1].wait_recv()
        weights[0][0][2].start()

    gather_x.take_far()
    norm_block(place.member(0, 1))
    gather_x.take_corner()
    norm_block(place.member(1, 1))

    @when_swapped
    def _():
        weights[0][0][2].wait_recv()

    @when_stays
    def _():
        weights[0][1].wait()

    def project(member, carry):
        source = normed[member]
        for kind in range(3):
            block = dot_nn(source, wq_m[kind])
            narrow = block.astype(BF16)
            for head in range(heads):
                heads_out[kind, head, member] = narrow[:, head * HEAD : (head + 1) * HEAD]
            if kind == 1:
                keys_t[member] = block.T.astype(BF16)
            if kind == 2:
                values_t[member] = block.T.astype(BF16)
        return carry

    lax.fori_loop(0, MEMBERS, project, 0)

    @when_swapped
    def _():
        dy_trade.wait_recv()

    gather_dy = Gather(wire, place, dy_all)
    gather_dy.start()

    @when_swapped
    def _():
        for steps, _ in weights[1:]:
            steps[0].wait_recv()
            steps[1].start()
        weights[1][0][1].wait_recv()
        weights[1][0][2].start()
        weights[1][0][2].wait_recv()

    @when_stays
    def _():
        weights[1][1].wait()

    shift = (HEAD ** -0.5) * LOG2E
    scatter1 = Scatter(wire, place, part1, near1, joined1, far1)

    def attend(step, carry):
        flip_core, flip_chip = swap_order(3 - step)
        block = place.member(flip_core, flip_chip)

        def score(tile, peaks):
            seen = visible_tile(first, block, tile, rows)
            higher = []
            for head in range(heads):
                raw = dot_nt(heads_out[1, head, tile], heads_out[0, head, block])
                raw = jnp.where(seen, raw, NEGATIVE)
                scores[head, tile] = raw
                higher.append(jnp.maximum(peaks[head], jnp.max(raw, axis=0, keepdims=True)))
            return tuple(higher)

        low = jnp.full((1, rows), NEGATIVE, F32)
        peaks = lax.fori_loop(0, block + 1, score, (low,) * heads)
        acc_t[...] = jnp.zeros_like(acc_t)

        def weigh(tile, totals):
            sums = []
            for head in range(heads):
                weight = jnp.exp2((scores[head, tile] - peaks[head]) * shift)
                sums.append(totals[head] + jnp.sum(weight, axis=0, keepdims=True))
                at = slice(head * HEAD, (head + 1) * HEAD)
                acc_t[at] += dot_nn(values_t[tile, at], weight.astype(BF16))
            return tuple(sums)

        none = jnp.zeros((1, rows), F32)
        totals = lax.fori_loop(0, block + 1, weigh, (none,) * heads)
        for head in range(heads):
            at = slice(head * HEAD, (head + 1) * HEAD)
            acc_t[at] = acc_t[at] / totals[head]
            lse[block, head : head + 1] = peaks[head] * shift + jnp.log2(totals[head])
        att_t[block] = acc_t[...].astype(BF16)
        attended = acc_t[...].T.astype(BF16)
        part1[block] = dot_nn(attended, wa_m[...]).astype(BF16)

        @pl.when(step == 0)
        def _():
            scatter1.send_corner()

        @pl.when(step == 1)
        def _():
            scatter1.send_far()

        @pl.when(step == 2)
        def _():
            scatter1.send_near()

        return carry

    lax.fori_loop(0, MEMBERS, attend, 0)

    gather_dy.take_near()
    gather_dy.take_far()
    gather_dy.take_corner()

    @when_swapped
    def _():
        for steps, _ in weights[2:]:
            steps[1].wait_recv()
            steps[2].start()

    scatter1.wait()
    gain2 = gain_mlp[...]

    def add_resid(at):
        total = x_all[me, at].astype(F32) + scatter1.total(at)
        resid[at] = total
        scale = lax.rsqrt(jnp.mean(total * total, axis=-1, keepdims=True) + EPSILON)
        normed_mlp[me, at] = (total * scale * gain2).astype(BF16)

    each_rows(rows, 64, add_resid)
    gather_n = Gather(wire, place, normed_mlp)
    gather_n.start()

    @when_swapped
    def _():
        for steps, _ in weights[2:]:
            steps[2].wait_recv()

    @when_stays
    def _():
        for _, local in weights[2:]:
            local.wait()

    span = 256
    scatter3 = Scatter(wire, place, part3, near3, joined3, far3)

    def feed(step, carry):
        flip_core = jnp.where((step == 1) | (step == 2), 1, 0)
        flip_chip = jnp.where(step >= 2, 1, 0)
        block = place.member(flip_core, flip_chip)

        @pl.when(step == 1)
        def _():
            gather_n.take_near()

        @pl.when(step == 2)
        def _():
            gather_n.take_far()
            gather_n.take_corner()

        def units(number, inner):
            at = pl.ds(pl.multiple_of(number * span, span), span)
            hidden = dot_nn(normed_mlp[block], wi_m[:, at])
            grad_active = dot_nt(dy_all[block], wo_m[at])
            square = hidden * hidden
            bend = jnp.tanh(GELU_A * hidden * (1.0 + GELU_B * square))
            half = 0.5 * (1.0 + bend)
            active[block, :, at] = (hidden * half).astype(BF16)
            slope = half + 0.5 * hidden * (1.0 - bend * bend) * (
                GELU_A * (1.0 + 3.0 * GELU_B * square)
            )
            grad_hidden[block, :, at] = (grad_active * slope).astype(BF16)
            return inner

        lax.fori_loop(0, hidden_units // span, units, 0)

        def features(number, inner):
            at = pl.ds(pl.multiple_of(number * span, span), span)
            part3[block, :, at] = dot_nt(grad_hidden[block], wi_m[at]).astype(BF16)
            outs[block, :, at] = dot_nn(active[block], wo_m[:, at]).astype(BF16)
            return inner

        lax.fori_loop(0, width // span, features, 0)

        @pl.when(step == 1)
        def _():
            scatter3.send_near()

        @pl.when(step == 2)
        def _():
            scatter3.send_corner()

        @pl.when(step == 3)
        def _():
            scatter3.send_far()

        return carry

    lax.fori_loop(0, MEMBERS, feed, 0)

    def weight_grads(number, carry):
        at = pl.ds(pl.multiple_of(number * span, span), span)
        down = pl.ds(pl.multiple_of(width + number * span, span), span)
        left = normed_mlp[:, :, at].reshape(frame_count, span)
        grads[at] = dot_tn(left, grad_hidden[...].reshape(frame_count, hidden_units)).astype(BF16)
        left = active[:, :, at].reshape(frame_count, span)
        grads[down] = dot_tn(left, dy_all[...].reshape(frame_count, width)).astype(BF16)
        return carry

    lax.fori_loop(0, width // span, weight_grads, 0)

    scatter3.wait()
    gain_part[...] = jnp.zeros_like(gain_part)

    def norm_back(at):
        grad = scatter3.total(at)
        values = resid[at]
        scale = lax.rsqrt(jnp.mean(values * values, axis=-1, keepdims=True) + EPSILON)
        gain_part[0:1] += jnp.sum(grad * values * scale, axis=0, keepdims=True)
        scaled = grad * gain2
        mean = jnp.mean(scaled * values, axis=-1, keepdims=True)
        grad_resid[at] = (
            dy_all[me, at].astype(F32) + scale * scaled - values * (scale * scale * scale) * mean
        )

    each_rows(rows, 64, norm_back)

    for one in (gather_x, gather_dy, gather_n, scatter1, scatter3):
        one.drain()
    first_trade.wait_send()

    @when_swapped
    def _():
        x_trade.wait_send()
        dy_trade.wait_send()
        for steps, _ in weights:
            for step in steps:
                step.wait_send()


def vmem(shape, kind):
    return pltpu.VMEM(shape, kind)


def forward_call(x_own, dy_own, lengths, gain_attn, gain_mlp, wq, wa, wi, wo):
    rows, width = x_own.shape
    heads = wa.shape[0] // HEAD
    features = wa.shape[0]
    units = wi.shape[1]
    frames = MEMBERS * rows
    outputs = [
        ((3, heads, MEMBERS, rows, HEAD), BF16),
        ((MEMBERS, features, rows), BF16),
        ((MEMBERS, features, rows), BF16),
        ((MEMBERS, 8, rows), F32),
        ((8, frames), jnp.int32),
        ((MEMBERS, rows, width), BF16),
        ((width + units, width), BF16),
        ((MEMBERS, rows, width), BF16),
        ((rows, width), F32),
        ((rows, width), F32),
        ((8, width), F32),
        (wq.shape, BF16),
        (wa.shape, BF16),
        ((rows, width), BF16),
    ]
    block = pl.BlockSpec(memory_space=pltpu.VMEM)
    whole = pl.BlockSpec(memory_space=pl.ANY)
    members = (MEMBERS, rows, width)
    return pl.pallas_call(
        functools.partial(forward_kernel, lengths.shape[1]),
        out_shape=[jax.ShapeDtypeStruct(shape, kind) for shape, kind in outputs],
        in_specs=[block, block, pl.BlockSpec(memory_space=pltpu.SMEM), block, block]
        + [whole] * 4,
        out_specs=[block] * len(outputs),
        scratch_shapes=[
            vmem(wi.shape, BF16),
            vmem(wo.shape, BF16),
            vmem(members, BF16),
            vmem(members, BF16),
            vmem((MEMBERS, features, rows), BF16),
            vmem((2, 8, frames), jnp.int32),
            vmem((heads, MEMBERS, rows, rows), F32),
            vmem((features, rows), F32),
            vmem(members, BF16),
            vmem((MEMBERS, rows, units), BF16),
            vmem((MEMBERS, rows, units), BF16),
        ]
        + scatter_shapes(rows, width) * 2
        + [
            pltpu.SemaphoreType.DMA((32,)),
            pltpu.SemaphoreType.DMA((32,)),
            pltpu.SemaphoreType.DMA((4,)),
        ],
        compiler_params=pltpu.CompilerParams(
            collective_id=0, has_side_effects=True, vmem_limit_bytes=VMEM_LIMIT
        ),
        name="forward",
    )(x_own, dy_own, lengths, gain_attn, gain_mlp, wq, wa, wi, wo)


def backward_kernel(
    bits,
    heads_in, keys_t, att_t, lse, first, normed, outs, resid, grad_resid, gain_in, wq, wa, x_keep,
    gain_attn,
    output, grad_frames, grads_attn, gains_out,
    grad_all, top_t, grad_qt, grad_k, grad_v, projected, gain_sum, gain_got, moved, moved_in,
    out_keep, out_in,
    near2, joined2, far2, part4, near4, joined4, far4,
    send_sems, recv_sems,
):
    place = Place()
    wire = Wire(send_sems, recv_sems)
    rows, width = x_keep.shape
    heads = heads_in.shape[1]
    features = heads * HEAD
    me = place.me
    frame_count = MEMBERS * rows

    meet(
        [place.sibling(), place.across(), place.trade()]
        + [{"pair": 1 - place.pair}]
        + [place.column(bit) for bit in range(bits)]
    )

    grad_all[me] = grad_resid[...].astype(BF16)
    gather_g = Gather(wire, place, grad_all)
    gather_g.start()
    scatter2 = Scatter(wire, place, outs, near2, joined2, far2)
    scatter2.send_corner()
    scatter2.send_near()
    grad_k[...] = jnp.zeros_like(grad_k)
    grad_v[...] = jnp.zeros_like(grad_v)
    shift = (HEAD ** -0.5) * LOG2E
    scaling = HEAD ** -0.5

    def block_back(step, carry):
        flip_core, flip_chip = swap_order(step)
        block = place.member(flip_core, flip_chip)

        @pl.when(step == 1)
        def _():
            gather_g.take_near()
            scatter2.send_far()

        @pl.when(step == 2)
        def _():
            gather_g.take_far()

        @pl.when(step == 3)
        def _():
            gather_g.take_corner()

        source = grad_all[block]
        top = dot_nt(source, wa[...]).astype(BF16)
        turned = dot_nt(wa[...], source).astype(BF16)
        top_t[...] = turned
        tops = [top[:, head * HEAD : (head + 1) * HEAD] for head in range(heads)]
        product = turned.astype(F32) * att_t[block].astype(F32)
        deltas = [
            jnp.sum(product[head * HEAD : (head + 1) * HEAD], axis=0, keepdims=True)
            for head in range(heads)
        ]
        grad_qt[...] = jnp.zeros_like(grad_qt)

        def tiles(tile, inner):
            seen = visible_tile(first, block, tile, rows)
            for head in range(heads):
                at = slice(head * HEAD, (head + 1) * HEAD)
                query = heads_in[0, head, block]
                raw = dot_nt(heads_in[1, head, tile], query)
                prob = jnp.where(
                    seen, jnp.exp2(raw * shift - lse[block, head : head + 1]), 0.0
                )
                grad_prob = dot_nt(heads_in[2, head, tile], tops[head])
                grad_score = (prob * (grad_prob - deltas[head])).astype(BF16)
                grad_v[head, tile] += dot_nn(prob.astype(BF16), tops[head])
                grad_k[head, tile] += dot_nn(grad_score, query)
                grad_qt[at] += dot_nn(keys_t[tile, at], grad_score)
            return inner

        lax.fori_loop(0, block + 1, tiles, 0)
        projected[0, block] = (grad_qt[...].T * scaling).astype(BF16)
        return carry

    lax.fori_loop(0, MEMBERS, block_back, 0)

    scatter4 = Scatter(wire, place, part4, near4, joined4, far4)

    def inputs_back(step, carry):
        flip_core, flip_chip = swap_order(3 - step)
        block = place.member(flip_core, flip_chip)
        for head in range(heads):
            at = slice(head * HEAD, (head + 1) * HEAD)
            projected[1, block, :, at] = (grad_k[head, block] * scaling).astype(BF16)
            projected[2, block, :, at] = grad_v[head, block].astype(BF16)
        span = 256

        def columns(number, inner):
            down = pl.ds(pl.multiple_of(number * span, span), span)
            total = dot_nt(projected[0, block], wq[0, down])
            total += dot_nt(projected[1, block], wq[1, down])
            total += dot_nt(projected[2, block], wq[2, down])
            part4[block, :, down] = total.astype(BF16)
            return inner

        lax.fori_loop(0, width // span, columns, 0)

        @pl.when(step == 0)
        def _():
            scatter4.send_corner()

        @pl.when(step == 1)
        def _():
            scatter4.send_far()

        @pl.when(step == 2)
        def _():
            scatter4.send_near()

        return carry

    lax.fori_loop(0, MEMBERS, inputs_back, 0)

    for kind in range(3):
        right = projected[kind].reshape(frame_count, features)

        def weight_grads(number, carry, kind=kind, right=right):
            at = pl.ds(pl.multiple_of(number * 256, 256), 256)
            to = pl.ds(pl.multiple_of(kind * width + number * 256, 256), 256)
            left = normed[:, :, at].reshape(frame_count, 256)
            grads_attn[to] = dot_tn(left, right).astype(BF16)
            return carry

        lax.fori_loop(0, width // 256, weight_grads, 0)

    def out_grads(number, carry):
        at = pl.ds(pl.multiple_of(number * features, features), features)
        to = pl.ds(pl.multiple_of(3 * width + number * features, features), features)
        total = dot_nn(att_t[0], grad_all[0, :, at])
        for member in range(1, MEMBERS):
            total += dot_nn(att_t[member], grad_all[member, :, at])
        grads_attn[to] = total.astype(BF16)
        return carry

    lax.fori_loop(0, width // features, out_grads, 0)

    scatter2.wait()

    def finish_output(at):
        out_keep[at] = (resid[at] + scatter2.total(at)).astype(BF16)

    each_rows(rows, 64, finish_output)
    out_trade = wire.copy(out_keep, out_in, place.trade())

    @pl.when(place.swapped)
    def _():
        out_trade.start()

    scatter4.wait()
    gain = gain_attn[...]
    gain_sum[...] = jnp.zeros_like(gain_sum)
    gain_sum[0:1] = gain_in[0:1]

    def finish_frames(at):
        grad = scatter4.total(at)
        values = x_keep[at].astype(F32)
        scale = lax.rsqrt(jnp.mean(values * values, axis=-1, keepdims=True) + EPSILON)
        gain_sum[1:2] += jnp.sum(grad * values * scale, axis=0, keepdims=True)
        scaled = grad * gain
        mean = jnp.mean(scaled * values, axis=-1, keepdims=True)
        total = grad_resid[at] + scale * scaled - values * (scale * scale * scale) * mean
        grad_frames[at] = total
        moved[at] = total.astype(BF16)

    each_rows(rows, 64, finish_frames)
    frames_trade = wire.copy(moved, moved_in, place.trade())

    @pl.when(place.swapped)
    def _():
        frames_trade.start()

    partners = [place.sibling(), place.across(), {"pair": 1 - place.pair}]
    partners += [place.column(bit) for bit in range(bits)]
    for number, partner in enumerate(partners):
        trade = wire.copy(gain_sum.at[pl.ds(8 * number, 8)], gain_got.at[number], partner)
        trade.start()
        trade.wait_recv()
        here = slice(8 * number, 8 * number + 8)
        gain_sum[8 * number + 8 : 8 * number + 16] = gain_sum[here] + gain_got[number]
        trade.wait_send()
    gains_out[...] = gain_sum[8 * len(partners) : 8 * len(partners) + 8]

    @pl.when(place.swapped)
    def _():
        out_trade.wait_recv()
        output[...] = out_in[...]
        frames_trade.wait_recv()
        grad_frames[...] = moved_in[...].astype(F32)
        out_trade.wait_send()
        frames_trade.wait_send()

    @pl.when(place.stays)
    def _():
        output[...] = out_keep[...]

    for one in (gather_g, scatter2, scatter4):
        one.drain()


def backward_call(bits, saved, gain_attn):
    (heads_in, keys_t, att_t, lse, first, normed, _, outs, resid, grad_resid, gain_part,
     wq, wa, x_keep) = saved
    rows, width = x_keep.shape
    features = wa.shape[0]
    heads = features // HEAD
    members = (MEMBERS, rows, width)
    steps = 3 + bits
    block = pl.BlockSpec(memory_space=pltpu.VMEM)
    outputs = [
        ((rows, width), BF16),
        ((rows, width), F32),
        ((4 * width, features), BF16),
        ((8, width), F32),
    ]
    args = (heads_in, keys_t, att_t, lse, first, normed, outs, resid, grad_resid, gain_part,
            wq, wa, x_keep, gain_attn)
    return pl.pallas_call(
        functools.partial(backward_kernel, bits),
        out_shape=[jax.ShapeDtypeStruct(shape, kind) for shape, kind in outputs],
        in_specs=[block] * len(args),
        out_specs=[block] * len(outputs),
        scratch_shapes=[
            vmem(members, BF16),
            vmem((features, rows), BF16),
            vmem((features, rows), F32),
            vmem((heads, MEMBERS, rows, HEAD), F32),
            vmem((heads, MEMBERS, rows, HEAD), F32),
            vmem((3, MEMBERS, rows, features), BF16),
            vmem((8 * steps + 8, width), F32),
            vmem((steps, 8, width), F32),
            vmem((rows, width), BF16),
            vmem((rows, width), BF16),
            vmem((rows, width), BF16),
            vmem((rows, width), BF16),
        ]
        + scatter_shapes(rows, width)[1:]
        + scatter_shapes(rows, width)
        + [pltpu.SemaphoreType.DMA((24,)), pltpu.SemaphoreType.DMA((24,))],
        compiler_params=pltpu.CompilerParams(
            collective_id=1, has_side_effects=True, vmem_limit_bytes=VMEM_LIMIT
        ),
        name="backward",
    )(*args)


def spread_grads(grads):
    piece = lax.psum_scatter(grads, ("col", "pair"), scatter_dimension=0, tiled=True)
    moves = []
    for core in range(2):
        for pair in range(2):
            source = core * 2 + pair
            moves.append((source, source if core == pair else 3 - source))
    piece = lax.ppermute(piece, ("core", "pair"), moves)
    return lax.all_gather(piece, ("col", "core"), axis=0, tiled=True)


def per_device(bits, frames, lengths, wq, wa, wi, wo, gain_attn, gain_mlp, cotangent):
    width = frames.shape[1]
    features = wa.shape[0]
    first_gain = gain_attn.reshape(1, width)
    second_gain = gain_mlp.reshape(1, width)
    saved = forward_call(frames, cotangent, lengths, first_gain, second_gain, wq, wa, wi, wo)
    grads_mlp = spread_grads(saved[6]).astype(F32)
    output, grad_frames, grads_attn, gains = backward_call(bits, saved, first_gain)
    grads_attn = spread_grads(grads_attn).astype(F32)
    grad_wq = grads_attn[: 3 * width].reshape(3, width, features)
    turned = grads_attn[3 * width :].reshape(width // features, features, features)
    grad_wa = jnp.transpose(turned, (1, 0, 2)).reshape(features, width)
    return (
        output,
        grad_frames,
        grad_wq,
        grad_wa,
        grads_mlp[:width],
        grads_mlp[width:],
        gains[1],
        gains[0],
    )


def solution(mesh):
    batches = mesh.shape["dp"]
    bits = (batches // 2).bit_length() - 1
    inner = Mesh(mesh.devices.reshape(batches // 2, 2, 2, 2), AXES)
    dp, mp = ("col", "core"), ("pair", "zz")
    rows = P(dp + mp, None)
    weights = (P(None, None, mp), P(mp, None), P(None, mp), P(mp, None))
    return jax.shard_map(
        functools.partial(per_device, bits),
        mesh=inner,
        in_specs=(rows, P(dp, None)) + weights + (P(), P(), rows),
        out_specs=(rows, rows) + weights + (P(), P()),
        check_vma=False,
    )
```

```python
import functools
import math

import jax
import jax.numpy as jnp
from jax import lax
from jax.experimental import pallas as pl
from jax.experimental.pallas import tpu as pltpu
from jax.sharding import Mesh
from jax.sharding import PartitionSpec as P

HEAD = 64
EPSILON = 1e-06
NEGATIVE = -1e30
MEMBERS = 4
LOG2E = math.log2(math.e)
GELU_A = math.sqrt(2.0 / math.pi)
GELU_B = 0.044715
AXES = ("col", "core", "pair", "zz")
BF16 = jnp.bfloat16
F32 = jnp.float32
VMEM_LIMIT = 62 << 20
MESH_ID = pl.DeviceIdType.MESH


def dot_nn(a, b):
    return lax.dot_general(a, b, (((1,), (0,)), ((), ())), preferred_element_type=F32)


def dot_nt(a, b):
    return lax.dot_general(a, b, (((1,), (1,)), ((), ())), preferred_element_type=F32)


def dot_tn(a, b):
    return lax.dot_general(a, b, (((0,), (0,)), ((), ())), preferred_element_type=F32)


def flip(bit, amount):
    return bit + amount - 2 * bit * amount


class Place:
    def __init__(self):
        self.col = lax.axis_index("col")
        self.core = lax.axis_index("core")
        self.pair = lax.axis_index("pair")
        self.zz = lax.axis_index("zz")
        self.swapped = self.core != self.pair
        self.stays = self.core == self.pair
        self.me = self.member(0, 0)

    def member(self, other_core, other_chip):
        return 2 * flip(self.core, other_core) + flip(self.zz, other_chip)

    def sibling(self):
        return {"core": 1 - self.core}

    def across(self):
        return {"zz": 1 - self.zz}

    def trade(self):
        return {"pair": 1 - self.pair, "core": 1 - self.core}

    def column(self, bit):
        step = 1 << bit
        here = lax.rem(lax.div(self.col, step), 2)
        return {"col": self.col + step * (1 - 2 * here)}


class Wire:
    def __init__(self, send_sems, recv_sems):
        self.send_sems = send_sems
        self.recv_sems = recv_sems
        self.used = 0

    def copy(self, src, dst, target, got=None):
        number = self.used
        self.used += 1
        return Transfer(
            src, dst, target, dst if got is None else got,
            self.send_sems.at[number], self.recv_sems.at[number],
        )


class Transfer:
    def __init__(self, src, dst, target, got, send_sem, recv_sem):
        self.args = (src, dst, target, got, send_sem, recv_sem)

    def start(self):
        src, dst, target, _, send_sem, recv_sem = self.args
        pltpu.make_async_remote_copy(
            src_ref=src, dst_ref=dst, send_sem=send_sem, recv_sem=recv_sem,
            device_id=target, device_id_type=MESH_ID,
        ).start()

    def wait_send(self):
        src, dst, target, _, send_sem, recv_sem = self.args
        pltpu.make_async_remote_copy(
            src_ref=src, dst_ref=dst, send_sem=send_sem, recv_sem=recv_sem,
            device_id=target, device_id_type=MESH_ID,
        ).wait_send()

    def wait_recv(self):
        _, _, target, got, send_sem, recv_sem = self.args
        pltpu.make_async_remote_copy(
            src_ref=got, dst_ref=got, send_sem=send_sem, recv_sem=recv_sem,
            device_id=target, device_id_type=MESH_ID,
        ).wait_recv()


def meet(targets):
    barrier = pltpu.get_barrier_semaphore()
    for target in targets:
        pl.semaphore_signal(barrier, inc=1, device_id=target, device_id_type=MESH_ID)
    pl.semaphore_wait(barrier, len(targets))


class Gather:
    def __init__(self, wire, place, whole, count=1):
        me, near = place.me, place.member(1, 0)
        far, corner = place.member(0, 1), place.member(1, 1)
        size = whole.shape[1] // count
        self.to_near, self.to_far, self.relay = [], [], []
        for number in range(count):
            at = pl.ds(number * size, size)
            mine, its, across, last = (whole.at[one, at] for one in (me, near, far, corner))
            self.to_near.append(wire.copy(mine, mine, place.sibling(), its))
            self.to_far.append(wire.copy(mine, mine, place.across(), across))
            self.relay.append(wire.copy(across, across, place.sibling(), last))

    def start(self, number=0):
        self.to_far[number].start()
        self.to_near[number].start()

    def take_near(self, number=0):
        self.to_near[number].wait_recv()

    def take_far(self, number=0):
        self.to_far[number].wait_recv()
        self.relay[number].start()

    def take_corner(self, number=0):
        self.relay[number].wait_recv()

    def drain(self):
        for one in self.to_near + self.to_far + self.relay:
            one.wait_send()


class Scatter:
    def __init__(self, wire, place, part, near_in, joined, far_in):
        self.place, self.part = place, part
        self.near_in, self.joined, self.far_in = near_in, joined, far_in
        corner, near = place.member(1, 1), place.member(1, 0)
        self.corner = wire.copy(part.at[corner], near_in.at[0], place.sibling())
        self.near = wire.copy(part.at[near], near_in.at[1], place.sibling())
        self.far = wire.copy(joined, far_in, place.across())

    def send_corner(self):
        self.corner.start()

    def send_near(self):
        self.near.start()

    def send_far(self):
        self.corner.wait_recv()
        far = self.place.member(0, 1)

        def add(at):
            total = self.part[far, at].astype(F32) + self.near_in[0, at].astype(F32)
            self.joined[at] = total.astype(BF16)

        each_rows(self.joined.shape[0], 64, add)
        self.far.start()

    def wait(self):
        self.near.wait_recv()
        self.far.wait_recv()

    def total(self, at):
        return (
            self.part[self.place.me, at].astype(F32)
            + self.near_in[1, at].astype(F32)
            + self.far_in[at].astype(F32)
        )

    def drain(self):
        self.corner.wait_send()
        self.near.wait_send()
        self.far.wait_send()


def window(start, size, unit=16):
    return pl.ds(pl.multiple_of(start, unit), size)


def each_rows(count, size, body):
    def step(number, carry):
        body(window(number * size, size))
        return carry

    lax.fori_loop(0, count // size, step, 0)


def add_rows(count, target, start, one, one_start, two, two_start):
    size = next(size for size in (128, 64, 48, 32, 16) if count % size == 0)

    def step(number, carry):
        moved = number * size
        total = (
            one[window(one_start + moved, size)].astype(F32)
            + two[window(two_start + moved, size)].astype(F32)
        )
        target[window(start + moved, size)] = total.astype(BF16)
        return carry

    lax.fori_loop(0, count // size, step, 0)


class Steps:
    def __init__(self, actions):
        self.actions = list(actions)

    def advance(self):
        if self.actions:
            self.actions.pop(0)()


def advance_all(chains):
    while any(chain.actions for chain in chains):
        for chain in chains:
            chain.advance()


class Reduce(Steps):
    def __init__(self, wire, place, source, start, slots, result, order, local_sem):
        self.place = place
        count, bits = slots.shape[0], len(order)
        here = [lax.rem(lax.div(place.col, 1 << bit), 2) for bit in order]
        offsets = [count - (count >> step) for step in range(bits + 1)]
        piece = count >> bits
        sends, keeps = [], []
        view, view_start = source, start
        for step, bit in enumerate(order):
            half = count >> (step + 1)
            away = view_start + (1 - here[step]) * half
            slot = slots.at[pl.ds(offsets[step], half)]
            sends.append(wire.copy(view.at[window(away, half)], slot, place.column(bit)))
            keeps.append((half, offsets[step], view, view_start + here[step] * half))
            view, view_start = slots, offsets[step]
        final = offsets[bits]
        last = pl.ds(offsets[bits - 1], piece)
        move = wire.copy(slots.at[last], slots.at[pl.ds(final, piece)], {"pair": 1 - place.pair})
        low = jnp.int32(0)
        for step in range(bits):
            low = low + here[step] * (count >> (step + 1))
        owned = result.at[window(low, piece)]
        keep_local = pltpu.make_async_copy(slots.at[pl.ds(final, piece)], owned, local_sem)
        shares = [wire.copy(slots.at[pl.ds(final, piece)], owned, place.sibling())]
        grows = []
        for step in reversed(range(bits)):
            size = count >> (step + 1)
            mine = result.at[window(low, size)]
            other_low = low + (1 - 2 * here[step]) * size
            other = result.at[window(other_low, size)]
            grows.append(wire.copy(mine, mine, place.column(order[step]), other))
            shares.append(wire.copy(other, other, place.sibling()))
            low = low - here[step] * size

        def stays(action):
            pl.when(place.stays)(action)

        def swapped(action):
            pl.when(place.swapped)(action)

        def gather_half(step):
            size, offset, view, start = keeps[step]
            sends[step].wait_recv()
            add_rows(size, slots, offset, slots, offset, view, start)

        def narrow(step):
            gather_half(step)
            sends[step + 1].start()

        def cross():
            gather_half(bits - 1)
            swapped(move.start)

        def settle():
            @stays
            def _():
                move.wait_recv()
                add_rows(piece, slots, final, slots, final, slots, offsets[bits - 1])
                keep_local.start()
                shares[0].start()
                keep_local.wait()
                grows[0].start()

        def widen(step):
            @stays
            def _():
                grows[step].wait_recv()
                if step + 1 < bits:
                    grows[step + 1].start()
                shares[step + 1].start()

        actions = [sends[0].start]
        actions += [functools.partial(narrow, step) for step in range(bits - 1)]
        actions += [cross, settle]
        actions += [functools.partial(widen, step) for step in range(bits)]
        super().__init__(actions)

        def finish():
            for one in sends:
                one.wait_send()

            @swapped
            def _():
                move.wait_send()
                for share in shares:
                    share.wait_recv()

            @stays
            def _():
                for one in grows + shares:
                    one.wait_send()

        self.finish = finish


class Weight:
    def __init__(self, wire, place, source, target, axis, start, size, order, local_sem):
        quarter = lax.rem(place.col, MEMBERS)
        if order[0] == 1:
            quarter = 2 * lax.rem(quarter, 2) + lax.div(quarter, 2)
        depth = size // MEMBERS

        def cut(ref, first, many):
            at = window(start + first, many)
            return ref.at[:, at] if axis == 1 else ref.at[at]

        other = quarter + 1 - 2 * lax.rem(quarter, 2)
        duo = lax.div(quarter, 2)
        mine = cut(target, quarter * depth, depth)
        both = cut(target, duo * 2 * depth, 2 * depth)
        rest = cut(target, (1 - duo) * 2 * depth, 2 * depth)
        self.moves = [
            wire.copy(cut(source, quarter * depth, depth), mine, place.trade()),
            wire.copy(mine, mine, place.column(order[0]), cut(target, other * depth, depth)),
            wire.copy(both, both, place.column(order[1]), rest),
        ]
        self.local = pltpu.make_async_copy(cut(source, 0, size), cut(target, 0, size), local_sem)

    def bring(self):
        self.moves[0].start()

    def pass_on(self, step):
        self.moves[step].wait_recv()
        self.moves[step + 1].start()

    def ready(self):
        self.moves[2].wait_recv()

    def drain(self):
        for one in self.moves:
            one.wait_send()


def scatter_shapes(rows, width):
    return [
        pltpu.VMEM((MEMBERS, rows, width), BF16),
        pltpu.VMEM((2, rows, width), BF16),
        pltpu.VMEM((rows, width), BF16),
        pltpu.VMEM((rows, width), BF16),
    ]


def visible_tile(first_ref, block, tile, rows):
    key_at = tile * rows + lax.broadcasted_iota(jnp.int32, (rows, rows), 0)
    query_at = block * rows + lax.broadcasted_iota(jnp.int32, (rows, rows), 1)
    first = first_ref[0:1, pl.ds(pl.multiple_of(block * rows, rows), rows)]
    return (key_at >= first) & (key_at <= query_at)


def swap_order(step):
    return lax.rem(step, 2), lax.div(step, 2)


def layer_kernel(
    items,
    bits,
    x_own, dy_own, lengths, gain_attn, gain_mlp, wq, wa, wi, wo,
    output, grad_frames, mlp_sums, attn_sums, gains_out,
    wq_m, wa_m, wi_m, wo_m,
    x_all, x_keep, dy_all, normed, normed_mlp, active, grad_hidden,
    qkv, keys_t, values_t, att_t, acc_t, lse, first, first_near, scores,
    part, near, joined, far_in, outs, near2, joined2, far2,
    resid, grad_resid, mlp_grads, mlp_slots, attn_grads, attn_slots, wa_slots,
    projected, gain_sum, gain_got, moved, moved_in, out_keep, out_in,
    send_sems, recv_sems, local_sems,
):
    place = Place()
    wire = Wire(send_sems, recv_sems)
    rows, width = x_keep.shape
    heads = qkv.shape[1]
    features = heads * HEAD
    me = place.me
    frame_count = MEMBERS * rows
    hidden_units = wi.shape[1]
    span = 256
    shift = (HEAD ** -0.5) * LOG2E
    scaling = HEAD ** -0.5
    near_member = place.member(1, 0)

    def when_swapped(action):
        pl.when(place.swapped)(action)

    def when_stays(action):
        pl.when(place.stays)(action)

    chunks = 2
    half = rows // chunks
    x_trades = []
    for number in range(chunks):
        at = pl.ds(number * half, half)
        x_trades.append(
            wire.copy(x_own.at[at], x_all.at[near_member, at], place.trade(), x_all.at[me, at])
        )
    dy_trade = wire.copy(dy_own, dy_all.at[near_member], place.trade(), dy_all.at[me])
    first_trade = wire.copy(first_near.at[0], first_near.at[1], place.sibling())
    x_local = pltpu.make_async_copy(x_own, x_all.at[me], local_sems.at[0])
    dy_local = pltpu.make_async_copy(dy_own, dy_all.at[me], local_sems.at[1])

    def weight(number, source, target, axis, start, size, order):
        return Weight(
            wire, place, source, target, axis, start, size, order, local_sems.at[2 + number]
        )

    part_units = wi.shape[0] // 2
    wq_part = weight(0, wq, wq_m, 1, 0, width, (0, 1))
    wa_part = weight(1, wa, wa_m, 0, 0, features, (1, 0))
    wi_parts = [
        weight(2 + n, wi, wi_m, 0, n * part_units, part_units, (n, 1 - n)) for n in range(2)
    ]
    part_units = wo.shape[0] // 2
    wo_parts = [
        weight(4 + n, wo, wo_m, 0, n * part_units, part_units, (n, 1 - n)) for n in range(2)
    ]
    weights = [wq_part, wa_part] + wi_parts + wo_parts

    meet(
        [place.sibling(), place.across(), place.trade(), {"pair": 1 - place.pair}]
        + [place.column(bit) for bit in range(bits)]
    )

    when_swapped(wq_part.bring)

    @when_stays
    def _():
        x_local.start()
        dy_local.start()
        for one in weights:
            one.local.start()

    position = lax.broadcasted_iota(jnp.int32, (8, frame_count), 1)
    begin = jnp.zeros((8, frame_count), jnp.int32)
    end = jnp.int32(0)
    for item in range(items):
        size = lengths[0, item]
        end = end + size
        begin = begin + jnp.where(position >= end, size, 0)
    first_near[0] = jnp.where(position >= end, position, begin)
    first_trade.start()

    gather_x = Gather(wire, place, x_all, chunks)
    gather_dy = Gather(wire, place, dy_all)
    gather_n = Gather(wire, place, normed_mlp)
    grad_all = x_all
    gather_g = Gather(wire, place, grad_all)

    @when_swapped
    def _():
        wq_part.pass_on(0)
        for one in x_trades:
            one.start()
        wq_part.pass_on(1)
        for number in range(chunks):
            x_trades[number].wait_recv()
            gather_x.start(number)
        wa_part.bring()
        dy_trade.start()

    @when_stays
    def _():
        x_local.wait()
        for number in range(chunks):
            gather_x.start(number)

    gain = gain_attn[...]

    def norm_block(member):
        def some(at):
            values = x_all[member, at].astype(F32)
            scale = lax.rsqrt(jnp.mean(values * values, axis=-1, keepdims=True) + EPSILON)
            normed[member, at] = (values * scale * gain).astype(BF16)

        each_rows(rows, 64, some)

    def project(member):
        source = normed[member]
        for kind in range(3):
            block = dot_nn(source, wq_m[kind])
            narrow = block.astype(BF16)
            for head in range(heads):
                qkv[kind, head, member] = narrow[:, head * HEAD : (head + 1) * HEAD]
            if kind == 1:
                keys_t[member] = block.T.astype(BF16)
            if kind == 2:
                values_t[member] = block.T.astype(BF16)

    def arrive(step, carry):
        member = place.member(*swap_order(step))

        @pl.when(step == 1)
        def _():
            for number in range(chunks):
                gather_x.take_near(number)

        @pl.when(step == 2)
        def _():
            for number in range(chunks):
                gather_x.take_far(number)

        @pl.when(step == 3)
        def _():
            for number in range(chunks):
                gather_x.take_corner(number)

        norm_block(member)

        @pl.when(step == 0)
        def _():
            when_swapped(wq_part.ready)
            when_stays(wq_part.local.wait)

        @pl.when((step == 2) & place.swapped)
        def _():
            wa_part.pass_on(0)

        project(member)
        return carry

    lax.fori_loop(0, MEMBERS, arrive, 0)
    x_keep[...] = x_all[me]
    first_trade.wait_recv()

    @when_swapped
    def _():
        first[...] = first_near[1]
        wa_part.pass_on(1)
        dy_trade.wait_recv()
        for one in wi_parts:
            one.bring()

    @when_stays
    def _():
        first[...] = first_near[0]
        dy_local.wait()
        wa_part.local.wait()

    gather_dy.start()
    scatter1 = Scatter(wire, place, part, near, joined, far_in)

    def attend(step, carry):
        block = place.member(*swap_order(3 - step))

        def score(tile, peaks):
            seen = visible_tile(first, block, tile, rows)
            higher = []
            for head in range(heads):
                raw = dot_nt(qkv[1, head, tile], qkv[0, head, block])
                raw = jnp.where(seen, raw, NEGATIVE)
                scores[head, tile] = raw
                higher.append(jnp.maximum(peaks[head], jnp.max(raw, axis=0, keepdims=True)))
            return tuple(higher)

        low = jnp.full((1, rows), NEGATIVE, F32)
        peaks = lax.fori_loop(0, block + 1, score, (low,) * heads)
        acc_t[...] = jnp.zeros_like(acc_t)

        def weigh(tile, totals):
            sums = []
            for head in range(heads):
                prob = jnp.exp2((scores[head, tile] - peaks[head]) * shift)
                sums.append(totals[head] + jnp.sum(prob, axis=0, keepdims=True))
                at = slice(head * HEAD, (head + 1) * HEAD)
                acc_t[at] += dot_nn(values_t[tile, at], prob.astype(BF16))
            return tuple(sums)

        none = jnp.zeros((1, rows), F32)
        totals = lax.fori_loop(0, block + 1, weigh, (none,) * heads)
        for head in range(heads):
            at = slice(head * HEAD, (head + 1) * HEAD)
            acc_t[at] = acc_t[at] / totals[head]
            lse[block, head : head + 1] = peaks[head] * shift + jnp.log2(totals[head])
        att_t[block] = acc_t[...].astype(BF16)

        @pl.when((step == 0) & place.swapped)
        def _():
            wa_part.ready()

        attended = acc_t[...].T.astype(BF16)
        part[block] = dot_nn(attended, wa_m[...]).astype(BF16)

        @pl.when(step == 0)
        def _():
            scatter1.send_corner()

        @pl.when(step == 1)
        def _():
            scatter1.send_far()

            @when_swapped
            def _():
                wi_parts[0].pass_on(0)
                wo_parts[0].bring()

        @pl.when(step == 2)
        def _():
            scatter1.send_near()

        @pl.when((step == 3) & place.swapped)
        def _():
            wi_parts[1].pass_on(0)
            wo_parts[1].bring()

        return carry

    lax.fori_loop(0, MEMBERS, attend, 0)

    gather_dy.take_near()
    gather_dy.take_far()

    @when_swapped
    def _():
        for one in wi_parts:
            one.pass_on(1)
        for one in wo_parts:
            one.pass_on(0)

    scatter1.wait()
    gain2 = gain_mlp[...]

    def add_resid(at):
        total = x_keep[at].astype(F32) + scatter1.total(at)
        resid[at] = total
        scale = lax.rsqrt(jnp.mean(total * total, axis=-1, keepdims=True) + EPSILON)
        normed_mlp[me, at] = (total * scale * gain2).astype(BF16)

    each_rows(rows, 64, add_resid)
    gather_n.start()
    gather_x.drain()
    scatter1.drain()

    @when_swapped
    def _():
        for one in wo_parts:
            one.pass_on(1)
        for one in wi_parts + wo_parts:
            one.ready()

    @when_stays
    def _():
        for one in wi_parts + wo_parts:
            one.local.wait()

    gather_dy.take_corner()
    scatter3 = Scatter(wire, place, part, near, joined, far_in)

    def feed(step, carry):
        flip_core = jnp.where((step == 1) | (step == 2), 1, 0)
        flip_chip = jnp.where(step >= 2, 1, 0)
        block = place.member(flip_core, flip_chip)

        @pl.when(step == 1)
        def _():
            gather_n.take_near()

        @pl.when(step == 2)
        def _():
            gather_n.take_far()
            gather_n.take_corner()

        def units(number, inner):
            at = pl.ds(pl.multiple_of(number * span, span), span)
            hidden = dot_nn(normed_mlp[block], wi_m[:, at])
            grad_active = dot_nt(dy_all[block], wo_m[at])
            square = hidden * hidden
            bend = jnp.tanh(GELU_A * hidden * (1.0 + GELU_B * square))
            upper = 0.5 * (1.0 + bend)
            active[block, :, at] = (hidden * upper).astype(BF16)
            slope = upper + 0.5 * hidden * (1.0 - bend * bend) * (
                GELU_A * (1.0 + 3.0 * GELU_B * square)
            )
            grad_hidden[block, :, at] = (grad_active * slope).astype(BF16)
            return inner

        lax.fori_loop(0, hidden_units // span, units, 0)

        def across_features(number, inner):
            at = pl.ds(pl.multiple_of(number * span, span), span)
            part[block, :, at] = dot_nt(grad_hidden[block], wi_m[at]).astype(BF16)
            outs[block, :, at] = dot_nn(active[block], wo_m[:, at]).astype(BF16)
            return inner

        lax.fori_loop(0, width // span, across_features, 0)

        @pl.when(step == 1)
        def _():
            scatter3.send_near()

        @pl.when(step == 2)
        def _():
            scatter3.send_corner()

        @pl.when(step == 3)
        def _():
            scatter3.send_far()

        return carry

    lax.fori_loop(0, MEMBERS, feed, 0)

    ahead, back = tuple(range(bits)), tuple(reversed(range(bits)))
    sum_in = Reduce(
        wire, place, mlp_grads, 0, mlp_slots.at[pl.ds(0, width)],
        mlp_sums.at[pl.ds(0, width)], ahead, local_sems.at[8],
    )
    sum_out = Reduce(
        wire, place, mlp_grads, width, mlp_slots.at[pl.ds(width, hidden_units)],
        mlp_sums.at[pl.ds(width, hidden_units)], back, local_sems.at[9],
    )
    split = 3 * width // 2
    sum_one = Reduce(
        wire, place, attn_grads, 0, attn_slots.at[pl.ds(0, split)],
        attn_sums.at[pl.ds(0, split)], ahead, local_sems.at[10],
    )
    sum_two = Reduce(
        wire, place, attn_grads, split, attn_slots.at[pl.ds(split, split)],
        attn_sums.at[pl.ds(split, split)], back, local_sems.at[11],
    )
    sum_proj = Reduce(
        wire, place, attn_grads, 3 * width, wa_slots,
        attn_sums.at[pl.ds(3 * width, width)], ahead, local_sems.at[12],
    )

    def in_grads(number, carry):
        at = pl.ds(pl.multiple_of(number * span, span), span)
        left = normed_mlp[:, :, at].reshape(frame_count, span)
        right = grad_hidden[...].reshape(frame_count, hidden_units)
        mlp_grads[at] = dot_tn(left, right).astype(BF16)
        return carry

    def out_grads(number, carry):
        at = pl.ds(pl.multiple_of(number * span, span), span)
        down = pl.ds(pl.multiple_of(width + number * span, span), span)
        left = active[:, :, at].reshape(frame_count, span)
        right = dy_all[...].reshape(frame_count, width)
        mlp_grads[down] = dot_tn(left, right).astype(BF16)
        return carry

    lax.fori_loop(0, width // span, in_grads, 0)
    sum_in.advance()
    lax.fori_loop(0, hidden_units // span, out_grads, 0)
    sum_out.advance()

    scatter3.wait()
    gain_sum[...] = jnp.zeros_like(gain_sum)

    def norm_back(at):
        grad = scatter3.total(at)
        values = resid[at]
        scale = lax.rsqrt(jnp.mean(values * values, axis=-1, keepdims=True) + EPSILON)
        gain_sum[0:1] += jnp.sum(grad * values * scale, axis=0, keepdims=True)
        scaled = grad * gain2
        mean = jnp.mean(scaled * values, axis=-1, keepdims=True)
        total = (
            dy_all[me, at].astype(F32) + scale * scaled - values * (scale * scale * scale) * mean
        )
        grad_resid[at] = total
        grad_all[me, at] = total.astype(BF16)

    each_rows(rows, 64, norm_back)
    gather_g.start()
    scatter3.drain()
    scatter2 = Scatter(wire, place, outs, near2, joined2, far2)
    scatter2.send_corner()
    scatter2.send_near()
    scores[...] = jnp.zeros_like(scores)

    def block_back(step, carry):
        block = place.member(*swap_order(step))

        @pl.when(step == 1)
        def _():
            gather_g.take_near()

        @pl.when(step == 2)
        def _():
            gather_g.take_far()
            scatter2.send_far()
            sum_in.advance()

        @pl.when(step == 3)
        def _():
            sum_out.advance()
            gather_g.take_corner()

        source = grad_all[block]
        top = dot_nt(source, wa_m[...]).astype(BF16)
        turned = dot_nt(wa_m[...], source).astype(BF16)
        tops = [top[:, head * HEAD : (head + 1) * HEAD] for head in range(heads)]
        product = turned.astype(F32) * att_t[block].astype(F32)
        deltas = [
            jnp.sum(product[head * HEAD : (head + 1) * HEAD], axis=0, keepdims=True)
            for head in range(heads)
        ]
        acc_t[...] = jnp.zeros_like(acc_t)

        def tiles(tile, inner):
            seen = visible_tile(first, block, tile, rows)
            for head in range(heads):
                at = slice(head * HEAD, (head + 1) * HEAD)
                query = qkv[0, head, block]
                raw = dot_nt(qkv[1, head, tile], query)
                prob = jnp.where(
                    seen, jnp.exp2(raw * shift - lse[block, head : head + 1]), 0.0
                )
                grad_prob = dot_nt(qkv[2, head, tile], tops[head])
                grad_score = (prob * (grad_prob - deltas[head])).astype(BF16)
                scores[head, tile, :, 128 : 128 + HEAD] += dot_nn(prob.astype(BF16), tops[head])
                scores[head, tile, :, 0:HEAD] += dot_nn(grad_score, query)
                acc_t[at] += dot_nn(keys_t[tile, at], grad_score)
            return inner

        lax.fori_loop(0, block + 1, tiles, 0)
        projected[0, block] = (acc_t[...].T * scaling).astype(BF16)
        return carry

    lax.fori_loop(0, MEMBERS, block_back, 0)

    def settle_heads(block, carry):
        for head in range(heads):
            at = slice(head * HEAD, (head + 1) * HEAD)
            grad_keys = scores[head, block, :, 0:HEAD] * scaling
            projected[1, block, :, at] = grad_keys.astype(BF16)
            projected[2, block, :, at] = scores[head, block, :, 128 : 128 + HEAD].astype(BF16)
        return carry

    lax.fori_loop(0, MEMBERS, settle_heads, 0)

    for kind in range(3):

        def qkv_grads(number, carry, kind=kind):
            at = pl.ds(pl.multiple_of(number * span, span), span)
            to = pl.ds(pl.multiple_of(kind * width + number * span, span), span)
            left = normed[:, :, at].reshape(frame_count, span)
            right = projected[kind].reshape(frame_count, features)
            attn_grads[to] = dot_tn(left, right).astype(BF16)
            return carry

        lax.fori_loop(0, width // span, qkv_grads, 0)

    sum_one.advance()
    sum_two.advance()
    scatter4 = Scatter(wire, place, part, near, joined, far_in)

    def inputs_back(step, carry):
        block = place.member(*swap_order(3 - step))

        def columns(number, inner):
            down = pl.ds(pl.multiple_of(number * span, span), span)
            total = dot_nt(projected[0, block], wq_m[0, down])
            total += dot_nt(projected[1, block], wq_m[1, down])
            total += dot_nt(projected[2, block], wq_m[2, down])
            part[block, :, down] = total.astype(BF16)
            return inner

        lax.fori_loop(0, width // span, columns, 0)

        @pl.when(step == 0)
        def _():
            scatter4.send_corner()

        @pl.when(step == 1)
        def _():
            scatter4.send_far()

        @pl.when(step == 2)
        def _():
            scatter4.send_near()

        return carry

    lax.fori_loop(0, MEMBERS, inputs_back, 0)

    def proj_grads(number, carry):
        at = pl.ds(pl.multiple_of(number * features, features), features)
        to = pl.ds(pl.multiple_of(3 * width + number * features, features), features)
        total = dot_nn(att_t[0], grad_all[0, :, at])
        for member in range(1, MEMBERS):
            total += dot_nn(att_t[member], grad_all[member, :, at])
        attn_grads[to] = total.astype(BF16)
        return carry

    lax.fori_loop(0, width // features, proj_grads, 0)
    sum_proj.advance()
    sum_in.advance()
    scatter2.wait()

    def finish_output(at):
        out_keep[at] = (resid[at] + scatter2.total(at)).astype(BF16)

    each_rows(rows, 64, finish_output)
    out_trade = wire.copy(out_keep, out_in, place.trade())
    when_swapped(out_trade.start)
    sum_out.advance()
    sum_one.advance()
    sum_two.advance()
    sum_proj.advance()

    scatter4.wait()

    def finish_frames(at):
        grad = scatter4.total(at)
        values = x_keep[at].astype(F32)
        scale = lax.rsqrt(jnp.mean(values * values, axis=-1, keepdims=True) + EPSILON)
        gain_sum[1:2] += jnp.sum(grad * values * scale, axis=0, keepdims=True)
        scaled = grad * gain
        mean = jnp.mean(scaled * values, axis=-1, keepdims=True)
        total = grad_resid[at] + scale * scaled - values * (scale * scale * scale) * mean
        grad_frames[at] = total
        moved[at] = total.astype(BF16)

    each_rows(rows, 64, finish_frames)
    frames_trade = wire.copy(moved, moved_in, place.trade())
    when_swapped(frames_trade.start)

    partners = [place.sibling(), place.across(), {"pair": 1 - place.pair}]
    partners += [place.column(bit) for bit in range(bits)]
    gain_trades = [
        wire.copy(gain_sum.at[pl.ds(8 * number, 8)], gain_got.at[number], partner)
        for number, partner in enumerate(partners)
    ]

    def gain_step(number):
        gain_trades[number].wait_recv()
        here = slice(8 * number, 8 * number + 8)
        gain_sum[8 * number + 8 : 8 * number + 16] = gain_sum[here] + gain_got[number]
        if number + 1 < len(gain_trades):
            gain_trades[number + 1].start()

    gain_trades[0].start()
    gain_chain = Steps([functools.partial(gain_step, n) for n in range(len(partners))])
    sums = [sum_one, sum_two, sum_proj, sum_in, sum_out]
    advance_all([gain_chain] + sums)
    gains_out[...] = gain_sum[8 * len(partners) : 8 * len(partners) + 8]

    @when_swapped
    def _():
        out_trade.wait_recv()
        output[...] = out_in[...]
        frames_trade.wait_recv()
        grad_frames[...] = moved_in[...].astype(F32)
        out_trade.wait_send()
        frames_trade.wait_send()
        for one in x_trades + [dy_trade]:
            one.wait_send()
        for one in weights:
            one.drain()

    @when_stays
    def _():
        output[...] = out_keep[...]

    for one in (gather_dy, gather_n, gather_g, scatter2, scatter4):
        one.drain()
    first_trade.wait_send()
    for one in gain_trades:
        one.wait_send()
    for one in sums:
        one.finish()


def layer_call(bits, x_own, dy_own, lengths, gain_attn, gain_mlp, wq, wa, wi, wo):
    rows, width = x_own.shape
    features = wa.shape[0]
    heads = features // HEAD
    units = wi.shape[1]
    frames = MEMBERS * rows
    steps = 3 + bits
    members = (MEMBERS, rows, width)
    block = pl.BlockSpec(memory_space=pltpu.VMEM)
    whole = pl.BlockSpec(memory_space=pl.ANY)
    outputs = [
        ((rows, width), BF16, block),
        ((rows, width), F32, block),
        ((width + units, width), BF16, whole),
        ((4 * width, features), BF16, whole),
        ((8, width), F32, block),
    ]
    scratch = [
        (wq.shape, BF16),
        (wa.shape, BF16),
        (wi.shape, BF16),
        (wo.shape, BF16),
        (members, BF16),
        ((rows, width), BF16),
        (members, BF16),
        (members, BF16),
        (members, BF16),
        ((MEMBERS, rows, units), BF16),
        ((MEMBERS, rows, units), BF16),
        ((3, heads, MEMBERS, rows, HEAD), BF16),
        ((MEMBERS, features, rows), BF16),
        ((MEMBERS, features, rows), BF16),
        ((MEMBERS, features, rows), BF16),
        ((features, rows), F32),
        ((MEMBERS, 8, rows), F32),
        ((8, frames), jnp.int32),
        ((2, 8, frames), jnp.int32),
        ((heads, MEMBERS, rows, rows), F32),
    ]
    scatter = [(members, BF16), ((2, rows, width), BF16), ((rows, width), BF16),
               ((rows, width), BF16)]
    scratch += scatter * 2
    scratch += [
        ((rows, width), F32),
        ((rows, width), F32),
        ((width + units, width), BF16),
        ((width + units, width), BF16),
        ((4 * width, features), BF16),
        ((3 * width, features), BF16),
        ((width, features), BF16),
        ((3, MEMBERS, rows, features), BF16),
        ((8 * steps + 8, width), F32),
        ((steps, 8, width), F32),
    ]
    scratch += [((rows, width), BF16)] * 4
    count = 64 + 5 * (3 * bits + 2)
    return pl.pallas_call(
        functools.partial(layer_kernel, lengths.shape[1], bits),
        out_shape=[jax.ShapeDtypeStruct(shape, kind) for shape, kind, _ in outputs],
        in_specs=[whole, whole, pl.BlockSpec(memory_space=pltpu.SMEM), block, block]
        + [whole] * 4,
        out_specs=[spec for _, _, spec in outputs],
        scratch_shapes=[pltpu.VMEM(shape, kind) for shape, kind in scratch]
        + [
            pltpu.SemaphoreType.DMA((count,)),
            pltpu.SemaphoreType.DMA((count,)),
            pltpu.SemaphoreType.DMA((13,)),
        ],
        compiler_params=pltpu.CompilerParams(
            collective_id=0, has_side_effects=True, vmem_limit_bytes=VMEM_LIMIT
        ),
        name="layer",
    )(x_own, dy_own, lengths, gain_attn, gain_mlp, wq, wa, wi, wo)


def per_device(bits, frames, lengths, wq, wa, wi, wo, gain_attn, gain_mlp, cotangent):
    width = frames.shape[1]
    features = wa.shape[0]
    output, grad_frames, mlp_sums, attn_sums, gains = layer_call(
        bits, frames, cotangent, lengths, gain_attn.reshape(1, width),
        gain_mlp.reshape(1, width), wq, wa, wi, wo,
    )
    mlp_sums = mlp_sums.astype(F32)
    attn_sums = attn_sums.astype(F32)
    grad_wq = attn_sums[: 3 * width].reshape(3, width, features)
    turned = attn_sums[3 * width :].reshape(width // features, features, features)
    grad_wa = jnp.transpose(turned, (1, 0, 2)).reshape(features, width)
    return (
        output,
        grad_frames,
        grad_wq,
        grad_wa,
        mlp_sums[:width],
        mlp_sums[width:],
        gains[1],
        gains[0],
    )


def solution(mesh):
    batches = mesh.shape["dp"]
    bits = (batches // 2).bit_length() - 1
    inner = Mesh(mesh.devices.reshape(batches // 2, 2, 2, 2), AXES)
    dp, mp = ("col", "core"), ("pair", "zz")
    rows = P(dp + mp, None)
    weights = (P(None, None, mp), P(mp, None), P(None, mp), P(mp, None))
    return jax.shard_map(
        functools.partial(per_device, bits),
        mesh=inner,
        in_specs=(rows, P(dp, None)) + weights + (P(), P(), rows),
        out_specs=(rows, rows) + weights + (P(), P()),
        check_vma=False,
    )
```

```python
import functools
import math

import jax
import jax.numpy as jnp
from jax import lax
from jax.experimental import pallas as pl
from jax.experimental.pallas import tpu as pltpu
from jax.sharding import Mesh
from jax.sharding import PartitionSpec as P

HEAD = 64
EPSILON = 1e-06
NEGATIVE = -1e30
MEMBERS = 4
LOG2E = math.log2(math.e)
GELU_A = math.sqrt(2.0 / math.pi)
GELU_B = 0.044715
AXES = ("col", "core", "pair", "zz")
BF16 = jnp.bfloat16
F32 = jnp.float32
VMEM_LIMIT = 62 << 20
MESH_ID = pl.DeviceIdType.MESH


def dot_nn(a, b):
    return lax.dot_general(a, b, (((1,), (0,)), ((), ())), preferred_element_type=F32)


def dot_nt(a, b):
    return lax.dot_general(a, b, (((1,), (1,)), ((), ())), preferred_element_type=F32)


def dot_tn(a, b):
    return lax.dot_general(a, b, (((0,), (0,)), ((), ())), preferred_element_type=F32)


def flip(bit, amount):
    return bit + amount - 2 * bit * amount


class Place:
    def __init__(self):
        self.col = lax.axis_index("col")
        self.core = lax.axis_index("core")
        self.pair = lax.axis_index("pair")
        self.zz = lax.axis_index("zz")
        self.swapped = self.core != self.pair
        self.stays = self.core == self.pair
        self.me = self.member(0, 0)

    def member(self, other_core, other_chip):
        return 2 * flip(self.core, other_core) + flip(self.zz, other_chip)

    def sibling(self):
        return {"core": 1 - self.core}

    def across(self):
        return {"zz": 1 - self.zz}

    def trade(self):
        return {"pair": 1 - self.pair, "core": 1 - self.core}

    def column(self, bit):
        step = 1 << bit
        here = lax.rem(lax.div(self.col, step), 2)
        return {"col": self.col + step * (1 - 2 * here)}


class Wire:
    def __init__(self, send_sems, recv_sems):
        self.send_sems = send_sems
        self.recv_sems = recv_sems
        self.used = 0

    def copy(self, src, dst, target, got=None):
        number = self.used
        self.used += 1
        return Transfer(
            src, dst, target, dst if got is None else got,
            self.send_sems.at[number], self.recv_sems.at[number],
        )


class Transfer:
    def __init__(self, src, dst, target, got, send_sem, recv_sem):
        self.args = (src, dst, target, got, send_sem, recv_sem)

    def start(self):
        src, dst, target, _, send_sem, recv_sem = self.args
        pltpu.make_async_remote_copy(
            src_ref=src, dst_ref=dst, send_sem=send_sem, recv_sem=recv_sem,
            device_id=target, device_id_type=MESH_ID,
        ).start()

    def wait_send(self):
        src, dst, target, _, send_sem, recv_sem = self.args
        pltpu.make_async_remote_copy(
            src_ref=src, dst_ref=dst, send_sem=send_sem, recv_sem=recv_sem,
            device_id=target, device_id_type=MESH_ID,
        ).wait_send()

    def wait_recv(self):
        _, _, target, got, send_sem, recv_sem = self.args
        pltpu.make_async_remote_copy(
            src_ref=got, dst_ref=got, send_sem=send_sem, recv_sem=recv_sem,
            device_id=target, device_id_type=MESH_ID,
        ).wait_recv()


def meet(targets):
    barrier = pltpu.get_barrier_semaphore()
    for target in targets:
        pl.semaphore_signal(barrier, inc=1, device_id=target, device_id_type=MESH_ID)
    pl.semaphore_wait(barrier, len(targets))


class Gather:
    def __init__(self, wire, place, whole, count=1):
        me, near = place.me, place.member(1, 0)
        far, corner = place.member(0, 1), place.member(1, 1)
        size = whole.shape[1] // count
        self.to_near, self.to_far, self.relay = [], [], []
        for number in range(count):
            at = pl.ds(number * size, size)
            mine, its, across, last = (whole.at[one, at] for one in (me, near, far, corner))
            self.to_near.append(wire.copy(mine, mine, place.sibling(), its))
            self.to_far.append(wire.copy(mine, mine, place.across(), across))
            self.relay.append(wire.copy(across, across, place.sibling(), last))

    def start(self, number=0):
        self.to_far[number].start()
        self.to_near[number].start()

    def take_near(self, number=0):
        self.to_near[number].wait_recv()

    def take_far(self, number=0):
        self.to_far[number].wait_recv()
        self.relay[number].start()

    def take_corner(self, number=0):
        self.relay[number].wait_recv()

    def drain(self):
        for one in self.to_near + self.to_far + self.relay:
            one.wait_send()


class Scatter:
    def __init__(self, wire, place, part, near_in, joined, far_in, count=1):
        self.place, self.part = place, part
        self.near_in, self.joined, self.far_in = near_in, joined, far_in
        corner, near = place.member(1, 1), place.member(1, 0)
        self.corner = wire.copy(part.at[corner], near_in.at[0], place.sibling())
        self.near = wire.copy(part.at[near], near_in.at[1], place.sibling())
        self.size = joined.shape[0] // count
        self.far = []
        for number in range(count):
            at = pl.ds(number * self.size, self.size)
            self.far.append(wire.copy(joined.at[at], far_in.at[at], place.across()))

    def send_corner(self):
        self.corner.start()

    def send_near(self):
        self.near.start()

    def send_far(self):
        self.corner.wait_recv()
        far = self.place.member(0, 1)

        def add(at):
            total = self.part[far, at].astype(F32) + self.near_in[0, at].astype(F32)
            self.joined[at] = total.astype(BF16)

        for number, one in enumerate(self.far):
            each_rows(self.size, 64, add, number * self.size)
            one.start()

    def finish(self, body, after=None):
        self.near.wait_recv()
        for number, one in enumerate(self.far):
            one.wait_recv()
            each_rows(self.size, 64, body, number * self.size)
            if after is not None:
                after(number)

    def total(self, at):
        return (
            self.part[self.place.me, at].astype(F32)
            + self.near_in[1, at].astype(F32)
            + self.far_in[at].astype(F32)
        )

    def drain(self):
        self.corner.wait_send()
        self.near.wait_send()
        for one in self.far:
            one.wait_send()


def window(start, size, unit=16):
    return pl.ds(pl.multiple_of(start, unit), size)


def each_rows(count, size, body, start=0):
    def step(number, carry):
        body(window(start + number * size, size))
        return carry

    lax.fori_loop(0, count // size, step, 0)


def add_rows(count, target, start, one, one_start, two, two_start):
    size = next(size for size in (128, 64, 48, 32, 16) if count % size == 0)

    def step(number, carry):
        moved = number * size
        total = (
            one[window(one_start + moved, size)].astype(F32)
            + two[window(two_start + moved, size)].astype(F32)
        )
        target[window(start + moved, size)] = total.astype(BF16)
        return carry

    lax.fori_loop(0, count // size, step, 0)


class Steps:
    def __init__(self, actions):
        self.actions = list(actions)

    def advance(self):
        if self.actions:
            self.actions.pop(0)()


def advance_all(chains):
    while any(chain.actions for chain in chains):
        for chain in chains:
            chain.advance()


class Reduce(Steps):
    def __init__(self, wire, place, source, start, slots, result, order, local_sem):
        self.place = place
        count, bits = slots.shape[0], len(order)
        here = [lax.rem(lax.div(place.col, 1 << bit), 2) for bit in order]
        offsets = [count - (count >> step) for step in range(bits + 1)]
        piece = count >> bits
        sends, keeps = [], []
        view, view_start = source, start
        for step, bit in enumerate(order):
            half = count >> (step + 1)
            away = view_start + (1 - here[step]) * half
            slot = slots.at[pl.ds(offsets[step], half)]
            sends.append(wire.copy(view.at[window(away, half)], slot, place.column(bit)))
            keeps.append((half, offsets[step], view, view_start + here[step] * half))
            view, view_start = slots, offsets[step]
        final = offsets[bits]
        last = pl.ds(offsets[bits - 1], piece)
        move = wire.copy(slots.at[last], slots.at[pl.ds(final, piece)], {"pair": 1 - place.pair})
        low = jnp.int32(0)
        for step in range(bits):
            low = low + here[step] * (count >> (step + 1))
        owned = result.at[window(low, piece)]
        keep_local = pltpu.make_async_copy(slots.at[pl.ds(final, piece)], owned, local_sem)
        whole = slots.at[pl.ds(final, piece)]
        shares = [wire.copy(whole, owned, place.sibling())]
        grows = []
        for step in reversed(range(bits)):
            size = count >> (step + 1)
            mine = result.at[window(low, size)]
            other_low = low + (1 - 2 * here[step]) * size
            other = result.at[window(other_low, size)]
            held = mine if grows else whole
            grows.append(wire.copy(held, mine, place.column(order[step]), other))
            shares.append(wire.copy(other, other, place.sibling()))
            low = low - here[step] * size

        def stays(action):
            pl.when(place.stays)(action)

        def swapped(action):
            pl.when(place.swapped)(action)

        def gather_half(step):
            size, offset, view, start = keeps[step]
            sends[step].wait_recv()
            add_rows(size, slots, offset, slots, offset, view, start)

        def narrow(step):
            gather_half(step)
            sends[step + 1].start()

        def cross():
            gather_half(bits - 1)
            swapped(move.start)

        def settle():
            @stays
            def _():
                move.wait_recv()
                add_rows(piece, slots, final, slots, final, slots, offsets[bits - 1])
                grows[0].start()
                shares[0].start()
                keep_local.start()

        def widen(step):
            @stays
            def _():
                grows[step].wait_recv()
                if step == 0:
                    keep_local.wait()
                if step + 1 < bits:
                    grows[step + 1].start()
                shares[step + 1].start()

        actions = [sends[0].start]
        actions += [functools.partial(narrow, step) for step in range(bits - 1)]
        actions += [cross, settle]
        actions += [functools.partial(widen, step) for step in range(bits)]
        super().__init__(actions)

        def finish():
            for one in sends:
                one.wait_send()

            @swapped
            def _():
                move.wait_send()
                for share in shares:
                    share.wait_recv()

            @stays
            def _():
                for one in grows + shares:
                    one.wait_send()

        self.finish = finish


class Weight:
    def __init__(self, wire, place, source, target, axis, start, size, order, local_sem):
        quarter = lax.rem(place.col, MEMBERS)
        if order[0] == 1:
            quarter = 2 * lax.rem(quarter, 2) + lax.div(quarter, 2)
        depth = size // MEMBERS

        def cut(ref, first, many):
            at = window(start + first, many)
            return ref.at[:, at] if axis == 1 else ref.at[at]

        other = quarter + 1 - 2 * lax.rem(quarter, 2)
        duo = lax.div(quarter, 2)
        mine = cut(target, quarter * depth, depth)
        both = cut(target, duo * 2 * depth, 2 * depth)
        rest = cut(target, (1 - duo) * 2 * depth, 2 * depth)
        self.moves = [
            wire.copy(cut(source, quarter * depth, depth), mine, place.trade()),
            wire.copy(mine, mine, place.column(order[0]), cut(target, other * depth, depth)),
            wire.copy(both, both, place.column(order[1]), rest),
        ]
        self.local = pltpu.make_async_copy(cut(source, 0, size), cut(target, 0, size), local_sem)

    def bring(self):
        self.moves[0].start()

    def pass_on(self, step):
        self.moves[step].wait_recv()
        self.moves[step + 1].start()

    def ready(self):
        self.moves[2].wait_recv()

    def drain(self):
        for one in self.moves:
            one.wait_send()


def scatter_shapes(rows, width):
    return [
        pltpu.VMEM((MEMBERS, rows, width), BF16),
        pltpu.VMEM((2, rows, width), BF16),
        pltpu.VMEM((rows, width), BF16),
        pltpu.VMEM((rows, width), BF16),
    ]


def visible_tile(first_ref, block, tile, rows):
    key_at = tile * rows + lax.broadcasted_iota(jnp.int32, (rows, rows), 0)
    query_at = block * rows + lax.broadcasted_iota(jnp.int32, (rows, rows), 1)
    first = first_ref[0:1, pl.ds(pl.multiple_of(block * rows, rows), rows)]
    return (key_at >= first) & (key_at <= query_at)


def swap_order(step):
    return lax.rem(step, 2), lax.div(step, 2)


def layer_kernel(
    items,
    bits,
    x_own, dy_own, lengths, gain_attn, gain_mlp, wq, wa, wi, wo,
    output, grad_frames, in_sums, out_sums, qkv_sums, wa_sums, gains_out,
    wq_m, wa_m, wi_m, wo_m,
    x_all, x_keep, dy_all, normed, normed_mlp, active, grad_hidden,
    qkv, keys_t, values_t, att_t, acc_t, lse, first, first_near, scores,
    part, near, joined, far_in, outs, near2, joined2, far2,
    resid, grad_resid, mlp_grads, mlp_slots, attn_grads, attn_slots, wa_grads, wa_slots,
    projected, gain_sum, gain_got, moved, moved_in, out_keep, out_in,
    send_sems, recv_sems, local_sems,
):
    place = Place()
    wire = Wire(send_sems, recv_sems)
    rows, width = x_keep.shape
    heads = qkv.shape[1]
    features = heads * HEAD
    me = place.me
    frame_count = MEMBERS * rows
    hidden_units = wi.shape[1]
    span = rows
    shift = (HEAD ** -0.5) * LOG2E
    scaling = HEAD ** -0.5
    near_member = place.member(1, 0)

    def when_swapped(action):
        pl.when(place.swapped)(action)

    def when_stays(action):
        pl.when(place.stays)(action)

    chunks = 2
    half = rows // chunks
    x_trades = []
    for number in range(chunks):
        at = pl.ds(number * half, half)
        x_trades.append(
            wire.copy(x_own.at[at], x_all.at[near_member, at], place.trade(), x_all.at[me, at])
        )
    dy_trade = wire.copy(dy_own, dy_all.at[near_member], place.trade(), dy_all.at[me])
    first_trade = wire.copy(first_near.at[0], first_near.at[1], place.sibling())
    x_local = pltpu.make_async_copy(x_own, x_all.at[me], local_sems.at[0])
    dy_local = pltpu.make_async_copy(dy_own, dy_all.at[me], local_sems.at[1])

    def weight(number, source, target, axis, start, size, order):
        return Weight(
            wire, place, source, target, axis, start, size, order, local_sems.at[2 + number]
        )

    def halves(number, source, target, axis):
        size = source.shape[axis] // 2
        return [
            weight(number + n, source, target, axis, n * size, size, (n, 1 - n)) for n in range(2)
        ]

    wq_parts = halves(0, wq, wq_m, 1)
    wi_parts = halves(2, wi, wi_m, 0)
    wo_parts = halves(4, wo, wo_m, 0)
    wa_part = weight(6, wa, wa_m, 0, 0, features, (1, 0))
    weights = wq_parts + [wa_part] + wi_parts + wo_parts

    meet(
        [place.sibling(), place.across(), place.trade(), {"pair": 1 - place.pair}]
        + [place.column(bit) for bit in range(bits)]
    )

    @when_swapped
    def _():
        for one in wq_parts:
            one.bring()
        for one in x_trades:
            one.start()
        wa_part.bring()

    @when_stays
    def _():
        x_local.start()
        dy_local.start()
        for one in weights:
            one.local.start()

    position = lax.broadcasted_iota(jnp.int32, (8, frame_count), 1)
    begin = jnp.zeros((8, frame_count), jnp.int32)
    end = jnp.int32(0)
    for item in range(items):
        size = lengths[0, item]
        end = end + size
        begin = begin + jnp.where(position >= end, size, 0)
    first_near[0] = jnp.where(position >= end, position, begin)
    first_trade.start()

    gather_x = Gather(wire, place, x_all, chunks)
    gather_dy = Gather(wire, place, dy_all)
    gather_n = Gather(wire, place, normed_mlp, chunks)
    grad_all = x_all
    slopes = scores
    gather_g = Gather(wire, place, grad_all, chunks)

    @when_swapped
    def _():
        for one in wq_parts:
            one.pass_on(0)
        for one in wq_parts:
            one.pass_on(1)
        for number in range(chunks):
            x_trades[number].wait_recv()
            gather_x.start(number)

    @when_stays
    def _():
        x_local.wait()
        for number in range(chunks):
            gather_x.start(number)
        dy_local.wait()
        gather_dy.start()

    gain = gain_attn[...]

    def norm_block(member):
        def some(at):
            values = x_all[member, at].astype(F32)
            scale = lax.rsqrt(jnp.mean(values * values, axis=-1, keepdims=True) + EPSILON)
            normed[member, at] = (values * scale * gain).astype(BF16)

        each_rows(rows, 64, some)

    def project(member):
        source = normed[member]
        for kind in range(3):
            block = dot_nn(source, wq_m[kind])
            narrow = block.astype(BF16)
            for head in range(heads):
                qkv[kind, head, member] = narrow[:, head * HEAD : (head + 1) * HEAD]
            if kind == 1:
                keys_t[member] = block.T.astype(BF16)
            if kind == 2:
                values_t[member] = block.T.astype(BF16)

    def arrive(step, carry):
        member = place.member(*swap_order(step))

        @pl.when(step == 1)
        def _():
            for number in range(chunks):
                gather_x.take_near(number)

        @pl.when(step == 2)
        def _():
            for number in range(chunks):
                gather_x.take_far(number)

            @when_swapped
            def _():
                for one in wi_parts:
                    one.bring()
                dy_trade.start()
                for one in wo_parts:
                    one.bring()

        @pl.when(step == 3)
        def _():
            for number in range(chunks):
                gather_x.take_corner(number)

        norm_block(member)

        @pl.when(step == 0)
        def _():
            for one in wq_parts:
                when_swapped(one.ready)
                when_stays(one.local.wait)

        @pl.when((step == 2) & place.swapped)
        def _():
            wa_part.pass_on(0)

        project(member)
        return carry

    lax.fori_loop(0, MEMBERS, arrive, 0)
    x_keep[...] = x_all[me]
    first_trade.wait_recv()

    @when_swapped
    def _():
        first[...] = first_near[1]
        wa_part.pass_on(1)

    @when_stays
    def _():
        first[...] = first_near[0]
        wa_part.local.wait()

    scatter1 = Scatter(wire, place, part, near, joined, far_in, chunks)

    def attend(step, carry):
        block = place.member(*swap_order(3 - step))

        def score(tile, peaks):
            seen = visible_tile(first, block, tile, rows)
            higher = []
            for head in range(heads):
                raw = dot_nt(qkv[1, head, tile], qkv[0, head, block])
                raw = jnp.where(seen, raw, NEGATIVE)
                scores[tile, :, head * rows : (head + 1) * rows] = raw
                higher.append(jnp.maximum(peaks[head], jnp.max(raw, axis=0, keepdims=True)))
            return tuple(higher)

        low = jnp.full((1, rows), NEGATIVE, F32)
        peaks = lax.fori_loop(0, block + 1, score, (low,) * heads)
        acc_t[...] = jnp.zeros_like(acc_t)

        def weigh(tile, totals):
            sums = []
            for head in range(heads):
                raw = scores[tile, :, head * rows : (head + 1) * rows]
                prob = jnp.exp2((raw - peaks[head]) * shift)
                sums.append(totals[head] + jnp.sum(prob, axis=0, keepdims=True))
                at = slice(head * HEAD, (head + 1) * HEAD)
                acc_t[at] += dot_nn(values_t[tile, at], prob.astype(BF16))
            return tuple(sums)

        none = jnp.zeros((1, rows), F32)
        totals = lax.fori_loop(0, block + 1, weigh, (none,) * heads)
        for head in range(heads):
            at = slice(head * HEAD, (head + 1) * HEAD)
            acc_t[at] = acc_t[at] / totals[head]
            lse[block, head : head + 1] = peaks[head] * shift + jnp.log2(totals[head])
        att_t[block] = acc_t[...].astype(BF16)

        @pl.when((step == 0) & place.swapped)
        def _():
            wa_part.ready()

        attended = acc_t[...].T.astype(BF16)
        part[block] = dot_nn(attended, wa_m[...]).astype(BF16)

        @pl.when(step == 0)
        def _():
            scatter1.send_corner()

        @pl.when(step == 1)
        def _():
            scatter1.send_far()

        @pl.when(step == 2)
        def _():
            scatter1.send_near()

        @pl.when((step == 2) & place.swapped)
        def _():
            wi_parts[0].pass_on(0)

        @pl.when((step == 3) & place.swapped)
        def _():
            wi_parts[1].pass_on(0)

        return carry

    lax.fori_loop(0, MEMBERS, attend, 0)

    @when_swapped
    def _():
        wi_parts[0].pass_on(1)
        wi_parts[1].pass_on(1)
        dy_trade.wait_recv()
        gather_dy.start()

    when_swapped(functools.partial(wo_parts[0].pass_on, 0))
    gain2 = gain_mlp[...]

    def add_resid(at):
        total = x_keep[at].astype(F32) + scatter1.total(at)
        resid[at] = total
        scale = lax.rsqrt(jnp.mean(total * total, axis=-1, keepdims=True) + EPSILON)
        normed_mlp[me, at] = (total * scale * gain2).astype(BF16)

    scatter1.finish(add_resid, gather_n.start)
    gather_dy.take_near()
    gather_x.drain()
    scatter1.drain()

    @when_swapped
    def _():
        for one in wi_parts:
            one.ready()

    @when_stays
    def _():
        for one in wi_parts + wo_parts:
            one.local.wait()

    scatter3 = Scatter(wire, place, part, near, joined, far_in, chunks)

    def feed_order(step):
        flip_core = jnp.where((step == 1) | (step == 2), 1, 0)
        flip_chip = jnp.where(step >= 2, 1, 0)
        return place.member(flip_core, flip_chip)

    def feed(step, carry):
        block = feed_order(step)

        @pl.when(step == 1)
        def _():
            for number in range(chunks):
                gather_n.take_near(number)

        @pl.when((step == 1) & place.swapped)
        def _():
            wo_parts[1].pass_on(0)
            wo_parts[0].pass_on(1)

        @pl.when(step == 2)
        def _():
            gather_dy.take_far()
            for number in range(chunks):
                gather_n.take_far(number)
            for number in range(chunks):
                gather_n.take_corner(number)

        @pl.when((step == 2) & place.swapped)
        def _():
            wo_parts[1].pass_on(1)

        hidden = dot_nn(normed_mlp[block], wi_m[...])
        square = hidden * hidden
        bend = jnp.tanh(GELU_A * hidden * (1.0 + GELU_B * square))
        upper = 0.5 * (1.0 + bend)
        active[block] = (hidden * upper).astype(BF16)
        slopes[block] = upper + 0.5 * hidden * (1.0 - bend * bend) * (
            GELU_A * (1.0 + 3.0 * GELU_B * square)
        )
        return carry

    lax.fori_loop(0, MEMBERS, feed, 0)
    gather_dy.take_corner()

    @when_swapped
    def _():
        for one in wo_parts:
            one.ready()

    def feed_back(step, carry):
        block = place.member(*swap_order(3 - step))

        grad_active = dot_nt(dy_all[block], wo_m[...])
        grad_hidden[block] = (grad_active * slopes[block]).astype(BF16)
        part[block] = dot_nt(grad_hidden[block], wi_m[...]).astype(BF16)

        @pl.when(step == 0)
        def _():
            scatter3.send_corner()

        @pl.when(step == 1)
        def _():
            scatter3.send_far()

        @pl.when(step == 2)
        def _():
            scatter3.send_near()

        return carry

    lax.fori_loop(0, MEMBERS, feed_back, 0)

    ahead, back = tuple(range(bits)), tuple(reversed(range(bits)))
    used = [9]

    def advance(*chains):
        for chain in chains:
            chain.advance()

    def reduce(source, start, slots, slot_start, result, result_start, size, order):
        used[0] += 1
        return Reduce(
            wire, place, source, start, slots.at[pl.ds(slot_start, size)],
            result.at[pl.ds(result_start, size)], order, local_sems.at[used[0] - 1],
        )

    quarter = width // 2
    sum_in = [
        reduce(mlp_grads, n * quarter, mlp_slots, n * quarter, in_sums, n * quarter, quarter, ahead)
        for n in range(2)
    ]
    quarter = hidden_units // 2
    sum_out = [
        reduce(
            mlp_grads, width + n * quarter, mlp_slots, width + n * quarter,
            out_sums, n * quarter, quarter, back,
        )
        for n in range(2)
    ]
    count = 4 if (3 * width // 4 >> bits) % 16 == 0 else 2
    split = 3 * width // count
    sum_qkv = [
        reduce(
            attn_grads, n * split, attn_slots, n * split, qkv_sums, n * split, split,
            back if n % 2 else ahead,
        )
        for n in range(count)
    ]
    sum_proj = reduce(wa_grads, 0, wa_slots, 0, wa_sums, 0, wa_grads.shape[0], ahead)

    def in_grads(number, carry):
        at = pl.ds(pl.multiple_of(number * span, span), span)
        left = normed_mlp[:, :, at].reshape(frame_count, span)
        right = grad_hidden[...].reshape(frame_count, hidden_units)
        mlp_grads[at] = dot_tn(left, right).astype(BF16)
        return carry

    def out_grads(number, carry):
        at = pl.ds(pl.multiple_of(number * span, span), span)
        down = pl.ds(pl.multiple_of(width + number * span, span), span)
        left = active[:, :, at].reshape(frame_count, span)
        right = dy_all[...].reshape(frame_count, width)
        mlp_grads[down] = dot_tn(left, right).astype(BF16)
        return carry

    for n in range(2):
        count = width // span // 2
        lax.fori_loop(n * count, (n + 1) * count, in_grads, 0)
        sum_in[n].advance()
        count = hidden_units // span // 2
        lax.fori_loop(n * count, (n + 1) * count, out_grads, 0)
        sum_out[n].advance()

    def feed_out(block, carry):
        outs[block] = dot_nn(active[block], wo_m[...]).astype(BF16)
        return carry

    lax.fori_loop(0, MEMBERS, feed_out, 0)
    scatter2 = Scatter(wire, place, outs, near2, joined2, far2)
    scatter2.send_corner()
    scatter2.send_near()
    gain_sum[...] = jnp.zeros_like(gain_sum)
    scores[...] = jnp.zeros_like(scores)

    def norm_back(at):
        grad = scatter3.total(at)
        values = resid[at]
        scale = lax.rsqrt(jnp.mean(values * values, axis=-1, keepdims=True) + EPSILON)
        gain_sum[0:1] += jnp.sum(grad * values * scale, axis=0, keepdims=True)
        scaled = grad * gain2
        mean = jnp.mean(scaled * values, axis=-1, keepdims=True)
        total = (
            dy_all[me, at].astype(F32) + scale * scaled - values * (scale * scale * scale) * mean
        )
        grad_resid[at] = total
        grad_all[me, at] = total.astype(BF16)

    scatter3.finish(norm_back, gather_g.start)
    scatter3.drain()
    scatter2.send_far()

    def block_back(step, carry):
        block = place.member(*swap_order(step))

        @pl.when(step == 1)
        def _():
            for number in range(chunks):
                gather_g.take_near(number)
            sum_in[0].advance()
            sum_out[0].advance()

        @pl.when(step == 2)
        def _():
            advance(sum_in[0], sum_out[0])
            for number in range(chunks):
                gather_g.take_far(number)
            advance(sum_in[1], sum_out[1])

        @pl.when(step == 3)
        def _():
            for number in range(chunks):
                gather_g.take_corner(number)

        source = grad_all[block]
        top = dot_nt(source, wa_m[...]).astype(BF16)
        turned = dot_nt(wa_m[...], source).astype(BF16)
        tops = [top[:, head * HEAD : (head + 1) * HEAD] for head in range(heads)]
        product = turned.astype(F32) * att_t[block].astype(F32)
        deltas = [
            jnp.sum(product[head * HEAD : (head + 1) * HEAD], axis=0, keepdims=True)
            for head in range(heads)
        ]
        acc_t[...] = jnp.zeros_like(acc_t)

        def tiles(tile, inner):
            seen = visible_tile(first, block, tile, rows)
            for head in range(heads):
                at = slice(head * HEAD, (head + 1) * HEAD)
                query = qkv[0, head, block]
                raw = dot_nt(qkv[1, head, tile], query)
                prob = jnp.where(
                    seen, jnp.exp2(raw * shift - lse[block, head : head + 1]), 0.0
                )
                grad_prob = dot_nt(qkv[2, head, tile], tops[head])
                grad_score = (prob * (grad_prob - deltas[head])).astype(BF16)
                scores[tile, :, head * 256 + 128 : head * 256 + 128 + HEAD] += dot_nn(
                    prob.astype(BF16), tops[head]
                )
                scores[tile, :, head * 256 : head * 256 + HEAD] += dot_nn(grad_score, query)
                acc_t[at] += dot_nn(keys_t[tile, at], grad_score)
            return inner

        lax.fori_loop(0, block + 1, tiles, 0)
        projected[0, block] = (acc_t[...].T * scaling).astype(BF16)
        return carry

    lax.fori_loop(0, MEMBERS, block_back, 0)

    def settle_heads(block, carry):
        for head in range(heads):
            at = slice(head * HEAD, (head + 1) * HEAD)
            grad_keys = scores[block, :, head * 256 : head * 256 + HEAD] * scaling
            projected[1, block, :, at] = grad_keys.astype(BF16)
            grad_values = scores[block, :, head * 256 + 128 : head * 256 + 128 + HEAD]
            projected[2, block, :, at] = grad_values.astype(BF16)
        return carry

    lax.fori_loop(0, MEMBERS, settle_heads, 0)

    def finish_output(at):
        out_keep[at] = (resid[at] + scatter2.total(at)).astype(BF16)

    scatter2.finish(finish_output)
    out_trade = wire.copy(out_keep, out_in, place.trade())
    when_swapped(out_trade.start)
    advance(sum_in[1], sum_out[1])

    def qkv_grads(kind, carry):
        to = pl.ds(pl.multiple_of(kind * width, width), width)
        left = normed[...].reshape(frame_count, width)
        right = projected[kind].reshape(frame_count, features)
        attn_grads[to] = dot_tn(left, right).astype(BF16)
        return carry

    for kind in range(3):
        lax.fori_loop(kind, kind + 1, qkv_grads, 0)
        done = (kind + 1) * count // 3
        advance(*sum_qkv[kind * count // 3 : done])
    scatter4 = Scatter(wire, place, part, near, joined, far_in, chunks)

    def inputs_back(step, carry):
        block = place.member(*swap_order(3 - step))

        total = dot_nt(projected[0, block], wq_m[0])
        total += dot_nt(projected[1, block], wq_m[1])
        total += dot_nt(projected[2, block], wq_m[2])
        part[block] = total.astype(BF16)

        @pl.when(step == 0)
        def _():
            scatter4.send_corner()

        @pl.when(step == 1)
        def _():
            scatter4.send_far()

        @pl.when(step == 2)
        def _():
            scatter4.send_near()

        return carry

    lax.fori_loop(0, MEMBERS, inputs_back, 0)

    if wa_grads.shape[1] == width:
        blocks = [att_t[member] for member in range(MEMBERS)]

        def proj_grads(number, carry):
            at = pl.ds(pl.multiple_of(number * span, span), span)
            total = dot_nn(blocks[0], grad_all[0, :, at])
            for member in range(1, MEMBERS):
                total += dot_nn(blocks[member], grad_all[member, :, at])
            wa_grads[:, at] = total.astype(BF16)
            return carry

        lax.fori_loop(0, width // span, proj_grads, 0)
    else:

        def proj_grads(number, carry):
            at = pl.ds(pl.multiple_of(number * features, features), features)
            total = dot_nn(att_t[0], grad_all[0, :, at])
            for member in range(1, MEMBERS):
                total += dot_nn(att_t[member], grad_all[member, :, at])
            wa_grads[at] = total.astype(BF16)
            return carry

        lax.fori_loop(0, width // features, proj_grads, 0)
    advance(sum_proj, sum_in[0], sum_out[0])
    advance(*sum_qkv[:2], sum_proj, *sum_qkv[2:], sum_in[0], sum_out[0])

    def finish_frames(at):
        grad = scatter4.total(at)
        values = x_keep[at].astype(F32)
        scale = lax.rsqrt(jnp.mean(values * values, axis=-1, keepdims=True) + EPSILON)
        gain_sum[1:2] += jnp.sum(grad * values * scale, axis=0, keepdims=True)
        scaled = grad * gain
        mean = jnp.mean(scaled * values, axis=-1, keepdims=True)
        total = grad_resid[at] + scale * scaled - values * (scale * scale * scale) * mean
        grad_frames[at] = total
        moved[at] = total.astype(BF16)

    frames_trades = []
    for number in range(chunks):
        at = pl.ds(number * half, half)
        frames_trades.append(wire.copy(moved.at[at], moved_in.at[at], place.trade()))

    scatter4.finish(finish_frames, lambda number: when_swapped(frames_trades[number].start))

    partners = [place.sibling(), place.across(), {"pair": 1 - place.pair}]
    partners += [place.column(bit) for bit in range(bits)]
    gain_trades = [
        wire.copy(gain_sum.at[pl.ds(8 * number, 8)], gain_got.at[number], partner)
        for number, partner in enumerate(partners)
    ]

    def gain_step(number):
        gain_trades[number].wait_recv()
        here = slice(8 * number, 8 * number + 8)
        gain_sum[8 * number + 8 : 8 * number + 16] = gain_sum[here] + gain_got[number]
        if number + 1 < len(gain_trades):
            gain_trades[number + 1].start()

    gain_trades[0].start()
    gain_chain = Steps([functools.partial(gain_step, n) for n in range(len(partners))])
    sums = sum_qkv + [sum_proj] + sum_in + sum_out
    early, late = sum_qkv[:2], sum_qkv[2:]
    advance(*early, sum_proj, sum_in[1], sum_out[1], *late, sum_in[0], sum_out[0], gain_chain)
    advance(sum_in[1], sum_out[1], *early, gain_chain, sum_proj, *late, gain_chain)
    advance(sum_in[1], sum_out[1], *early, sum_proj, *late, gain_chain)
    advance_all([gain_chain] + sums)
    gains_out[...] = gain_sum[8 * len(partners) : 8 * len(partners) + 8]

    @when_swapped
    def _():
        out_trade.wait_recv()
        output[...] = out_in[...]
        for one in frames_trades:
            one.wait_recv()
        grad_frames[...] = moved_in[...].astype(F32)
        for one in x_trades + frames_trades + [dy_trade, out_trade]:
            one.wait_send()
        for one in weights:
            one.drain()

    @when_stays
    def _():
        output[...] = out_keep[...]

    for one in (gather_dy, gather_n, gather_g, scatter2, scatter4):
        one.drain()
    first_trade.wait_send()
    for one in gain_trades:
        one.wait_send()
    for one in sums:
        one.finish()


def layer_call(bits, x_own, dy_own, lengths, gain_attn, gain_mlp, wq, wa, wi, wo):
    rows, width = x_own.shape
    features = wa.shape[0]
    heads = features // HEAD
    units = wi.shape[1]
    frames = MEMBERS * rows
    steps = 3 + bits
    members = (MEMBERS, rows, width)
    wa_shape = wa.shape if (features >> bits) % 16 == 0 else (width, features)
    block = pl.BlockSpec(memory_space=pltpu.VMEM)
    whole = pl.BlockSpec(memory_space=pl.ANY)
    outputs = [
        ((rows, width), BF16, block),
        ((rows, width), F32, block),
        ((width, units), BF16, whole),
        ((units, width), BF16, whole),
        ((3 * width, features), BF16, whole),
        (wa_shape, BF16, whole),
        ((8, width), F32, block),
    ]
    scratch = [
        (wq.shape, BF16),
        (wa.shape, BF16),
        (wi.shape, BF16),
        (wo.shape, BF16),
        (members, BF16),
        ((rows, width), BF16),
        (members, BF16),
        (members, BF16),
        (members, BF16),
        ((MEMBERS, rows, units), BF16),
        ((MEMBERS, rows, units), BF16),
        ((3, heads, MEMBERS, rows, HEAD), BF16),
        ((MEMBERS, features, rows), BF16),
        ((MEMBERS, features, rows), BF16),
        ((MEMBERS, features, rows), BF16),
        ((features, rows), F32),
        ((MEMBERS, 8, rows), F32),
        ((8, frames), jnp.int32),
        ((2, 8, frames), jnp.int32),
        ((MEMBERS, rows, max(heads * max(rows, 256), units)), F32),
    ]
    scatter = [(members, BF16), ((2, rows, width), BF16), ((rows, width), BF16),
               ((rows, width), BF16)]
    scratch += scatter * 2
    scratch += [
        ((rows, width), F32),
        ((rows, width), F32),
        ((width + units, width), BF16),
        ((width + units, width), BF16),
        ((3 * width, features), BF16),
        ((3 * width, features), BF16),
        (wa_shape, BF16),
        (wa_shape, BF16),
        ((3, MEMBERS, rows, features), BF16),
        ((8 * steps + 8, width), F32),
        ((steps, 8, width), F32),
    ]
    scratch += [((rows, width), BF16)] * 4
    count = 72 + 9 * (3 * bits + 2)
    return pl.pallas_call(
        functools.partial(layer_kernel, lengths.shape[1], bits),
        out_shape=[jax.ShapeDtypeStruct(shape, kind) for shape, kind, _ in outputs],
        in_specs=[whole, whole, pl.BlockSpec(memory_space=pltpu.SMEM), block, block]
        + [whole] * 4,
        out_specs=[spec for _, _, spec in outputs],
        scratch_shapes=[pltpu.VMEM(shape, kind) for shape, kind in scratch]
        + [
            pltpu.SemaphoreType.DMA((count,)),
            pltpu.SemaphoreType.DMA((count,)),
            pltpu.SemaphoreType.DMA((20,)),
        ],
        compiler_params=pltpu.CompilerParams(
            collective_id=0, has_side_effects=True, vmem_limit_bytes=VMEM_LIMIT
        ),
        name="layer",
    )(x_own, dy_own, lengths, gain_attn, gain_mlp, wq, wa, wi, wo)


def per_device(bits, frames, lengths, wq, wa, wi, wo, gain_attn, gain_mlp, cotangent):
    width = frames.shape[1]
    features = wa.shape[0]
    output, grad_frames, in_sums, out_sums, qkv_sums, wa_sums, gains = layer_call(
        bits, frames, cotangent, lengths, gain_attn.reshape(1, width),
        gain_mlp.reshape(1, width), wq, wa, wi, wo,
    )
    if wa_sums.shape != wa.shape:
        turned = wa_sums.reshape(width // features, features, features)
        wa_sums = jnp.transpose(turned, (1, 0, 2)).reshape(features, width)
    return (
        output,
        grad_frames,
        qkv_sums.astype(F32).reshape(3, width, features),
        wa_sums.astype(F32),
        in_sums.astype(F32),
        out_sums.astype(F32),
        gains[1],
        gains[0],
    )


def solution(mesh):
    batches = mesh.shape["dp"]
    bits = (batches // 2).bit_length() - 1
    inner = Mesh(mesh.devices.reshape(batches // 2, 2, 2, 2), AXES)
    dp, mp = ("col", "core"), ("pair", "zz")
    rows = P(dp + mp, None)
    weights = (P(None, None, mp), P(mp, None), P(None, mp), P(mp, None))
    return jax.shard_map(
        functools.partial(per_device, bits),
        mesh=inner,
        in_specs=(rows, P(dp, None)) + weights + (P(), P(), rows),
        out_specs=(rows, rows) + weights + (P(), P()),
        check_vma=False,
    )
```

```python
import functools
import math

import jax
import jax.numpy as jnp
from jax import lax
from jax.experimental import pallas as pl
from jax.experimental.pallas import tpu as pltpu
from jax.sharding import Mesh
from jax.sharding import PartitionSpec as P

HEAD = 64
EPSILON = 1e-06
NEGATIVE = -1e30
MEMBERS = 4
LOG2E = math.log2(math.e)
GELU_A = math.sqrt(2.0 / math.pi)
GELU_B = 0.044715
AXES = ("col", "core", "pair", "zz")
BF16 = jnp.bfloat16
F32 = jnp.float32
VMEM_LIMIT = 62 << 20
MESH_ID = pl.DeviceIdType.MESH


def dot_nn(a, b):
    return lax.dot_general(a, b, (((1,), (0,)), ((), ())), preferred_element_type=F32)


def dot_nt(a, b):
    return lax.dot_general(a, b, (((1,), (1,)), ((), ())), preferred_element_type=F32)


def dot_tn(a, b):
    return lax.dot_general(a, b, (((0,), (0,)), ((), ())), preferred_element_type=F32)


def flip(bit, amount):
    return bit + amount - 2 * bit * amount


class Place:
    def __init__(self):
        self.col = lax.axis_index("col")
        self.core = lax.axis_index("core")
        self.pair = lax.axis_index("pair")
        self.zz = lax.axis_index("zz")
        self.swapped = self.core != self.pair
        self.stays = self.core == self.pair
        self.me = self.member(0, 0)

    def member(self, other_core, other_chip):
        return 2 * flip(self.core, other_core) + flip(self.zz, other_chip)

    def sibling(self):
        return {"core": 1 - self.core}

    def across(self):
        return {"zz": 1 - self.zz}

    def trade(self):
        return {"pair": 1 - self.pair, "core": 1 - self.core}

    def column(self, bit):
        step = 1 << bit
        here = lax.rem(lax.div(self.col, step), 2)
        return {"col": self.col + step * (1 - 2 * here)}

    def columns(self):
        first, second = self.column(0)["col"], self.column(1)["col"]
        return [{"col": first + second - self.col}, {"col": first}, {"col": second}]


class Wire:
    def __init__(self, send_sems, recv_sems):
        self.send_sems = send_sems
        self.recv_sems = recv_sems
        self.used = 0

    def copy(self, src, dst, target, got=None):
        number = self.used
        self.used += 1
        return Transfer(
            src, dst, target, dst if got is None else got,
            self.send_sems.at[number], self.recv_sems.at[number],
        )


class Transfer:
    def __init__(self, src, dst, target, got, send_sem, recv_sem):
        self.args = (src, dst, target, got, send_sem, recv_sem)

    def start(self):
        src, dst, target, _, send_sem, recv_sem = self.args
        pltpu.make_async_remote_copy(
            src_ref=src, dst_ref=dst, send_sem=send_sem, recv_sem=recv_sem,
            device_id=target, device_id_type=MESH_ID,
        ).start()

    def wait_send(self):
        src, dst, target, _, send_sem, recv_sem = self.args
        pltpu.make_async_remote_copy(
            src_ref=src, dst_ref=dst, send_sem=send_sem, recv_sem=recv_sem,
            device_id=target, device_id_type=MESH_ID,
        ).wait_send()

    def wait_recv(self):
        _, _, target, got, send_sem, recv_sem = self.args
        pltpu.make_async_remote_copy(
            src_ref=got, dst_ref=got, send_sem=send_sem, recv_sem=recv_sem,
            device_id=target, device_id_type=MESH_ID,
        ).wait_recv()


def meet(targets):
    barrier = pltpu.get_barrier_semaphore()
    for target in targets:
        pl.semaphore_signal(barrier, inc=1, device_id=target, device_id_type=MESH_ID)
    pl.semaphore_wait(barrier, len(targets))


class Gather:
    def __init__(self, wire, place, whole, count=1):
        me, near = place.me, place.member(1, 0)
        far, corner = place.member(0, 1), place.member(1, 1)
        size = whole.shape[1] // count
        self.to_near, self.to_far, self.relay = [], [], []
        for number in range(count):
            at = pl.ds(number * size, size)
            mine, its, across, last = (whole.at[one, at] for one in (me, near, far, corner))
            self.to_near.append(wire.copy(mine, mine, place.sibling(), its))
            self.to_far.append(wire.copy(mine, mine, place.across(), across))
            self.relay.append(wire.copy(across, across, place.sibling(), last))

    def start(self, number=0):
        self.to_far[number].start()
        self.to_near[number].start()

    def take_near(self, number=0):
        self.to_near[number].wait_recv()

    def take_far(self, number=0):
        self.to_far[number].wait_recv()
        self.relay[number].start()

    def take_corner(self, number=0):
        self.relay[number].wait_recv()

    def drain(self):
        for one in self.to_near + self.to_far + self.relay:
            one.wait_send()


class Scatter:
    def __init__(self, wire, place, part, near_in, joined, far_in, count=1):
        self.place, self.part = place, part
        self.near_in, self.joined, self.far_in = near_in, joined, far_in
        corner, near = place.member(1, 1), place.member(1, 0)
        self.corner = wire.copy(part.at[corner], near_in.at[0], place.sibling())
        self.near = wire.copy(part.at[near], near_in.at[1], place.sibling())
        self.size = joined.shape[0] // count
        self.far = []
        for number in range(count):
            at = pl.ds(number * self.size, self.size)
            self.far.append(wire.copy(joined.at[at], far_in.at[at], place.across()))

    def send_corner(self):
        self.corner.start()

    def send_near(self):
        self.near.start()

    def send_far(self):
        self.corner.wait_recv()
        far = self.place.member(0, 1)

        def add(at):
            total = self.part[far, at].astype(F32) + self.near_in[0, at].astype(F32)
            self.joined[at] = total.astype(BF16)

        for number, one in enumerate(self.far):
            each_rows(self.size, 64, add, number * self.size)
            one.start()

    def finish(self, body, after=None):
        self.near.wait_recv()
        for number, one in enumerate(self.far):
            one.wait_recv()
            each_rows(self.size, 64, body, number * self.size)
            if after is not None:
                after(number)

    def total(self, at):
        return (
            self.part[self.place.me, at].astype(F32)
            + self.near_in[1, at].astype(F32)
            + self.far_in[at].astype(F32)
        )

    def drain(self):
        self.corner.wait_send()
        self.near.wait_send()
        for one in self.far:
            one.wait_send()


def window(start, size, unit=16):
    return pl.ds(pl.multiple_of(start, unit), size)


def each_rows(count, size, body, start=0):
    def step(number, carry):
        body(window(start + number * size, size))
        return carry

    lax.fori_loop(0, count // size, step, 0)


def add_rows(count, target, start, one, one_start, two, two_start):
    size = next(size for size in (128, 64, 48, 32, 16) if count % size == 0)

    def step(number, carry):
        moved = number * size
        total = (
            one[window(one_start + moved, size)].astype(F32)
            + two[window(two_start + moved, size)].astype(F32)
        )
        target[window(start + moved, size)] = total.astype(BF16)
        return carry

    lax.fori_loop(0, count // size, step, 0)


class Steps:
    def __init__(self, actions):
        self.actions = list(actions)

    def advance(self):
        if self.actions:
            self.actions.pop(0)()


def advance_all(chains):
    while any(chain.actions for chain in chains):
        for chain in chains:
            chain.advance()


class Reduce(Steps):
    def __init__(self, wire, place, source, start, slots, result, order, local_sem):
        self.place = place
        count, bits = slots.shape[0], len(order)
        here = [lax.rem(lax.div(place.col, 1 << bit), 2) for bit in order]
        offsets = [count - (count >> step) for step in range(bits + 1)]
        piece = count >> bits
        sends, keeps = [], []
        view, view_start = source, start
        for step, bit in enumerate(order):
            half = count >> (step + 1)
            away = view_start + (1 - here[step]) * half
            slot = slots.at[pl.ds(offsets[step], half)]
            sends.append(wire.copy(view.at[window(away, half)], slot, place.column(bit)))
            keeps.append((half, offsets[step], view, view_start + here[step] * half))
            view, view_start = slots, offsets[step]
        final = offsets[bits]
        last = pl.ds(offsets[bits - 1], piece)
        move = wire.copy(slots.at[last], slots.at[pl.ds(final, piece)], {"pair": 1 - place.pair})
        low = jnp.int32(0)
        for step in range(bits):
            low = low + here[step] * (count >> (step + 1))
        owned = result.at[window(low, piece)]
        keep_local = pltpu.make_async_copy(slots.at[pl.ds(final, piece)], owned, local_sem)
        whole = slots.at[pl.ds(final, piece)]
        shares = [wire.copy(whole, owned, place.sibling())]
        grows = []
        for step in reversed(range(bits)):
            size = count >> (step + 1)
            mine = result.at[window(low, size)]
            other_low = low + (1 - 2 * here[step]) * size
            other = result.at[window(other_low, size)]
            held = mine if grows else whole
            grows.append(wire.copy(held, mine, place.column(order[step]), other))
            shares.append(wire.copy(other, other, place.sibling()))
            low = low - here[step] * size

        def stays(action):
            pl.when(place.stays)(action)

        def swapped(action):
            pl.when(place.swapped)(action)

        def gather_half(step):
            size, offset, view, start = keeps[step]
            sends[step].wait_recv()
            add_rows(size, slots, offset, slots, offset, view, start)

        def narrow(step):
            gather_half(step)
            sends[step + 1].start()

        def cross():
            gather_half(bits - 1)
            swapped(move.start)

        def settle():
            @stays
            def _():
                move.wait_recv()
                add_rows(piece, slots, final, slots, final, slots, offsets[bits - 1])
                grows[0].start()
                shares[0].start()
                keep_local.start()

        def widen(step):
            @stays
            def _():
                grows[step].wait_recv()
                if step == 0:
                    keep_local.wait()
                if step + 1 < bits:
                    grows[step + 1].start()
                shares[step + 1].start()

        actions = [sends[0].start]
        actions += [functools.partial(narrow, step) for step in range(bits - 1)]
        actions += [cross, settle]
        actions += [functools.partial(widen, step) for step in range(bits)]
        super().__init__(actions)

        def finish():
            for one in sends:
                one.wait_send()

            @swapped
            def _():
                move.wait_send()
                for share in shares:
                    share.wait_recv()

            @stays
            def _():
                for one in grows + shares:
                    one.wait_send()

        self.finish = finish


class Weight:
    def __init__(self, wire, place, source, target, axis, start, size, local_sem):
        quarter = lax.rem(place.col, MEMBERS)
        depth = size // MEMBERS

        def cut(ref, first, many):
            at = window(start + first, many)
            return ref.at[:, at] if axis == 1 else ref.at[at]

        mine = cut(target, quarter * depth, depth)
        self.cross = wire.copy(cut(source, quarter * depth, depth), mine, place.trade())
        self.spread = []
        for other in place.columns():
            theirs = cut(target, lax.rem(other["col"], MEMBERS) * depth, depth)
            self.spread.append(wire.copy(mine, mine, other, theirs))
        self.local = pltpu.make_async_copy(cut(source, 0, size), cut(target, 0, size), local_sem)

    def bring(self):
        self.cross.start()

    def pass_on(self):
        self.cross.wait_recv()
        for one in self.spread:
            one.start()

    def ready(self):
        for one in self.spread:
            one.wait_recv()

    def drain(self):
        for one in [self.cross] + self.spread:
            one.wait_send()


def scatter_shapes(rows, width):
    return [
        pltpu.VMEM((MEMBERS, rows, width), BF16),
        pltpu.VMEM((2, rows, width), BF16),
        pltpu.VMEM((rows, width), BF16),
        pltpu.VMEM((rows, width), BF16),
    ]


def visible_tile(first_ref, block, tile, rows):
    key_at = tile * rows + lax.broadcasted_iota(jnp.int32, (rows, rows), 0)
    query_at = block * rows + lax.broadcasted_iota(jnp.int32, (rows, rows), 1)
    first = first_ref[0:1, pl.ds(pl.multiple_of(block * rows, rows), rows)]
    return (key_at >= first) & (key_at <= query_at)


def swap_order(step):
    return lax.rem(step, 2), lax.div(step, 2)


def layer_kernel(
    items,
    bits,
    x_own, dy_own, lengths, gain_attn, gain_mlp, wq, wa, wi, wo,
    output, grad_frames, in_sums, out_sums, qkv_sums, wa_sums, gains_out,
    wq_m, wa_m, wi_m, wo_m,
    x_all, x_keep, dy_all, normed, normed_mlp, active, grad_hidden,
    qkv, keys_t, values_t, att_t, acc_t, lse, first, first_near, scores,
    part, near, joined, far_in, outs, near2, joined2, far2,
    resid, grad_resid, mlp_grads, mlp_slots, attn_grads, attn_slots, wa_grads, wa_slots,
    projected, gain_sum, gain_got, moved, moved_in, out_keep, out_in,
    send_sems, recv_sems, local_sems,
):
    place = Place()
    wire = Wire(send_sems, recv_sems)
    rows, width = x_keep.shape
    heads = qkv.shape[1]
    features = heads * HEAD
    me = place.me
    frame_count = MEMBERS * rows
    hidden_units = wi.shape[1]
    span = rows
    shift = (HEAD ** -0.5) * LOG2E
    scaling = HEAD ** -0.5
    near_member = place.member(1, 0)

    def when_swapped(action):
        pl.when(place.swapped)(action)

    def when_stays(action):
        pl.when(place.stays)(action)

    chunks = 2
    half = rows // chunks
    x_trades = []
    for number in range(chunks):
        at = pl.ds(number * half, half)
        x_trades.append(
            wire.copy(x_own.at[at], x_all.at[near_member, at], place.trade(), x_all.at[me, at])
        )
    dy_trade = wire.copy(dy_own, dy_all.at[near_member], place.trade(), dy_all.at[me])
    first_trade = wire.copy(first_near.at[0], first_near.at[1], place.sibling())
    x_local = pltpu.make_async_copy(x_own, x_all.at[me], local_sems.at[0])
    dy_local = pltpu.make_async_copy(dy_own, dy_all.at[me], local_sems.at[1])

    def weight(number, source, target, axis, start, size):
        return Weight(wire, place, source, target, axis, start, size, local_sems.at[2 + number])

    def halves(number, source, target, axis):
        size = source.shape[axis] // 2
        return [
            weight(number + n, source, target, axis, n * size, size) for n in range(2)
        ]

    wq_parts = halves(0, wq, wq_m, 1)
    wi_parts = halves(2, wi, wi_m, 0)
    wo_parts = halves(4, wo, wo_m, 0)
    wa_part = weight(6, wa, wa_m, 0, 0, features)
    weights = wq_parts + [wa_part] + wi_parts + wo_parts

    meet(
        [place.sibling(), place.across(), place.trade(), {"pair": 1 - place.pair}]
        + place.columns()
        + [place.column(bit) for bit in range(2, bits)]
    )

    @when_swapped
    def _():
        for one in wq_parts:
            one.bring()
        for one in x_trades:
            one.start()
        wa_part.bring()

    @when_stays
    def _():
        x_local.start()
        dy_local.start()
        for one in weights:
            one.local.start()

    position = lax.broadcasted_iota(jnp.int32, (8, frame_count), 1)
    begin = jnp.zeros((8, frame_count), jnp.int32)
    end = jnp.int32(0)
    for item in range(items):
        size = lengths[0, item]
        end = end + size
        begin = begin + jnp.where(position >= end, size, 0)
    first_near[0] = jnp.where(position >= end, position, begin)
    first_trade.start()

    gather_x = Gather(wire, place, x_all, chunks)
    gather_dy = Gather(wire, place, dy_all)
    gather_n = Gather(wire, place, normed_mlp, chunks)
    grad_all = x_all
    slopes = scores
    gather_g = Gather(wire, place, grad_all, chunks)

    @when_swapped
    def _():
        for one in wq_parts:
            one.pass_on()
        for number in range(chunks):
            x_trades[number].wait_recv()
            gather_x.start(number)

    @when_stays
    def _():
        x_local.wait()
        for number in range(chunks):
            gather_x.start(number)
        dy_local.wait()
        gather_dy.start()

    gain = gain_attn[...]

    def norm_block(member):
        def some(at):
            values = x_all[member, at].astype(F32)
            scale = lax.rsqrt(jnp.mean(values * values, axis=-1, keepdims=True) + EPSILON)
            normed[member, at] = (values * scale * gain).astype(BF16)

        each_rows(rows, 64, some)

    def project(member):
        source = normed[member]
        for kind in range(3):
            block = dot_nn(source, wq_m[kind])
            narrow = block.astype(BF16)
            for head in range(heads):
                qkv[kind, head, member] = narrow[:, head * HEAD : (head + 1) * HEAD]
            if kind == 1:
                keys_t[member] = block.T.astype(BF16)
            if kind == 2:
                values_t[member] = block.T.astype(BF16)

    def arrive(step, carry):
        member = place.member(*swap_order(step))

        @pl.when(step == 1)
        def _():
            for number in range(chunks):
                gather_x.take_near(number)

        @pl.when(step == 2)
        def _():
            for number in range(chunks):
                gather_x.take_far(number)

            @when_swapped
            def _():
                for one in wi_parts:
                    one.bring()
                dy_trade.start()
                for one in wo_parts:
                    one.bring()

        @pl.when(step == 3)
        def _():
            for number in range(chunks):
                gather_x.take_corner(number)

        norm_block(member)

        @pl.when(step == 0)
        def _():
            for one in wq_parts:
                when_swapped(one.ready)
                when_stays(one.local.wait)

        @pl.when((step == 2) & place.swapped)
        def _():
            wa_part.pass_on()

        project(member)
        return carry

    lax.fori_loop(0, MEMBERS, arrive, 0)
    x_keep[...] = x_all[me]
    first_trade.wait_recv()

    @when_swapped
    def _():
        first[...] = first_near[1]

    @when_stays
    def _():
        first[...] = first_near[0]
        wa_part.local.wait()

    scatter1 = Scatter(wire, place, part, near, joined, far_in, chunks)

    def attend(step, carry):
        block = place.member(*swap_order(3 - step))

        def score(tile, peaks):
            seen = visible_tile(first, block, tile, rows)
            higher = []
            for head in range(heads):
                raw = dot_nt(qkv[1, head, tile], qkv[0, head, block])
                raw = jnp.where(seen, raw, NEGATIVE)
                scores[tile, :, head * rows : (head + 1) * rows] = raw
                higher.append(jnp.maximum(peaks[head], jnp.max(raw, axis=0, keepdims=True)))
            return tuple(higher)

        low = jnp.full((1, rows), NEGATIVE, F32)
        peaks = lax.fori_loop(0, block + 1, score, (low,) * heads)
        acc_t[...] = jnp.zeros_like(acc_t)

        def weigh(tile, totals):
            sums = []
            for head in range(heads):
                raw = scores[tile, :, head * rows : (head + 1) * rows]
                prob = jnp.exp2((raw - peaks[head]) * shift)
                sums.append(totals[head] + jnp.sum(prob, axis=0, keepdims=True))
                at = slice(head * HEAD, (head + 1) * HEAD)
                acc_t[at] += dot_nn(values_t[tile, at], prob.astype(BF16))
            return tuple(sums)

        none = jnp.zeros((1, rows), F32)
        totals = lax.fori_loop(0, block + 1, weigh, (none,) * heads)
        for head in range(heads):
            at = slice(head * HEAD, (head + 1) * HEAD)
            acc_t[at] = acc_t[at] / totals[head]
            lse[block, head : head + 1] = peaks[head] * shift + jnp.log2(totals[head])
        att_t[block] = acc_t[...].astype(BF16)

        @pl.when((step == 0) & place.swapped)
        def _():
            wa_part.ready()

        attended = acc_t[...].T.astype(BF16)
        part[block] = dot_nn(attended, wa_m[...]).astype(BF16)

        @pl.when(step == 0)
        def _():
            scatter1.send_corner()

        @pl.when(step == 1)
        def _():
            scatter1.send_far()

        @pl.when(step == 2)
        def _():
            scatter1.send_near()

        return carry

    lax.fori_loop(0, MEMBERS, attend, 0)

    @when_swapped
    def _():
        wi_parts[0].pass_on()
        wi_parts[1].pass_on()
        dy_trade.wait_recv()
        gather_dy.start()

    gain2 = gain_mlp[...]

    def add_resid(at):
        total = x_keep[at].astype(F32) + scatter1.total(at)
        resid[at] = total
        scale = lax.rsqrt(jnp.mean(total * total, axis=-1, keepdims=True) + EPSILON)
        normed_mlp[me, at] = (total * scale * gain2).astype(BF16)

    scatter1.finish(add_resid, gather_n.start)
    gather_dy.take_near()
    gather_x.drain()
    scatter1.drain()

    @when_swapped
    def _():
        for one in wi_parts:
            one.ready()

    @when_stays
    def _():
        for one in wi_parts + wo_parts:
            one.local.wait()

    scatter3 = Scatter(wire, place, part, near, joined, far_in, chunks)

    def feed_order(step):
        flip_core = jnp.where((step == 1) | (step == 2), 1, 0)
        flip_chip = jnp.where(step >= 2, 1, 0)
        return place.member(flip_core, flip_chip)

    def feed(step, carry):
        block = feed_order(step)

        @pl.when(step == 1)
        def _():
            for number in range(chunks):
                gather_n.take_near(number)

        @pl.when((step == 1) & place.swapped)
        def _():
            wo_parts[0].pass_on()

        @pl.when(step == 2)
        def _():
            gather_dy.take_far()
            for number in range(chunks):
                gather_n.take_far(number)
            for number in range(chunks):
                gather_n.take_corner(number)

        @pl.when((step == 2) & place.swapped)
        def _():
            wo_parts[1].pass_on()

        hidden = dot_nn(normed_mlp[block], wi_m[...])
        square = hidden * hidden
        bend = jnp.tanh(GELU_A * hidden * (1.0 + GELU_B * square))
        upper = 0.5 * (1.0 + bend)
        active[block] = (hidden * upper).astype(BF16)
        slopes[block] = upper + 0.5 * hidden * (1.0 - bend * bend) * (
            GELU_A * (1.0 + 3.0 * GELU_B * square)
        )
        return carry

    lax.fori_loop(0, MEMBERS, feed, 0)
    gather_dy.take_corner()
    ahead, back = tuple(range(bits)), tuple(reversed(range(bits)))
    used = [9]

    def advance(*chains):
        for chain in chains:
            chain.advance()

    def reduce(source, start, slots, slot_start, result, result_start, size, order):
        used[0] += 1
        return Reduce(
            wire, place, source, start, slots.at[pl.ds(slot_start, size)],
            result.at[pl.ds(result_start, size)], order, local_sems.at[used[0] - 1],
        )

    quarter = width // 2
    half_in, half_out = width // 2, hidden_units // 2
    sum_in = [
        reduce(
            mlp_grads, n * half_in, mlp_slots, n * half_in, in_sums, n * half_in, half_in, order
        )
        for n, order in enumerate((ahead, back))
    ]
    sum_out = [
        reduce(
            mlp_grads, width + n * half_out, mlp_slots, width + n * half_out,
            out_sums, n * half_out, half_out, order,
        )
        for n, order in enumerate((ahead, back))
    ]
    count = 4 if (3 * width // 4 >> bits) % 16 == 0 else 2
    split = 3 * width // count
    sum_qkv = [
        reduce(
            attn_grads, n * split, attn_slots, n * split, qkv_sums, n * split, split,
            back if n % 2 else ahead,
        )
        for n in range(count)
    ]
    sum_proj = reduce(wa_grads, 0, wa_slots, 0, wa_sums, 0, wa_grads.shape[0], ahead)

    def in_grads(number, carry):
        at = pl.ds(pl.multiple_of(number * span, span), span)
        left = normed_mlp[:, :, at].reshape(frame_count, span)
        right = grad_hidden[...].reshape(frame_count, hidden_units)
        mlp_grads[at] = dot_tn(left, right).astype(BF16)
        return carry

    def out_grads(number, carry):
        at = pl.ds(pl.multiple_of(number * span, span), span)
        down = pl.ds(pl.multiple_of(width + number * span, span), span)
        left = active[:, :, at].reshape(frame_count, span)
        right = dy_all[...].reshape(frame_count, width)
        mlp_grads[down] = dot_tn(left, right).astype(BF16)
        return carry

    tiles_here = hidden_units // span // 2
    for n in range(2):
        lax.fori_loop(n * tiles_here, (n + 1) * tiles_here, out_grads, 0)
        sum_out[n].advance()

    @when_swapped
    def _():
        for one in wo_parts:
            one.ready()

    def feed_back(step, carry):
        block = place.member(*swap_order(3 - step))

        grad_active = dot_nt(dy_all[block], wo_m[...])
        grad_hidden[block] = (grad_active * slopes[block]).astype(BF16)
        part[block] = dot_nt(grad_hidden[block], wi_m[...]).astype(BF16)

        @pl.when(step == 0)
        def _():
            scatter3.send_corner()

        @pl.when(step == 1)
        def _():
            scatter3.send_far()

        @pl.when(step == 2)
        def _():
            scatter3.send_near()

        return carry

    lax.fori_loop(0, MEMBERS, feed_back, 0)

    tiles_here = width // span // 2
    for n in range(2):
        lax.fori_loop(n * tiles_here, (n + 1) * tiles_here, in_grads, 0)
        sum_in[n].advance()

    def feed_out(block, carry):
        outs[block] = dot_nn(active[block], wo_m[...]).astype(BF16)
        return carry

    lax.fori_loop(0, MEMBERS, feed_out, 0)
    advance(*sum_out)
    scatter2 = Scatter(wire, place, outs, near2, joined2, far2)
    scatter2.send_corner()
    scatter2.send_near()
    gain_sum[...] = jnp.zeros_like(gain_sum)
    scores[...] = jnp.zeros_like(scores)

    def norm_back(at):
        grad = scatter3.total(at)
        values = resid[at]
        scale = lax.rsqrt(jnp.mean(values * values, axis=-1, keepdims=True) + EPSILON)
        gain_sum[0:1] += jnp.sum(grad * values * scale, axis=0, keepdims=True)
        scaled = grad * gain2
        mean = jnp.mean(scaled * values, axis=-1, keepdims=True)
        total = (
            dy_all[me, at].astype(F32) + scale * scaled - values * (scale * scale * scale) * mean
        )
        grad_resid[at] = total
        grad_all[me, at] = total.astype(BF16)

    scatter3.finish(norm_back, gather_g.start)
    scatter3.drain()
    scatter2.send_far()
    advance(*sum_out)

    def block_back(step, carry):
        block = place.member(*swap_order(step))

        @pl.when(step == 1)
        def _():
            for number in range(chunks):
                gather_g.take_near(number)
            advance(*sum_in)

        @pl.when(step == 2)
        def _():
            for number in range(chunks):
                gather_g.take_far(number)

        @pl.when(step == 3)
        def _():
            for number in range(chunks):
                gather_g.take_corner(number)
            advance(*sum_in)

        source = grad_all[block]
        top = dot_nt(source, wa_m[...]).astype(BF16)
        turned = dot_nt(wa_m[...], source).astype(BF16)
        tops = [top[:, head * HEAD : (head + 1) * HEAD] for head in range(heads)]
        product = turned.astype(F32) * att_t[block].astype(F32)
        deltas = [
            jnp.sum(product[head * HEAD : (head + 1) * HEAD], axis=0, keepdims=True)
            for head in range(heads)
        ]
        acc_t[...] = jnp.zeros_like(acc_t)

        def tiles(tile, inner):
            seen = visible_tile(first, block, tile, rows)
            for head in range(heads):
                at = slice(head * HEAD, (head + 1) * HEAD)
                query = qkv[0, head, block]
                raw = dot_nt(qkv[1, head, tile], query)
                prob = jnp.where(
                    seen, jnp.exp2(raw * shift - lse[block, head : head + 1]), 0.0
                )
                grad_prob = dot_nt(qkv[2, head, tile], tops[head])
                grad_score = (prob * (grad_prob - deltas[head])).astype(BF16)
                scores[tile, :, head * 256 + 128 : head * 256 + 128 + HEAD] += dot_nn(
                    prob.astype(BF16), tops[head]
                )
                scores[tile, :, head * 256 : head * 256 + HEAD] += dot_nn(grad_score, query)
                acc_t[at] += dot_nn(keys_t[tile, at], grad_score)
            return inner

        lax.fori_loop(0, block + 1, tiles, 0)
        projected[0, block] = (acc_t[...].T * scaling).astype(BF16)
        return carry

    lax.fori_loop(0, MEMBERS, block_back, 0)

    if wa_grads.shape[1] == width:
        blocks = [att_t[member] for member in range(MEMBERS)]

        def proj_grads(number, carry):
            at = pl.ds(pl.multiple_of(number * span, span), span)
            total = dot_nn(blocks[0], grad_all[0, :, at])
            for member in range(1, MEMBERS):
                total += dot_nn(blocks[member], grad_all[member, :, at])
            wa_grads[:, at] = total.astype(BF16)
            return carry

        lax.fori_loop(0, width // span, proj_grads, 0)
    else:

        def proj_grads(number, carry):
            at = pl.ds(pl.multiple_of(number * features, features), features)
            total = dot_nn(att_t[0], grad_all[0, :, at])
            for member in range(1, MEMBERS):
                total += dot_nn(att_t[member], grad_all[member, :, at])
            wa_grads[at] = total.astype(BF16)
            return carry

        lax.fori_loop(0, width // features, proj_grads, 0)
    advance(sum_proj)

    def settle_heads(block, carry):
        for head in range(heads):
            at = slice(head * HEAD, (head + 1) * HEAD)
            grad_keys = scores[block, :, head * 256 : head * 256 + HEAD] * scaling
            projected[1, block, :, at] = grad_keys.astype(BF16)
            grad_values = scores[block, :, head * 256 + 128 : head * 256 + 128 + HEAD]
            projected[2, block, :, at] = grad_values.astype(BF16)
        return carry

    lax.fori_loop(0, MEMBERS, settle_heads, 0)

    def finish_output(at):
        out_keep[at] = (resid[at] + scatter2.total(at)).astype(BF16)

    advance(*sum_out)

    def qkv_grads(kind, carry):
        to = pl.ds(pl.multiple_of(kind * width, width), width)
        left = normed[...].reshape(frame_count, width)
        right = projected[kind].reshape(frame_count, features)
        attn_grads[to] = dot_tn(left, right).astype(BF16)
        return carry

    for kind in range(3):
        lax.fori_loop(kind, kind + 1, qkv_grads, 0)
        done = (kind + 1) * count // 3
        advance(*sum_qkv[kind * count // 3 : done])
    scatter4 = Scatter(wire, place, part, near, joined, far_in, chunks)

    def inputs_back(step, carry):
        block = place.member(*swap_order(3 - step))

        total = dot_nt(projected[0, block], wq_m[0])
        total += dot_nt(projected[1, block], wq_m[1])
        total += dot_nt(projected[2, block], wq_m[2])
        part[block] = total.astype(BF16)

        @pl.when(step == 0)
        def _():
            scatter4.send_corner()

        @pl.when(step == 1)
        def _():
            scatter4.send_far()

        @pl.when(step == 2)
        def _():
            scatter4.send_near()

        return carry

    lax.fori_loop(0, MEMBERS, inputs_back, 0)

    scatter2.finish(finish_output)
    out_trade = wire.copy(out_keep, out_in, place.trade())
    when_swapped(out_trade.start)
    advance(sum_proj, *sum_out)
    advance(*sum_qkv[:2], *sum_qkv[2:], *sum_in)

    def finish_frames(at):
        grad = scatter4.total(at)
        values = x_keep[at].astype(F32)
        scale = lax.rsqrt(jnp.mean(values * values, axis=-1, keepdims=True) + EPSILON)
        gain_sum[1:2] += jnp.sum(grad * values * scale, axis=0, keepdims=True)
        scaled = grad * gain
        mean = jnp.mean(scaled * values, axis=-1, keepdims=True)
        total = grad_resid[at] + scale * scaled - values * (scale * scale * scale) * mean
        grad_frames[at] = total
        moved[at] = total.astype(BF16)

    frames_trades = []
    for number in range(chunks):
        at = pl.ds(number * half, half)
        frames_trades.append(wire.copy(moved.at[at], moved_in.at[at], place.trade()))

    scatter4.finish(finish_frames, lambda number: when_swapped(frames_trades[number].start))

    partners = [place.sibling(), place.across(), {"pair": 1 - place.pair}]
    partners += [place.column(bit) for bit in range(bits)]
    gain_trades = [
        wire.copy(gain_sum.at[pl.ds(8 * number, 8)], gain_got.at[number], partner)
        for number, partner in enumerate(partners)
    ]

    def gain_step(number):
        gain_trades[number].wait_recv()
        here = slice(8 * number, 8 * number + 8)
        gain_sum[8 * number + 8 : 8 * number + 16] = gain_sum[here] + gain_got[number]
        if number + 1 < len(gain_trades):
            gain_trades[number + 1].start()

    gain_trades[0].start()
    gain_chain = Steps([functools.partial(gain_step, n) for n in range(len(partners))])
    sums = sum_qkv + [sum_proj] + sum_in + sum_out
    early, late = sum_qkv[:2], sum_qkv[2:]
    advance(*early, sum_proj, *sum_out, *late, *sum_in, gain_chain)
    advance(*early, gain_chain, sum_proj, *late, gain_chain, *sum_in)
    advance(*early, sum_proj, *late, gain_chain)
    advance_all([gain_chain] + sums)
    gains_out[...] = gain_sum[8 * len(partners) : 8 * len(partners) + 8]

    @when_swapped
    def _():
        out_trade.wait_recv()
        output[...] = out_in[...]
        for one in frames_trades:
            one.wait_recv()
        grad_frames[...] = moved_in[...].astype(F32)
        for one in x_trades + frames_trades + [dy_trade, out_trade]:
            one.wait_send()
        for one in weights:
            one.drain()

    @when_stays
    def _():
        output[...] = out_keep[...]

    for one in (gather_dy, gather_n, gather_g, scatter2, scatter4):
        one.drain()
    first_trade.wait_send()
    for one in gain_trades:
        one.wait_send()
    for one in sums:
        one.finish()


def layer_call(bits, x_own, dy_own, lengths, gain_attn, gain_mlp, wq, wa, wi, wo):
    rows, width = x_own.shape
    features = wa.shape[0]
    heads = features // HEAD
    units = wi.shape[1]
    frames = MEMBERS * rows
    steps = 3 + bits
    members = (MEMBERS, rows, width)
    wa_shape = wa.shape if (features >> bits) % 16 == 0 else (width, features)
    block = pl.BlockSpec(memory_space=pltpu.VMEM)
    whole = pl.BlockSpec(memory_space=pl.ANY)
    outputs = [
        ((rows, width), BF16, block),
        ((rows, width), F32, block),
        ((width, units), BF16, whole),
        ((units, width), BF16, whole),
        ((3 * width, features), BF16, whole),
        (wa_shape, BF16, whole),
        ((8, width), F32, block),
    ]
    scratch = [
        (wq.shape, BF16),
        (wa.shape, BF16),
        (wi.shape, BF16),
        (wo.shape, BF16),
        (members, BF16),
        ((rows, width), BF16),
        (members, BF16),
        (members, BF16),
        (members, BF16),
        ((MEMBERS, rows, units), BF16),
        ((MEMBERS, rows, units), BF16),
        ((3, heads, MEMBERS, rows, HEAD), BF16),
        ((MEMBERS, features, rows), BF16),
        ((MEMBERS, features, rows), BF16),
        ((MEMBERS, features, rows), BF16),
        ((features, rows), F32),
        ((MEMBERS, 8, rows), F32),
        ((8, frames), jnp.int32),
        ((2, 8, frames), jnp.int32),
        ((MEMBERS, rows, max(heads * max(rows, 256), units)), F32),
    ]
    scatter = [(members, BF16), ((2, rows, width), BF16), ((rows, width), BF16),
               ((rows, width), BF16)]
    scratch += scatter * 2
    scratch += [
        ((rows, width), F32),
        ((rows, width), F32),
        ((width + units, width), BF16),
        ((width + units, width), BF16),
        ((3 * width, features), BF16),
        ((3 * width, features), BF16),
        (wa_shape, BF16),
        (wa_shape, BF16),
        ((3, MEMBERS, rows, features), BF16),
        ((8 * steps + 8, width), F32),
        ((steps, 8, width), F32),
    ]
    scratch += [((rows, width), BF16)] * 4
    count = 120 + 9 * (3 * bits + 2)
    return pl.pallas_call(
        functools.partial(layer_kernel, lengths.shape[1], bits),
        out_shape=[jax.ShapeDtypeStruct(shape, kind) for shape, kind, _ in outputs],
        in_specs=[whole, whole, pl.BlockSpec(memory_space=pltpu.SMEM), block, block]
        + [whole] * 4,
        out_specs=[spec for _, _, spec in outputs],
        scratch_shapes=[pltpu.VMEM(shape, kind) for shape, kind in scratch]
        + [
            pltpu.SemaphoreType.DMA((count,)),
            pltpu.SemaphoreType.DMA((count,)),
            pltpu.SemaphoreType.DMA((20,)),
        ],
        compiler_params=pltpu.CompilerParams(
            collective_id=0, has_side_effects=True, vmem_limit_bytes=VMEM_LIMIT
        ),
        name="layer",
    )(x_own, dy_own, lengths, gain_attn, gain_mlp, wq, wa, wi, wo)


def per_device(bits, frames, lengths, wq, wa, wi, wo, gain_attn, gain_mlp, cotangent):
    width = frames.shape[1]
    features = wa.shape[0]
    output, grad_frames, in_sums, out_sums, qkv_sums, wa_sums, gains = layer_call(
        bits, frames, cotangent, lengths, gain_attn.reshape(1, width),
        gain_mlp.reshape(1, width), wq, wa, wi, wo,
    )
    if wa_sums.shape != wa.shape:
        turned = wa_sums.reshape(width // features, features, features)
        wa_sums = jnp.transpose(turned, (1, 0, 2)).reshape(features, width)
    return (
        output,
        grad_frames,
        qkv_sums.astype(F32).reshape(3, width, features),
        wa_sums.astype(F32),
        in_sums.astype(F32),
        out_sums.astype(F32),
        gains[1],
        gains[0],
    )


def solution(mesh):
    batches = mesh.shape["dp"]
    bits = (batches // 2).bit_length() - 1
    inner = Mesh(mesh.devices.reshape(batches // 2, 2, 2, 2), AXES)
    dp, mp = ("col", "core"), ("pair", "zz")
    rows = P(dp + mp, None)
    weights = (P(None, None, mp), P(mp, None), P(None, mp), P(mp, None))
    return jax.shard_map(
        functools.partial(per_device, bits),
        mesh=inner,
        in_specs=(rows, P(dp, None)) + weights + (P(), P(), rows),
        out_specs=(rows, rows) + weights + (P(), P()),
        check_vma=False,
    )
```

```python
import functools
import math

import jax
import jax.numpy as jnp
from jax import lax
from jax.experimental import pallas as pl
from jax.experimental.pallas import tpu as pltpu
from jax.sharding import Mesh
from jax.sharding import PartitionSpec as P

HEAD = 64
EPSILON = 1e-06
NEGATIVE = -1e30
MEMBERS = 4
LOG2E = math.log2(math.e)
GELU_A = math.sqrt(2.0 / math.pi)
GELU_B = 0.044715
AXES = ("col", "core", "pair", "zz")
BF16 = jnp.bfloat16
F32 = jnp.float32
VMEM_LIMIT = 62 << 20
WIDEN_STEPS = 2
MESH_ID = pl.DeviceIdType.MESH


def dot_nn(a, b):
    return lax.dot_general(a, b, (((1,), (0,)), ((), ())), preferred_element_type=F32)


def dot_nt(a, b):
    return lax.dot_general(a, b, (((1,), (1,)), ((), ())), preferred_element_type=F32)


def dot_tn(a, b):
    return lax.dot_general(a, b, (((0,), (0,)), ((), ())), preferred_element_type=F32)


def flip(bit, amount):
    return bit + amount - 2 * bit * amount


class Place:
    def __init__(self):
        self.col = lax.axis_index("col")
        self.core = lax.axis_index("core")
        self.pair = lax.axis_index("pair")
        self.zz = lax.axis_index("zz")
        self.swapped = self.core != self.pair
        self.stays = self.core == self.pair
        self.me = self.member(0, 0)

    def member(self, other_core, other_chip):
        return 2 * flip(self.core, other_core) + flip(self.zz, other_chip)

    def sibling(self):
        return {"core": 1 - self.core}

    def across(self):
        return {"zz": 1 - self.zz}

    def trade(self):
        return {"pair": 1 - self.pair, "core": 1 - self.core}

    def column(self, bit):
        step = 1 << bit
        here = lax.rem(lax.div(self.col, step), 2)
        return {"col": self.col + step * (1 - 2 * here)}

    def columns(self):
        first, second = self.column(0)["col"], self.column(1)["col"]
        return [{"col": first + second - self.col}, {"col": first}, {"col": second}]


class Wire:
    def __init__(self, send_sems, recv_sems):
        self.send_sems = send_sems
        self.recv_sems = recv_sems
        self.used = 0

    def copy(self, src, dst, target, got=None):
        number = self.used
        self.used += 1
        return Transfer(
            src, dst, target, dst if got is None else got,
            self.send_sems.at[number], self.recv_sems.at[number],
        )


class Transfer:
    def __init__(self, src, dst, target, got, send_sem, recv_sem):
        self.args = (src, dst, target, got, send_sem, recv_sem)

    def start(self):
        src, dst, target, _, send_sem, recv_sem = self.args
        pltpu.make_async_remote_copy(
            src_ref=src, dst_ref=dst, send_sem=send_sem, recv_sem=recv_sem,
            device_id=target, device_id_type=MESH_ID,
        ).start()

    def wait_send(self):
        src, dst, target, _, send_sem, recv_sem = self.args
        pltpu.make_async_remote_copy(
            src_ref=src, dst_ref=dst, send_sem=send_sem, recv_sem=recv_sem,
            device_id=target, device_id_type=MESH_ID,
        ).wait_send()

    def wait_recv(self):
        _, _, target, got, send_sem, recv_sem = self.args
        pltpu.make_async_remote_copy(
            src_ref=got, dst_ref=got, send_sem=send_sem, recv_sem=recv_sem,
            device_id=target, device_id_type=MESH_ID,
        ).wait_recv()


def meet(targets):
    barrier = pltpu.get_barrier_semaphore()
    for target in targets:
        pl.semaphore_signal(barrier, inc=1, device_id=target, device_id_type=MESH_ID)
    pl.semaphore_wait(barrier, len(targets))


class Gather:
    def __init__(self, wire, place, whole, count=1):
        me, near = place.me, place.member(1, 0)
        far, corner = place.member(0, 1), place.member(1, 1)
        size = whole.shape[1] // count
        self.to_near, self.to_far, self.relay = [], [], []
        for number in range(count):
            at = pl.ds(number * size, size)
            mine, its, across, last = (whole.at[one, at] for one in (me, near, far, corner))
            self.to_near.append(wire.copy(mine, mine, place.sibling(), its))
            self.to_far.append(wire.copy(mine, mine, place.across(), across))
            self.relay.append(wire.copy(across, across, place.sibling(), last))

    def start(self, number=0):
        self.to_far[number].start()
        self.to_near[number].start()

    def take_near(self, number=0):
        self.to_near[number].wait_recv()

    def take_far(self, number=0):
        self.to_far[number].wait_recv()
        self.relay[number].start()

    def take_corner(self, number=0):
        self.relay[number].wait_recv()

    def drain(self):
        for one in self.to_near + self.to_far + self.relay:
            one.wait_send()


class Scatter:
    def __init__(self, wire, place, part, near_in, joined, far_in, count=1):
        self.place, self.part = place, part
        self.near_in, self.joined, self.far_in = near_in, joined, far_in
        corner, near = place.member(1, 1), place.member(1, 0)
        self.corner = wire.copy(part.at[corner], near_in.at[0], place.sibling())
        self.near = wire.copy(part.at[near], near_in.at[1], place.sibling())
        self.size = joined.shape[0] // count
        self.far = []
        for number in range(count):
            at = pl.ds(number * self.size, self.size)
            self.far.append(wire.copy(joined.at[at], far_in.at[at], place.across()))

    def send_corner(self):
        self.corner.start()

    def send_near(self):
        self.near.start()

    def send_far(self):
        self.corner.wait_recv()
        far = self.place.member(0, 1)

        def add(at):
            total = self.part[far, at].astype(F32) + self.near_in[0, at].astype(F32)
            self.joined[at] = total.astype(BF16)

        for number, one in enumerate(self.far):
            each_rows(self.size, 64, add, number * self.size)
            one.start()

    def finish(self, body, after=None):
        self.near.wait_recv()
        for number, one in enumerate(self.far):
            one.wait_recv()
            each_rows(self.size, 64, body, number * self.size)
            if after is not None:
                after(number)

    def total(self, at):
        return (
            self.part[self.place.me, at].astype(F32)
            + self.near_in[1, at].astype(F32)
            + self.far_in[at].astype(F32)
        )

    def drain(self):
        self.corner.wait_send()
        self.near.wait_send()
        for one in self.far:
            one.wait_send()


def window(start, size, unit=16):
    return pl.ds(pl.multiple_of(start, unit), size)


def each_rows(count, size, body, start=0):
    def step(number, carry):
        body(window(start + number * size, size))
        return carry

    lax.fori_loop(0, count // size, step, 0)


def add_rows(count, target, start, one, one_start, two, two_start):
    size = next(size for size in (128, 64, 48, 32, 16) if count % size == 0)

    def step(number, carry):
        moved = number * size
        total = (
            one[window(one_start + moved, size)].astype(F32)
            + two[window(two_start + moved, size)].astype(F32)
        )
        target[window(start + moved, size)] = total.astype(BF16)
        return carry

    lax.fori_loop(0, count // size, step, 0)


class Steps:
    def __init__(self, actions):
        self.actions = list(actions)

    def advance(self):
        if self.actions:
            self.actions.pop(0)()


def advance_all(chains):
    while any(chain.actions for chain in chains):
        for chain in chains:
            chain.advance()


class Reduce(Steps):
    def __init__(self, wire, place, source, start, slots, result, order, local_sem):
        self.place = place
        count, bits = slots.shape[0], len(order)
        here = [lax.rem(lax.div(place.col, 1 << bit), 2) for bit in order]
        offsets = [count - (count >> step) for step in range(bits + 1)]
        piece = count >> bits
        sends, keeps = [], []
        view, view_start = source, start
        for step, bit in enumerate(order):
            half = count >> (step + 1)
            away = view_start + (1 - here[step]) * half
            slot = slots.at[pl.ds(offsets[step], half)]
            sends.append(wire.copy(view.at[window(away, half)], slot, place.column(bit)))
            keeps.append((half, offsets[step], view, view_start + here[step] * half))
            view, view_start = slots, offsets[step]
        final = offsets[bits]
        last = pl.ds(offsets[bits - 1], piece)
        move = wire.copy(slots.at[last], slots.at[pl.ds(final, piece)], {"pair": 1 - place.pair})
        low = jnp.int32(0)
        for step in range(bits):
            low = low + here[step] * (count >> (step + 1))
        owned = result.at[window(low, piece)]
        keep_local = pltpu.make_async_copy(slots.at[pl.ds(final, piece)], owned, local_sem)
        whole = slots.at[pl.ds(final, piece)]
        shares = [wire.copy(whole, owned, place.sibling())]
        grows = []
        for step in reversed(range(bits)):
            size = count >> (step + 1)
            mine = result.at[window(low, size)]
            other_low = low + (1 - 2 * here[step]) * size
            other = result.at[window(other_low, size)]
            held = mine if grows else whole
            grows.append(wire.copy(held, mine, place.column(order[step]), other))
            shares.append(wire.copy(other, other, place.sibling()))
            low = low - here[step] * size

        def stays(action):
            pl.when(place.stays)(action)

        def swapped(action):
            pl.when(place.swapped)(action)

        def gather_half(step):
            size, offset, view, start = keeps[step]
            sends[step].wait_recv()
            add_rows(size, slots, offset, slots, offset, view, start)

        def narrow(step):
            gather_half(step)
            sends[step + 1].start()

        def cross():
            gather_half(bits - 1)
            swapped(move.start)

        def settle():
            @stays
            def _():
                move.wait_recv()
                add_rows(piece, slots, final, slots, final, slots, offsets[bits - 1])
                grows[0].start()
                shares[0].start()
                keep_local.start()

        def widen(step):
            @stays
            def _():
                grows[step].wait_recv()
                if step == 0:
                    keep_local.wait()
                if step + 1 < bits:
                    grows[step + 1].start()
                shares[step + 1].start()

        actions = [sends[0].start]
        actions += [functools.partial(narrow, step) for step in range(bits - 1)]
        actions += [cross, settle]
        actions += [functools.partial(widen, step) for step in range(bits)]
        super().__init__(actions)

        def finish():
            for one in sends:
                one.wait_send()

            @swapped
            def _():
                move.wait_send()
                for share in shares:
                    share.wait_recv()

            @stays
            def _():
                for one in grows + shares:
                    one.wait_send()

        self.finish = finish


class Weight:
    def __init__(self, wire, place, source, target, axis, start, size, local_sem):
        quarter = lax.rem(place.col, MEMBERS)
        depth = size // MEMBERS

        def cut(ref, first, many):
            at = window(start + first, many)
            return ref.at[:, at] if axis == 1 else ref.at[at]

        mine = cut(target, quarter * depth, depth)
        self.cross = wire.copy(cut(source, quarter * depth, depth), mine, place.trade())
        self.spread = []
        for other in place.columns():
            theirs = cut(target, lax.rem(other["col"], MEMBERS) * depth, depth)
            self.spread.append(wire.copy(mine, mine, other, theirs))
        self.local = pltpu.make_async_copy(cut(source, 0, size), cut(target, 0, size), local_sem)

    def bring(self):
        self.cross.start()

    def pass_on(self):
        self.cross.wait_recv()
        for one in self.spread:
            one.start()

    def ready(self):
        for one in self.spread:
            one.wait_recv()

    def drain(self):
        for one in [self.cross] + self.spread:
            one.wait_send()


def scatter_shapes(rows, width):
    return [
        pltpu.VMEM((MEMBERS, rows, width), BF16),
        pltpu.VMEM((2, rows, width), BF16),
        pltpu.VMEM((rows, width), BF16),
        pltpu.VMEM((rows, width), BF16),
    ]


def visible_tile(first_ref, block, tile, rows):
    key_at = tile * rows + lax.broadcasted_iota(jnp.int32, (rows, rows), 0)
    query_at = block * rows + lax.broadcasted_iota(jnp.int32, (rows, rows), 1)
    first = first_ref[0:1, pl.ds(pl.multiple_of(block * rows, rows), rows)]
    return (key_at >= first) & (key_at <= query_at)


def swap_order(step):
    return lax.rem(step, 2), lax.div(step, 2)


def layer_kernel(
    items,
    bits,
    x_own, dy_own, lengths, gain_attn, gain_mlp, wq, wa, wi, wo,
    output, grad_frames, in_sums, out_sums, qkv_sums, wa_sums, gains_out,
    wq_m, wa_m, wi_m, wo_m,
    x_all, x_keep, dy_all, normed, normed_mlp, active, grad_hidden,
    qkv, keys_t, values_t, att_t, acc_t, lse, first, first_near, scores,
    part, near, joined, far_in, outs, near2, joined2, far2,
    resid, grad_resid, mlp_grads, mlp_slots, attn_grads, attn_slots, wa_grads, wa_slots,
    projected, gain_sum, gain_got, moved, moved_in, out_keep, out_in,
    send_sems, recv_sems, local_sems,
):
    place = Place()
    wire = Wire(send_sems, recv_sems)
    rows, width = x_keep.shape
    heads = qkv.shape[1]
    features = heads * HEAD
    me = place.me
    frame_count = MEMBERS * rows
    hidden_units = wi.shape[1]
    span = rows
    shift = (HEAD ** -0.5) * LOG2E
    scaling = HEAD ** -0.5
    near_member = place.member(1, 0)

    def when_swapped(action):
        pl.when(place.swapped)(action)

    def when_stays(action):
        pl.when(place.stays)(action)

    chunks = 2
    half = rows // chunks
    x_trades = []
    for number in range(chunks):
        at = pl.ds(number * half, half)
        x_trades.append(
            wire.copy(x_own.at[at], x_all.at[near_member, at], place.trade(), x_all.at[me, at])
        )
    dy_trade = wire.copy(dy_own, dy_all.at[near_member], place.trade(), dy_all.at[me])
    first_trade = wire.copy(first_near.at[0], first_near.at[1], place.sibling())
    x_local = pltpu.make_async_copy(x_own, x_all.at[me], local_sems.at[0])
    dy_local = pltpu.make_async_copy(dy_own, dy_all.at[me], local_sems.at[1])

    def weight(number, source, target, axis, start, size):
        return Weight(wire, place, source, target, axis, start, size, local_sems.at[2 + number])

    def halves(number, source, target, axis):
        size = source.shape[axis] // 2
        return [
            weight(number + n, source, target, axis, n * size, size) for n in range(2)
        ]

    wq_parts = halves(0, wq, wq_m, 1)
    wi_parts = halves(2, wi, wi_m, 0)
    wo_parts = halves(4, wo, wo_m, 0)
    wa_part = weight(6, wa, wa_m, 0, 0, features)
    weights = wq_parts + [wa_part] + wi_parts + wo_parts

    meet(
        [place.sibling(), place.across(), place.trade(), {"pair": 1 - place.pair}]
        + place.columns()
        + [place.column(bit) for bit in range(2, bits)]
    )

    @when_swapped
    def _():
        for one in wq_parts:
            one.bring()
        for one in x_trades:
            one.start()
        wa_part.bring()

    @when_stays
    def _():
        x_local.start()
        dy_local.start()
        for one in weights:
            one.local.start()

    position = lax.broadcasted_iota(jnp.int32, (8, frame_count), 1)
    begin = jnp.zeros((8, frame_count), jnp.int32)
    end = jnp.int32(0)
    for item in range(items):
        size = lengths[0, item]
        end = end + size
        begin = begin + jnp.where(position >= end, size, 0)
    first_near[0] = jnp.where(position >= end, position, begin)
    first_trade.start()

    gather_x = Gather(wire, place, x_all, chunks)
    gather_dy = Gather(wire, place, dy_all)
    gather_n = Gather(wire, place, normed_mlp, chunks)
    grad_all = x_all
    slopes = scores
    gather_g = Gather(wire, place, grad_all, chunks)

    @when_swapped
    def _():
        for one in wq_parts:
            one.pass_on()
        for number in range(chunks):
            x_trades[number].wait_recv()
            gather_x.start(number)

    @when_stays
    def _():
        x_local.wait()
        for number in range(chunks):
            gather_x.start(number)
        dy_local.wait()
        gather_dy.start()

    gain = gain_attn[...]

    def norm_block(member):
        def some(at):
            values = x_all[member, at].astype(F32)
            scale = lax.rsqrt(jnp.mean(values * values, axis=-1, keepdims=True) + EPSILON)
            normed[member, at] = (values * scale * gain).astype(BF16)

        each_rows(rows, 64, some)

    def project(member):
        source = normed[member]
        for kind in range(3):
            block = dot_nn(source, wq_m[kind])
            narrow = block.astype(BF16)
            for head in range(heads):
                qkv[kind, head, member] = narrow[:, head * HEAD : (head + 1) * HEAD]
            if kind == 1:
                keys_t[member] = block.T.astype(BF16)
            if kind == 2:
                values_t[member] = block.T.astype(BF16)

    def arrive(step, carry):
        member = place.member(*swap_order(step))

        @pl.when(step == 1)
        def _():
            for number in range(chunks):
                gather_x.take_near(number)

        @pl.when(step == 2)
        def _():
            for number in range(chunks):
                gather_x.take_far(number)

            @when_swapped
            def _():
                for one in wi_parts:
                    one.bring()
                dy_trade.start()
                for one in wo_parts:
                    one.bring()

        @pl.when(step == 3)
        def _():
            for number in range(chunks):
                gather_x.take_corner(number)

        norm_block(member)

        @pl.when(step == 0)
        def _():
            for one in wq_parts:
                when_swapped(one.ready)
                when_stays(one.local.wait)

        @pl.when((step == 2) & place.swapped)
        def _():
            wa_part.pass_on()

        project(member)
        return carry

    lax.fori_loop(0, MEMBERS, arrive, 0)
    x_keep[...] = x_all[me]
    first_trade.wait_recv()

    @when_swapped
    def _():
        first[...] = first_near[1]

    @when_stays
    def _():
        first[...] = first_near[0]
        wa_part.local.wait()

    scatter1 = Scatter(wire, place, part, near, joined, far_in, chunks)

    def attend(step, carry):
        block = place.member(*swap_order(3 - step))

        def score(tile, peaks):
            seen = visible_tile(first, block, tile, rows)
            higher = []
            for head in range(heads):
                raw = dot_nt(qkv[1, head, tile], qkv[0, head, block])
                raw = jnp.where(seen, raw, NEGATIVE)
                scores[tile, :, head * rows : (head + 1) * rows] = raw
                higher.append(jnp.maximum(peaks[head], jnp.max(raw, axis=0, keepdims=True)))
            return tuple(higher)

        low = jnp.full((1, rows), NEGATIVE, F32)
        peaks = lax.fori_loop(0, block + 1, score, (low,) * heads)
        acc_t[...] = jnp.zeros_like(acc_t)

        def weigh(tile, totals):
            sums = []
            for head in range(heads):
                raw = scores[tile, :, head * rows : (head + 1) * rows]
                prob = jnp.exp2((raw - peaks[head]) * shift)
                sums.append(totals[head] + jnp.sum(prob, axis=0, keepdims=True))
                at = slice(head * HEAD, (head + 1) * HEAD)
                acc_t[at] += dot_nn(values_t[tile, at], prob.astype(BF16))
            return tuple(sums)

        none = jnp.zeros((1, rows), F32)
        totals = lax.fori_loop(0, block + 1, weigh, (none,) * heads)
        for head in range(heads):
            at = slice(head * HEAD, (head + 1) * HEAD)
            acc_t[at] = acc_t[at] / totals[head]
            lse[block, head : head + 1] = peaks[head] * shift + jnp.log2(totals[head])
        att_t[block] = acc_t[...].astype(BF16)

        @pl.when((step == 0) & place.swapped)
        def _():
            wa_part.ready()

        attended = acc_t[...].T.astype(BF16)
        part[block] = dot_nn(attended, wa_m[...]).astype(BF16)

        @pl.when(step == 0)
        def _():
            scatter1.send_corner()

        @pl.when(step == 1)
        def _():
            scatter1.send_far()

        @pl.when(step == 2)
        def _():
            scatter1.send_near()

        return carry

    lax.fori_loop(0, MEMBERS, attend, 0)

    @when_swapped
    def _():
        wi_parts[0].pass_on()
        wi_parts[1].pass_on()
        dy_trade.wait_recv()
        gather_dy.start()

    gain2 = gain_mlp[...]

    def add_resid(at):
        total = x_keep[at].astype(F32) + scatter1.total(at)
        resid[at] = total
        scale = lax.rsqrt(jnp.mean(total * total, axis=-1, keepdims=True) + EPSILON)
        normed_mlp[me, at] = (total * scale * gain2).astype(BF16)

    scatter1.finish(add_resid, gather_n.start)
    gather_dy.take_near()
    gather_x.drain()
    scatter1.drain()

    @when_swapped
    def _():
        for one in wi_parts:
            one.ready()

    @when_stays
    def _():
        for one in wi_parts + wo_parts:
            one.local.wait()

    scatter3 = Scatter(wire, place, part, near, joined, far_in, chunks)

    def feed_order(step):
        flip_core = jnp.where((step == 1) | (step == 2), 1, 0)
        flip_chip = jnp.where(step >= 2, 1, 0)
        return place.member(flip_core, flip_chip)

    def feed(step, carry):
        block = feed_order(step)

        @pl.when(step == 1)
        def _():
            for number in range(chunks):
                gather_n.take_near(number)

        @pl.when((step == 1) & place.swapped)
        def _():
            wo_parts[0].pass_on()

        @pl.when(step == 2)
        def _():
            gather_dy.take_far()
            for number in range(chunks):
                gather_n.take_far(number)
            for number in range(chunks):
                gather_n.take_corner(number)

        @pl.when((step == 2) & place.swapped)
        def _():
            wo_parts[1].pass_on()

        hidden = dot_nn(normed_mlp[block], wi_m[...])
        square = hidden * hidden
        bend = jnp.tanh(GELU_A * hidden * (1.0 + GELU_B * square))
        upper = 0.5 * (1.0 + bend)
        active[block] = (hidden * upper).astype(BF16)
        slopes[block] = upper + 0.5 * hidden * (1.0 - bend * bend) * (
            GELU_A * (1.0 + 3.0 * GELU_B * square)
        )
        return carry

    lax.fori_loop(0, MEMBERS, feed, 0)
    gather_dy.take_corner()
    ahead, back = tuple(range(bits)), tuple(reversed(range(bits)))
    used = [9]

    def advance(*chains):
        for chain in chains:
            chain.advance()

    def reduce(source, start, slots, slot_start, result, result_start, size, order):
        used[0] += 1
        return Reduce(
            wire, place, source, start, slots.at[pl.ds(slot_start, size)],
            result.at[pl.ds(result_start, size)], order, local_sems.at[used[0] - 1],
        )

    quarter = width // 2
    half_in, half_out = width // 2, hidden_units // 2
    sum_in = [
        reduce(
            mlp_grads, n * half_in, mlp_slots, n * half_in, in_sums, n * half_in, half_in, order
        )
        for n, order in enumerate((ahead, back))
    ]
    sum_out = [
        reduce(
            mlp_grads, width + n * half_out, mlp_slots, width + n * half_out,
            out_sums, n * half_out, half_out, order,
        )
        for n, order in enumerate((ahead, back))
    ]
    count = 4 if (3 * width // 4 >> bits) % 16 == 0 else 2
    split = 3 * width // count
    sum_qkv = [
        reduce(
            attn_grads, n * split, attn_slots, n * split, qkv_sums, n * split, split,
            back if n % 2 else ahead,
        )
        for n in range(count)
    ]
    sum_proj = reduce(wa_grads, 0, wa_slots, 0, wa_sums, 0, wa_grads.shape[0], ahead)

    def in_grads(number, carry):
        at = pl.ds(pl.multiple_of(number * span, span), span)
        left = normed_mlp[:, :, at].reshape(frame_count, span)
        right = grad_hidden[...].reshape(frame_count, hidden_units)
        mlp_grads[at] = dot_tn(left, right).astype(BF16)
        return carry

    def out_grads(number, carry):
        at = pl.ds(pl.multiple_of(number * span, span), span)
        down = pl.ds(pl.multiple_of(width + number * span, span), span)
        left = active[:, :, at].reshape(frame_count, span)
        right = dy_all[...].reshape(frame_count, width)
        mlp_grads[down] = dot_tn(left, right).astype(BF16)
        return carry

    tiles_here = hidden_units // span // 2
    for n in range(2):
        lax.fori_loop(n * tiles_here, (n + 1) * tiles_here, out_grads, 0)
        sum_out[n].advance()

    @when_swapped
    def _():
        for one in wo_parts:
            one.ready()

    def feed_back(step, carry):
        block = place.member(*swap_order(3 - step))

        grad_active = dot_nt(dy_all[block], wo_m[...])
        grad_hidden[block] = (grad_active * slopes[block]).astype(BF16)
        part[block] = dot_nt(grad_hidden[block], wi_m[...]).astype(BF16)

        @pl.when(step == 0)
        def _():
            scatter3.send_corner()

        @pl.when(step == 1)
        def _():
            scatter3.send_far()

        @pl.when(step == 2)
        def _():
            scatter3.send_near()

        return carry

    lax.fori_loop(0, MEMBERS, feed_back, 0)

    tiles_here = width // span // 2
    for n in range(2):
        lax.fori_loop(n * tiles_here, (n + 1) * tiles_here, in_grads, 0)
        sum_in[n].advance()

    def feed_out(block, carry):
        outs[block] = dot_nn(active[block], wo_m[...]).astype(BF16)
        return carry

    lax.fori_loop(0, MEMBERS, feed_out, 0)
    advance(*sum_out)
    scatter2 = Scatter(wire, place, outs, near2, joined2, far2)
    scatter2.send_corner()
    scatter2.send_near()
    gain_sum[...] = jnp.zeros_like(gain_sum)
    scores[...] = jnp.zeros_like(scores)

    def norm_back(at):
        grad = scatter3.total(at)
        values = resid[at]
        scale = lax.rsqrt(jnp.mean(values * values, axis=-1, keepdims=True) + EPSILON)
        gain_sum[0:1] += jnp.sum(grad * values * scale, axis=0, keepdims=True)
        scaled = grad * gain2
        mean = jnp.mean(scaled * values, axis=-1, keepdims=True)
        total = (
            dy_all[me, at].astype(F32) + scale * scaled - values * (scale * scale * scale) * mean
        )
        grad_resid[at] = total
        grad_all[me, at] = total.astype(BF16)

    scatter3.finish(norm_back, gather_g.start)
    scatter3.drain()
    scatter2.send_far()
    advance(*sum_out)

    def block_back(step, carry):
        block = place.member(*swap_order(step))

        @pl.when(step == 1)
        def _():
            for number in range(chunks):
                gather_g.take_near(number)
            advance(*sum_in)

        @pl.when(step == 2)
        def _():
            for number in range(chunks):
                gather_g.take_far(number)

        @pl.when(step == 3)
        def _():
            for number in range(chunks):
                gather_g.take_corner(number)
            advance(*sum_in)

        source = grad_all[block]
        top = dot_nt(source, wa_m[...]).astype(BF16)
        turned = dot_nt(wa_m[...], source).astype(BF16)
        tops = [top[:, head * HEAD : (head + 1) * HEAD] for head in range(heads)]
        product = turned.astype(F32) * att_t[block].astype(F32)
        deltas = [
            jnp.sum(product[head * HEAD : (head + 1) * HEAD], axis=0, keepdims=True)
            for head in range(heads)
        ]
        acc_t[...] = jnp.zeros_like(acc_t)

        def tiles(tile, inner):
            seen = visible_tile(first, block, tile, rows)
            for head in range(heads):
                at = slice(head * HEAD, (head + 1) * HEAD)
                query = qkv[0, head, block]
                raw = dot_nt(qkv[1, head, tile], query)
                prob = jnp.where(
                    seen, jnp.exp2(raw * shift - lse[block, head : head + 1]), 0.0
                )
                grad_prob = dot_nt(qkv[2, head, tile], tops[head])
                grad_score = (prob * (grad_prob - deltas[head])).astype(BF16)
                scores[tile, :, head * 256 + 128 : head * 256 + 128 + HEAD] += dot_nn(
                    prob.astype(BF16), tops[head]
                )
                scores[tile, :, head * 256 : head * 256 + HEAD] += dot_nn(grad_score, query)
                acc_t[at] += dot_nn(keys_t[tile, at], grad_score)
            return inner

        lax.fori_loop(0, block + 1, tiles, 0)
        projected[0, block] = (acc_t[...].T * scaling).astype(BF16)
        return carry

    lax.fori_loop(0, MEMBERS, block_back, 0)

    if wa_grads.shape[1] == width:
        blocks = [att_t[member] for member in range(MEMBERS)]

        def proj_grads(number, carry):
            at = pl.ds(pl.multiple_of(number * span, span), span)
            total = dot_nn(blocks[0], grad_all[0, :, at])
            for member in range(1, MEMBERS):
                total += dot_nn(blocks[member], grad_all[member, :, at])
            wa_grads[:, at] = total.astype(BF16)
            return carry

        lax.fori_loop(0, width // span, proj_grads, 0)
    else:

        def proj_grads(number, carry):
            at = pl.ds(pl.multiple_of(number * features, features), features)
            total = dot_nn(att_t[0], grad_all[0, :, at])
            for member in range(1, MEMBERS):
                total += dot_nn(att_t[member], grad_all[member, :, at])
            wa_grads[at] = total.astype(BF16)
            return carry

        lax.fori_loop(0, width // features, proj_grads, 0)
    advance(sum_proj)

    def settle_heads(block, carry):
        for head in range(heads):
            at = slice(head * HEAD, (head + 1) * HEAD)
            grad_keys = scores[block, :, head * 256 : head * 256 + HEAD] * scaling
            projected[1, block, :, at] = grad_keys.astype(BF16)
            grad_values = scores[block, :, head * 256 + 128 : head * 256 + 128 + HEAD]
            projected[2, block, :, at] = grad_values.astype(BF16)
        return carry

    lax.fori_loop(0, MEMBERS, settle_heads, 0)

    def finish_output(at):
        out_keep[at] = (resid[at] + scatter2.total(at)).astype(BF16)

    advance(*sum_out)

    def qkv_grads(kind, carry):
        to = pl.ds(pl.multiple_of(kind * width, width), width)
        left = normed[...].reshape(frame_count, width)
        right = projected[kind].reshape(frame_count, features)
        attn_grads[to] = dot_tn(left, right).astype(BF16)
        return carry

    for kind in range(3):
        lax.fori_loop(kind, kind + 1, qkv_grads, 0)
        done = (kind + 1) * count // 3
        advance(*sum_qkv[kind * count // 3 : done])
    scatter4 = Scatter(wire, place, part, near, joined, far_in, chunks)

    def inputs_back(step, carry):
        block = place.member(*swap_order(3 - step))

        total = dot_nt(projected[0, block], wq_m[0])
        total += dot_nt(projected[1, block], wq_m[1])
        total += dot_nt(projected[2, block], wq_m[2])
        part[block] = total.astype(BF16)

        @pl.when(step == 0)
        def _():
            scatter4.send_corner()

        @pl.when(step == 1)
        def _():
            scatter4.send_far()

        @pl.when(step == 2)
        def _():
            scatter4.send_near()

        return carry

    lax.fori_loop(0, MEMBERS, inputs_back, 0)

    scatter2.finish(finish_output)
    out_trade = wire.copy(out_keep, out_in, place.trade())
    when_swapped(out_trade.start)
    advance(sum_proj, *sum_out)
    advance(*sum_qkv[:2], *sum_qkv[2:], *sum_in)

    def finish_frames(at):
        grad = scatter4.total(at)
        values = x_keep[at].astype(F32)
        scale = lax.rsqrt(jnp.mean(values * values, axis=-1, keepdims=True) + EPSILON)
        gain_sum[1:2] += jnp.sum(grad * values * scale, axis=0, keepdims=True)
        scaled = grad * gain
        mean = jnp.mean(scaled * values, axis=-1, keepdims=True)
        total = grad_resid[at] + scale * scaled - values * (scale * scale * scale) * mean
        grad_frames[at] = total
        moved[at] = total.astype(BF16)

    frames_trades = []
    for number in range(chunks):
        at = pl.ds(number * half, half)
        frames_trades.append(wire.copy(moved.at[at], moved_in.at[at], place.trade()))

    scatter4.finish(finish_frames, lambda number: when_swapped(frames_trades[number].start))

    partners = [place.sibling(), place.across(), {"pair": 1 - place.pair}]
    partners += [place.column(bit) for bit in range(bits)]
    gain_trades = [
        wire.copy(gain_sum.at[pl.ds(8 * number, 8)], gain_got.at[number], partner)
        for number, partner in enumerate(partners)
    ]

    def gain_step(number):
        gain_trades[number].wait_recv()
        here = slice(8 * number, 8 * number + 8)
        gain_sum[8 * number + 8 : 8 * number + 16] = gain_sum[here] + gain_got[number]
        if number + 1 < len(gain_trades):
            gain_trades[number + 1].start()

    gain_trades[0].start()
    gain_chain = Steps([functools.partial(gain_step, n) for n in range(len(partners))])
    sums = sum_qkv + [sum_proj] + sum_in + sum_out
    early, late = sum_qkv[:2], sum_qkv[2:]
    advance(*early, sum_proj, *sum_out, *late, *sum_in, gain_chain)
    advance(*early, gain_chain, sum_proj, *late, gain_chain, *sum_in)
    advance(*early, sum_proj, *late, gain_chain)
    advance_all([gain_chain] + sums)
    gains_out[...] = gain_sum[8 * len(partners) : 8 * len(partners) + 8]

    @when_swapped
    def _():
        out_trade.wait_recv()
        output[...] = out_in[...]
        for one in frames_trades:
            one.wait_recv()
        grad_frames[...] = moved_in[...].astype(F32)
        for one in x_trades + frames_trades + [dy_trade, out_trade]:
            one.wait_send()
        for one in weights:
            one.drain()

    @when_stays
    def _():
        output[...] = out_keep[...]

    for one in (gather_dy, gather_n, gather_g, scatter2, scatter4):
        one.drain()
    first_trade.wait_send()
    for one in gain_trades:
        one.wait_send()
    for one in sums:
        one.finish()


def layer_call(bits, x_own, dy_own, lengths, gain_attn, gain_mlp, wq, wa, wi, wo):
    rows, width = x_own.shape
    features = wa.shape[0]
    heads = features // HEAD
    units = wi.shape[1]
    frames = MEMBERS * rows
    steps = 3 + bits
    members = (MEMBERS, rows, width)
    wa_shape = wa.shape if (features >> bits) % 16 == 0 else (width, features)
    block = pl.BlockSpec(memory_space=pltpu.VMEM)
    whole = pl.BlockSpec(memory_space=pl.ANY)
    outputs = [
        ((rows, width), BF16, block),
        ((rows, width), F32, block),
        ((width, units), BF16, whole),
        ((units, width), BF16, whole),
        ((3 * width, features), BF16, whole),
        (wa_shape, BF16, whole),
        ((8, width), F32, block),
    ]
    scratch = [
        (wq.shape, BF16),
        (wa.shape, BF16),
        (wi.shape, BF16),
        (wo.shape, BF16),
        (members, BF16),
        ((rows, width), BF16),
        (members, BF16),
        (members, BF16),
        (members, BF16),
        ((MEMBERS, rows, units), BF16),
        ((MEMBERS, rows, units), BF16),
        ((3, heads, MEMBERS, rows, HEAD), BF16),
        ((MEMBERS, features, rows), BF16),
        ((MEMBERS, features, rows), BF16),
        ((MEMBERS, features, rows), BF16),
        ((features, rows), F32),
        ((MEMBERS, 8, rows), F32),
        ((8, frames), jnp.int32),
        ((2, 8, frames), jnp.int32),
        ((MEMBERS, rows, max(heads * max(rows, 256), units)), F32),
    ]
    scatter = [(members, BF16), ((2, rows, width), BF16), ((rows, width), BF16),
               ((rows, width), BF16)]
    scratch += scatter * 2
    scratch += [
        ((rows, width), F32),
        ((rows, width), F32),
        ((width + units, width), BF16),
        ((width + units, width), BF16),
        ((3 * width, features), BF16),
        ((3 * width, features), BF16),
        (wa_shape, BF16),
        (wa_shape, BF16),
        ((3, MEMBERS, rows, features), BF16),
        ((8 * steps + 8, width), F32),
        ((steps, 8, width), F32),
    ]
    scratch += [((rows, width), BF16)] * 4
    count = 120 + 9 * (3 * bits + 2)
    return pl.pallas_call(
        functools.partial(layer_kernel, lengths.shape[1], bits),
        out_shape=[jax.ShapeDtypeStruct(shape, kind) for shape, kind, _ in outputs],
        in_specs=[whole, whole, pl.BlockSpec(memory_space=pltpu.SMEM), block, block]
        + [whole] * 4,
        out_specs=[spec for _, _, spec in outputs],
        scratch_shapes=[pltpu.VMEM(shape, kind) for shape, kind in scratch]
        + [
            pltpu.SemaphoreType.DMA((count,)),
            pltpu.SemaphoreType.DMA((count,)),
            pltpu.SemaphoreType.DMA((20,)),
        ],
        compiler_params=pltpu.CompilerParams(
            collective_id=0, has_side_effects=True, vmem_limit_bytes=VMEM_LIMIT
        ),
        name="layer",
    )(x_own, dy_own, lengths, gain_attn, gain_mlp, wq, wa, wi, wo)


def widen_kernel(*refs):
    count = (len(refs) - 3) // 2
    for source, target in zip(refs[:count], refs[count + 1 :]):
        target[...] = source[...].astype(target.dtype)
    for row, target in enumerate(refs[-2:]):
        target[...] = refs[count][row : row + 1]


def widen_call(arrays, kinds, gains, steps):
    specs = [
        pl.BlockSpec((array.shape[0] // steps, array.shape[1]), lambda step: (step, 0))
        for array in arrays
    ]
    moved = sum(array.size * (array.dtype.itemsize + 4) for array in arrays)
    return pl.pallas_call(
        widen_kernel,
        grid=(steps,),
        out_shape=[
            jax.ShapeDtypeStruct(array.shape, kind) for array, kind in zip(arrays, kinds)
        ]
        + [jax.ShapeDtypeStruct((1, gains.shape[1]), gains.dtype)] * 2,
        in_specs=specs + [pl.BlockSpec(gains.shape, lambda step: (0, 0))],
        out_specs=specs + [pl.BlockSpec((1, gains.shape[1]), lambda step: (0, 0))] * 2,
        cost_estimate=pl.CostEstimate(flops=0, bytes_accessed=moved, transcendentals=0),
        compiler_params=pltpu.CompilerParams(vmem_limit_bytes=VMEM_LIMIT),
        name="widen",
    )(*arrays, gains)


def per_device(bits, frames, lengths, wq, wa, wi, wo, gain_attn, gain_mlp, cotangent):
    width = frames.shape[1]
    features = wa.shape[0]
    output, grad_frames, in_sums, out_sums, qkv_sums, wa_sums, gains = layer_call(
        bits, frames, cotangent, lengths, gain_attn.reshape(1, width),
        gain_mlp.reshape(1, width), wq, wa, wi, wo,
    )
    output, grad_frames, in_sums, out_sums, qkv_sums, wa_sums, mlp_gain, attn_gain = widen_call(
        (output, grad_frames, in_sums, out_sums, qkv_sums, wa_sums),
        (output.dtype,) + (F32,) * 5, gains, WIDEN_STEPS,
    )
    if wa_sums.shape != wa.shape:
        turned = wa_sums.reshape(width // features, features, features)
        wa_sums = jnp.transpose(turned, (1, 0, 2)).reshape(features, width)
    return (
        output,
        grad_frames,
        qkv_sums.reshape(3, width, features),
        wa_sums,
        in_sums,
        out_sums,
        attn_gain.reshape(width),
        mlp_gain.reshape(width),
    )


def solution(mesh):
    batches = mesh.shape["dp"]
    bits = (batches // 2).bit_length() - 1
    inner = Mesh(mesh.devices.reshape(batches // 2, 2, 2, 2), AXES)
    dp, mp = ("col", "core"), ("pair", "zz")
    rows = P(dp + mp, None)
    weights = (P(None, None, mp), P(mp, None), P(None, mp), P(mp, None))
    return jax.shard_map(
        functools.partial(per_device, bits),
        mesh=inner,
        in_specs=(rows, P(dp, None)) + weights + (P(), P(), rows),
        out_specs=(rows, rows) + weights + (P(), P()),
        check_vma=False,
    )
```

```python
import functools
import math

import jax
import jax.numpy as jnp
from jax import lax
from jax.experimental import pallas as pl
from jax.experimental.pallas import tpu as pltpu
from jax.sharding import Mesh
from jax.sharding import PartitionSpec as P

HEAD = 64
EPSILON = 1e-06
NEGATIVE = -1e30
MEMBERS = 4
LOG2E = math.log2(math.e)
GELU_A = math.sqrt(2.0 / math.pi)
GELU_B = 0.044715
AXES = ("col", "core", "pair", "zz")
BF16 = jnp.bfloat16
F32 = jnp.float32
VMEM_LIMIT = 62 << 20
WIDEN_STEPS = 2
MESH_ID = pl.DeviceIdType.MESH


def dot_nn(a, b):
    return lax.dot_general(a, b, (((1,), (0,)), ((), ())), preferred_element_type=F32)


def dot_nt(a, b):
    return lax.dot_general(a, b, (((1,), (1,)), ((), ())), preferred_element_type=F32)


def dot_tn(a, b):
    return lax.dot_general(a, b, (((0,), (0,)), ((), ())), preferred_element_type=F32)


def flip(bit, amount):
    return bit + amount - 2 * bit * amount


class Place:
    def __init__(self):
        self.col = lax.axis_index("col")
        self.core = lax.axis_index("core")
        self.pair = lax.axis_index("pair")
        self.zz = lax.axis_index("zz")
        self.swapped = self.core != self.pair
        self.stays = self.core == self.pair
        self.me = self.member(0, 0)

    def member(self, other_core, other_chip):
        return 2 * flip(self.core, other_core) + flip(self.zz, other_chip)

    def sibling(self):
        return {"core": 1 - self.core}

    def across(self):
        return {"zz": 1 - self.zz}

    def trade(self):
        return {"pair": 1 - self.pair, "core": 1 - self.core}

    def column(self, bit):
        step = 1 << bit
        here = lax.rem(lax.div(self.col, step), 2)
        return {"col": self.col + step * (1 - 2 * here)}

    def columns(self):
        first, second = self.column(0)["col"], self.column(1)["col"]
        return [{"col": first + second - self.col}, {"col": first}, {"col": second}]


class Wire:
    def __init__(self, send_sems, recv_sems):
        self.send_sems = send_sems
        self.recv_sems = recv_sems
        self.used = 0

    def copy(self, src, dst, target, got=None):
        number = self.used
        self.used += 1
        return Transfer(
            src, dst, target, dst if got is None else got,
            self.send_sems.at[number], self.recv_sems.at[number],
        )


class Transfer:
    def __init__(self, src, dst, target, got, send_sem, recv_sem):
        self.args = (src, dst, target, got, send_sem, recv_sem)

    def start(self):
        src, dst, target, _, send_sem, recv_sem = self.args
        pltpu.make_async_remote_copy(
            src_ref=src, dst_ref=dst, send_sem=send_sem, recv_sem=recv_sem,
            device_id=target, device_id_type=MESH_ID,
        ).start()

    def wait_send(self):
        src, dst, target, _, send_sem, recv_sem = self.args
        pltpu.make_async_remote_copy(
            src_ref=src, dst_ref=dst, send_sem=send_sem, recv_sem=recv_sem,
            device_id=target, device_id_type=MESH_ID,
        ).wait_send()

    def wait_recv(self):
        _, _, target, got, send_sem, recv_sem = self.args
        pltpu.make_async_remote_copy(
            src_ref=got, dst_ref=got, send_sem=send_sem, recv_sem=recv_sem,
            device_id=target, device_id_type=MESH_ID,
        ).wait_recv()


def meet(targets):
    barrier = pltpu.get_barrier_semaphore()
    for target in targets:
        pl.semaphore_signal(barrier, inc=1, device_id=target, device_id_type=MESH_ID)
    pl.semaphore_wait(barrier, len(targets))


class Gather:
    def __init__(self, wire, place, whole, count=1):
        me, near = place.me, place.member(1, 0)
        far, corner = place.member(0, 1), place.member(1, 1)
        size = whole.shape[1] // count
        self.to_near, self.to_far, self.relay = [], [], []
        for number in range(count):
            at = pl.ds(number * size, size)
            mine, its, across, last = (whole.at[one, at] for one in (me, near, far, corner))
            self.to_near.append(wire.copy(mine, mine, place.sibling(), its))
            self.to_far.append(wire.copy(mine, mine, place.across(), across))
            self.relay.append(wire.copy(across, across, place.sibling(), last))

    def start(self, number=0):
        self.to_far[number].start()
        self.to_near[number].start()

    def take_near(self, number=0):
        self.to_near[number].wait_recv()

    def take_far(self, number=0):
        self.to_far[number].wait_recv()
        self.relay[number].start()

    def take_corner(self, number=0):
        self.relay[number].wait_recv()

    def drain(self):
        for one in self.to_near + self.to_far + self.relay:
            one.wait_send()


class Scatter:
    def __init__(self, wire, place, part, near_in, joined, far_in, count=1):
        self.place, self.part = place, part
        self.near_in, self.joined, self.far_in = near_in, joined, far_in
        corner, near = place.member(1, 1), place.member(1, 0)
        self.corner = wire.copy(part.at[corner], near_in.at[0], place.sibling())
        self.near = wire.copy(part.at[near], near_in.at[1], place.sibling())
        self.size = joined.shape[0] // count
        self.far = []
        for number in range(count):
            at = pl.ds(number * self.size, self.size)
            self.far.append(wire.copy(joined.at[at], far_in.at[at], place.across()))

    def send_corner(self):
        self.corner.start()

    def send_near(self):
        self.near.start()

    def send_far(self):
        self.corner.wait_recv()
        far = self.place.member(0, 1)

        def add(at):
            total = self.part[far, at].astype(F32) + self.near_in[0, at].astype(F32)
            self.joined[at] = total.astype(BF16)

        for number, one in enumerate(self.far):
            each_rows(self.size, 64, add, number * self.size)
            one.start()

    def finish(self, body, after=None):
        self.near.wait_recv()
        for number, one in enumerate(self.far):
            one.wait_recv()
            each_rows(self.size, 64, body, number * self.size)
            if after is not None:
                after(number)

    def total(self, at):
        return (
            self.part[self.place.me, at].astype(F32)
            + self.near_in[1, at].astype(F32)
            + self.far_in[at].astype(F32)
        )

    def drain(self):
        self.corner.wait_send()
        self.near.wait_send()
        for one in self.far:
            one.wait_send()


def window(start, size, unit=16):
    return pl.ds(pl.multiple_of(start, unit), size)


def each_rows(count, size, body, start=0):
    def step(number, carry):
        body(window(start + number * size, size))
        return carry

    lax.fori_loop(0, count // size, step, 0)


def add_rows(count, target, start, one, one_start, two, two_start):
    size = next(size for size in (128, 64, 48, 32, 16) if count % size == 0)

    def step(number, carry):
        moved = number * size
        total = (
            one[window(one_start + moved, size)].astype(F32)
            + two[window(two_start + moved, size)].astype(F32)
        )
        target[window(start + moved, size)] = total.astype(BF16)
        return carry

    lax.fori_loop(0, count // size, step, 0)


class Steps:
    def __init__(self, actions):
        self.actions = list(actions)

    def advance(self):
        if self.actions:
            self.actions.pop(0)()


def advance_all(chains):
    while any(chain.actions for chain in chains):
        for chain in chains:
            chain.advance()


class Reduce(Steps):
    def __init__(self, wire, place, source, start, slots, result, order, local_sem):
        self.place = place
        count, bits = slots.shape[0], len(order)
        here = [lax.rem(lax.div(place.col, 1 << bit), 2) for bit in order]
        offsets = [count - (count >> step) for step in range(bits + 1)]
        piece = count >> bits
        sends, keeps = [], []
        view, view_start = source, start
        for step, bit in enumerate(order):
            half = count >> (step + 1)
            away = view_start + (1 - here[step]) * half
            slot = slots.at[pl.ds(offsets[step], half)]
            sends.append(wire.copy(view.at[window(away, half)], slot, place.column(bit)))
            keeps.append((half, offsets[step], view, view_start + here[step] * half))
            view, view_start = slots, offsets[step]
        final = offsets[bits]
        last = pl.ds(offsets[bits - 1], piece)
        move = wire.copy(slots.at[last], slots.at[pl.ds(final, piece)], {"pair": 1 - place.pair})
        low = jnp.int32(0)
        for step in range(bits):
            low = low + here[step] * (count >> (step + 1))
        owned = result.at[window(low, piece)]
        keep_local = pltpu.make_async_copy(slots.at[pl.ds(final, piece)], owned, local_sem)
        whole = slots.at[pl.ds(final, piece)]
        shares = [wire.copy(whole, owned, place.sibling())]
        grows = []
        for step in reversed(range(bits)):
            size = count >> (step + 1)
            mine = result.at[window(low, size)]
            other_low = low + (1 - 2 * here[step]) * size
            other = result.at[window(other_low, size)]
            held = mine if grows else whole
            grows.append(wire.copy(held, mine, place.column(order[step]), other))
            shares.append(wire.copy(other, other, place.sibling()))
            low = low - here[step] * size

        def stays(action):
            pl.when(place.stays)(action)

        def swapped(action):
            pl.when(place.swapped)(action)

        def gather_half(step):
            size, offset, view, start = keeps[step]
            sends[step].wait_recv()
            add_rows(size, slots, offset, slots, offset, view, start)

        def narrow(step):
            gather_half(step)
            sends[step + 1].start()

        def cross():
            gather_half(bits - 1)
            swapped(move.start)

        def settle():
            @stays
            def _():
                move.wait_recv()
                add_rows(piece, slots, final, slots, final, slots, offsets[bits - 1])
                grows[0].start()
                shares[0].start()
                keep_local.start()

        def widen(step):
            @stays
            def _():
                grows[step].wait_recv()
                if step == 0:
                    keep_local.wait()
                if step + 1 < bits:
                    grows[step + 1].start()
                shares[step + 1].start()

        actions = [sends[0].start]
        actions += [functools.partial(narrow, step) for step in range(bits - 1)]
        actions += [cross, settle]
        actions += [functools.partial(widen, step) for step in range(bits)]
        super().__init__(actions)

        def finish():
            for one in sends:
                one.wait_send()

            @swapped
            def _():
                move.wait_send()
                for share in shares:
                    share.wait_recv()

            @stays
            def _():
                for one in grows + shares:
                    one.wait_send()

        self.finish = finish


class Weight:
    def __init__(self, wire, place, source, target, axis, start, size, local_sem):
        quarter = lax.rem(place.col, MEMBERS)
        depth = size // MEMBERS

        def cut(ref, first, many):
            at = window(start + first, many)
            return ref.at[:, at] if axis == 1 else ref.at[at]

        mine = cut(target, quarter * depth, depth)
        self.cross = wire.copy(cut(source, quarter * depth, depth), mine, place.trade())
        self.spread = []
        for other in place.columns():
            theirs = cut(target, lax.rem(other["col"], MEMBERS) * depth, depth)
            self.spread.append(wire.copy(mine, mine, other, theirs))
        self.local = pltpu.make_async_copy(cut(source, 0, size), cut(target, 0, size), local_sem)

    def bring(self):
        self.cross.start()

    def pass_on(self):
        self.cross.wait_recv()
        for one in self.spread:
            one.start()

    def ready(self):
        for one in self.spread:
            one.wait_recv()

    def drain(self):
        for one in [self.cross] + self.spread:
            one.wait_send()


def scatter_shapes(rows, width):
    return [
        pltpu.VMEM((MEMBERS, rows, width), BF16),
        pltpu.VMEM((2, rows, width), BF16),
        pltpu.VMEM((rows, width), BF16),
        pltpu.VMEM((rows, width), BF16),
    ]


def visible_tile(first_ref, block, tile, rows):
    key_at = tile * rows + lax.broadcasted_iota(jnp.int32, (rows, rows), 0)
    query_at = block * rows + lax.broadcasted_iota(jnp.int32, (rows, rows), 1)
    first = first_ref[0:1, pl.ds(pl.multiple_of(block * rows, rows), rows)]
    return (key_at >= first) & (key_at <= query_at)


def swap_order(step):
    return lax.rem(step, 2), lax.div(step, 2)


def layer_kernel(
    items,
    bits,
    x_own, dy_own, lengths, gain_attn, gain_mlp, wq, wa, wi, wo,
    output, grad_frames, in_sums, out_sums, qkv_sums, wa_sums, gains_out,
    wq_m, wa_m, wi_m, wo_m,
    x_all, x_keep, dy_all, normed, normed_mlp, active, grad_hidden,
    qkv, keys_t, values_t, att_t, acc_t, lse, first, first_near, scores,
    part, near, joined, far_in, outs, near2, joined2, far2,
    resid, grad_resid, mlp_grads, mlp_slots, attn_grads, attn_slots, wa_grads, wa_slots,
    projected, gain_sum, gain_got, moved, moved_in, out_keep, out_in,
    send_sems, recv_sems, local_sems,
):
    place = Place()
    wire = Wire(send_sems, recv_sems)
    rows, width = x_keep.shape
    heads = qkv.shape[1]
    features = heads * HEAD
    me = place.me
    frame_count = MEMBERS * rows
    hidden_units = wi.shape[1]
    span = rows
    shift = (HEAD ** -0.5) * LOG2E
    scaling = HEAD ** -0.5
    near_member = place.member(1, 0)

    def when_swapped(action):
        pl.when(place.swapped)(action)

    def when_stays(action):
        pl.when(place.stays)(action)

    chunks = 2
    half = rows // chunks
    x_trades = []
    for number in range(chunks):
        at = pl.ds(number * half, half)
        x_trades.append(
            wire.copy(x_own.at[at], x_all.at[near_member, at], place.trade(), x_all.at[me, at])
        )
    dy_trade = wire.copy(dy_own, dy_all.at[near_member], place.trade(), dy_all.at[me])
    first_trade = wire.copy(first_near.at[0], first_near.at[1], place.sibling())
    x_local = pltpu.make_async_copy(x_own, x_all.at[me], local_sems.at[0])
    dy_local = pltpu.make_async_copy(dy_own, dy_all.at[me], local_sems.at[1])

    def weight(number, source, target, axis, start, size):
        return Weight(wire, place, source, target, axis, start, size, local_sems.at[2 + number])

    def halves(number, source, target, axis):
        size = source.shape[axis] // 2
        return [
            weight(number + n, source, target, axis, n * size, size) for n in range(2)
        ]

    wq_parts = halves(0, wq, wq_m, 1)
    wi_parts = halves(2, wi, wi_m, 0)
    wo_parts = halves(4, wo, wo_m, 0)
    wa_part = weight(6, wa, wa_m, 0, 0, features)
    weights = wq_parts + [wa_part] + wi_parts + wo_parts

    meet(
        [place.sibling(), place.across(), place.trade(), {"pair": 1 - place.pair}]
        + place.columns()
        + [place.column(bit) for bit in range(2, bits)]
    )

    @when_swapped
    def _():
        for one in wq_parts:
            one.bring()
        for one in x_trades:
            one.start()
        wa_part.bring()

    @when_stays
    def _():
        x_local.start()
        dy_local.start()
        for one in weights:
            one.local.start()

    position = lax.broadcasted_iota(jnp.int32, (8, frame_count), 1)
    begin = jnp.zeros((8, frame_count), jnp.int32)
    end = jnp.int32(0)
    for item in range(items):
        size = lengths[0, item]
        end = end + size
        begin = begin + jnp.where(position >= end, size, 0)
    first_near[0] = jnp.where(position >= end, position, begin)
    first_trade.start()

    gather_x = Gather(wire, place, x_all, chunks)
    gather_dy = Gather(wire, place, dy_all)
    gather_n = Gather(wire, place, normed_mlp, chunks)
    grad_all = x_all
    slopes = scores
    gather_g = Gather(wire, place, grad_all, chunks)

    @when_swapped
    def _():
        for one in wq_parts:
            one.pass_on()
        for number in range(chunks):
            x_trades[number].wait_recv()
            gather_x.start(number)

    @when_stays
    def _():
        x_local.wait()
        for number in range(chunks):
            gather_x.start(number)
        dy_local.wait()
        gather_dy.start()

    gain = gain_attn[...]

    def norm_block(member):
        def some(at):
            values = x_all[member, at].astype(F32)
            scale = lax.rsqrt(jnp.mean(values * values, axis=-1, keepdims=True) + EPSILON)
            normed[member, at] = (values * scale * gain).astype(BF16)

        each_rows(rows, 64, some)

    def project(member):
        source = normed[member]
        for kind in range(3):
            block = dot_nn(source, wq_m[kind])
            narrow = block.astype(BF16)
            for head in range(heads):
                qkv[kind, head, member] = narrow[:, head * HEAD : (head + 1) * HEAD]
            if kind == 1:
                keys_t[member] = block.T.astype(BF16)
            if kind == 2:
                values_t[member] = block.T.astype(BF16)

    def arrive(step, carry):
        member = place.member(*swap_order(step))

        @pl.when(step == 1)
        def _():
            for number in range(chunks):
                gather_x.take_near(number)

        @pl.when(step == 2)
        def _():
            for number in range(chunks):
                gather_x.take_far(number)

            @when_swapped
            def _():
                for one in wi_parts:
                    one.bring()
                dy_trade.start()
                for one in wo_parts:
                    one.bring()

        @pl.when(step == 3)
        def _():
            for number in range(chunks):
                gather_x.take_corner(number)

        norm_block(member)

        @pl.when(step == 0)
        def _():
            for one in wq_parts:
                when_swapped(one.ready)
                when_stays(one.local.wait)

        @pl.when((step == 2) & place.swapped)
        def _():
            wa_part.pass_on()

        project(member)
        return carry

    lax.fori_loop(0, MEMBERS, arrive, 0)
    x_keep[...] = x_all[me]
    first_trade.wait_recv()

    @when_swapped
    def _():
        first[...] = first_near[1]

    @when_stays
    def _():
        first[...] = first_near[0]
        wa_part.local.wait()

    scatter1 = Scatter(wire, place, part, near, joined, far_in, chunks)

    def attend(step, carry):
        block = place.member(*swap_order(3 - step))

        def score(tile, peaks):
            seen = visible_tile(first, block, tile, rows)
            higher = []
            for head in range(heads):
                raw = dot_nt(qkv[1, head, tile], qkv[0, head, block])
                raw = jnp.where(seen, raw, NEGATIVE)
                scores[tile, :, head * rows : (head + 1) * rows] = raw
                higher.append(jnp.maximum(peaks[head], jnp.max(raw, axis=0, keepdims=True)))
            return tuple(higher)

        low = jnp.full((1, rows), NEGATIVE, F32)
        peaks = lax.fori_loop(0, block + 1, score, (low,) * heads)
        acc_t[...] = jnp.zeros_like(acc_t)

        def weigh(tile, totals):
            sums = []
            for head in range(heads):
                raw = scores[tile, :, head * rows : (head + 1) * rows]
                prob = jnp.exp2((raw - peaks[head]) * shift)
                sums.append(totals[head] + jnp.sum(prob, axis=0, keepdims=True))
                at = slice(head * HEAD, (head + 1) * HEAD)
                acc_t[at] += dot_nn(values_t[tile, at], prob.astype(BF16))
            return tuple(sums)

        none = jnp.zeros((1, rows), F32)
        totals = lax.fori_loop(0, block + 1, weigh, (none,) * heads)
        for head in range(heads):
            at = slice(head * HEAD, (head + 1) * HEAD)
            acc_t[at] = acc_t[at] / totals[head]
            lse[block, head : head + 1] = peaks[head] * shift + jnp.log2(totals[head])
        att_t[block] = acc_t[...].astype(BF16)

        @pl.when((step == 0) & place.swapped)
        def _():
            wa_part.ready()

        attended = acc_t[...].T.astype(BF16)
        part[block] = dot_nn(attended, wa_m[...]).astype(BF16)

        @pl.when(step == 0)
        def _():
            scatter1.send_corner()

        @pl.when(step == 1)
        def _():
            scatter1.send_far()

        @pl.when(step == 2)
        def _():
            scatter1.send_near()

        return carry

    lax.fori_loop(0, MEMBERS, attend, 0)

    @when_swapped
    def _():
        wi_parts[0].pass_on()
        wi_parts[1].pass_on()
        dy_trade.wait_recv()
        gather_dy.start()

    gain2 = gain_mlp[...]

    def add_resid(at):
        total = x_keep[at].astype(F32) + scatter1.total(at)
        resid[at] = total
        scale = lax.rsqrt(jnp.mean(total * total, axis=-1, keepdims=True) + EPSILON)
        normed_mlp[me, at] = (total * scale * gain2).astype(BF16)

    scatter1.finish(add_resid, gather_n.start)
    gather_dy.take_near()
    gather_x.drain()
    scatter1.drain()

    @when_swapped
    def _():
        for one in wi_parts:
            one.ready()

    @when_stays
    def _():
        for one in wi_parts + wo_parts:
            one.local.wait()

    scatter3 = Scatter(wire, place, part, near, joined, far_in, chunks)

    def feed_order(step):
        flip_core = jnp.where((step == 1) | (step == 2), 1, 0)
        flip_chip = jnp.where(step >= 2, 1, 0)
        return place.member(flip_core, flip_chip)

    def feed(step, carry):
        block = feed_order(step)

        @pl.when(step == 1)
        def _():
            for number in range(chunks):
                gather_n.take_near(number)

        @pl.when((step == 0) & place.swapped)
        def _():
            wo_parts[0].pass_on()

        @pl.when((step == 2) & place.swapped)
        def _():
            wo_parts[1].pass_on()

        @pl.when(step == 2)
        def _():
            gather_dy.take_far()
            for number in range(chunks):
                gather_n.take_far(number)
            for number in range(chunks):
                gather_n.take_corner(number)

        hidden = dot_nn(normed_mlp[block], wi_m[...])
        square = hidden * hidden
        bend = jnp.tanh(GELU_A * hidden * (1.0 + GELU_B * square))
        upper = 0.5 * (1.0 + bend)
        active[block] = (hidden * upper).astype(BF16)
        slopes[block] = upper + 0.5 * hidden * (1.0 - bend * bend) * (
            GELU_A * (1.0 + 3.0 * GELU_B * square)
        )
        return carry

    lax.fori_loop(0, MEMBERS, feed, 0)
    gather_dy.take_corner()
    ahead, back = tuple(range(bits)), tuple(reversed(range(bits)))
    used = [9]

    def advance(*chains):
        for chain in chains:
            chain.advance()

    def reduce(source, start, slots, slot_start, result, result_start, size, order):
        used[0] += 1
        return Reduce(
            wire, place, source, start, slots.at[pl.ds(slot_start, size)],
            result.at[pl.ds(result_start, size)], order, local_sems.at[used[0] - 1],
        )

    quarter = width // 2
    half_in, half_out = width // 2, hidden_units // 2
    sum_in = [
        reduce(
            mlp_grads, n * half_in, mlp_slots, n * half_in, in_sums, n * half_in, half_in, order
        )
        for n, order in enumerate((ahead, back))
    ]
    sum_out = [
        reduce(
            mlp_grads, width + n * half_out, mlp_slots, width + n * half_out,
            out_sums, n * half_out, half_out, order,
        )
        for n, order in enumerate((ahead, back))
    ]
    count = 4 if (3 * width // 4 >> bits) % 16 == 0 else 2
    split = 3 * width // count
    sum_qkv = [
        reduce(
            attn_grads, n * split, attn_slots, n * split, qkv_sums, n * split, split,
            back if n % 2 else ahead,
        )
        for n in range(count)
    ]
    sum_proj = reduce(wa_grads, 0, wa_slots, 0, wa_sums, 0, wa_grads.shape[0], ahead)

    def in_grads(number, carry):
        at = pl.ds(pl.multiple_of(number * span, span), span)
        left = normed_mlp[:, :, at].reshape(frame_count, span)
        right = grad_hidden[...].reshape(frame_count, hidden_units)
        mlp_grads[at] = dot_tn(left, right).astype(BF16)
        return carry

    def out_grads(number, carry):
        at = pl.ds(pl.multiple_of(number * span, span), span)
        down = pl.ds(pl.multiple_of(width + number * span, span), span)
        left = active[:, :, at].reshape(frame_count, span)
        right = dy_all[...].reshape(frame_count, width)
        mlp_grads[down] = dot_tn(left, right).astype(BF16)
        return carry

    tiles_here = hidden_units // span // 2
    for n in range(2):
        lax.fori_loop(n * tiles_here, (n + 1) * tiles_here, out_grads, 0)
        sum_out[n].advance()

    @when_swapped
    def _():
        for one in wo_parts:
            one.ready()

    def feed_back(step, carry):
        block = place.member(*swap_order(3 - step))

        grad_active = dot_nt(dy_all[block], wo_m[...])
        grad_hidden[block] = (grad_active * slopes[block]).astype(BF16)
        part[block] = dot_nt(grad_hidden[block], wi_m[...]).astype(BF16)

        @pl.when(step == 0)
        def _():
            scatter3.send_corner()

        @pl.when(step == 1)
        def _():
            scatter3.send_far()

        @pl.when(step == 2)
        def _():
            scatter3.send_near()

        return carry

    lax.fori_loop(0, MEMBERS, feed_back, 0)

    tiles_here = width // span // 2
    for n in range(2):
        lax.fori_loop(n * tiles_here, (n + 1) * tiles_here, in_grads, 0)
        sum_in[n].advance()

    def feed_out(block, carry):
        outs[block] = dot_nn(active[block], wo_m[...]).astype(BF16)
        return carry

    lax.fori_loop(0, MEMBERS, feed_out, 0)
    advance(*sum_out)
    scatter2 = Scatter(wire, place, outs, near2, joined2, far2)
    scatter2.send_corner()
    scatter2.send_near()
    gain_sum[...] = jnp.zeros_like(gain_sum)
    scores[...] = jnp.zeros_like(scores)

    def norm_back(at):
        grad = scatter3.total(at)
        values = resid[at]
        scale = lax.rsqrt(jnp.mean(values * values, axis=-1, keepdims=True) + EPSILON)
        gain_sum[0:1] += jnp.sum(grad * values * scale, axis=0, keepdims=True)
        scaled = grad * gain2
        mean = jnp.mean(scaled * values, axis=-1, keepdims=True)
        total = (
            dy_all[me, at].astype(F32) + scale * scaled - values * (scale * scale * scale) * mean
        )
        grad_resid[at] = total
        grad_all[me, at] = total.astype(BF16)

    scatter3.finish(norm_back, gather_g.start)
    scatter3.drain()
    scatter2.send_far()
    advance(*sum_out)

    def block_back(step, carry):
        block = place.member(*swap_order(step))

        @pl.when(step == 1)
        def _():
            for number in range(chunks):
                gather_g.take_near(number)
            advance(*sum_in)

        @pl.when(step == 2)
        def _():
            for number in range(chunks):
                gather_g.take_far(number)

        @pl.when(step == 3)
        def _():
            for number in range(chunks):
                gather_g.take_corner(number)
            advance(*sum_in)

        source = grad_all[block]
        top = dot_nt(source, wa_m[...]).astype(BF16)
        turned = dot_nt(wa_m[...], source).astype(BF16)
        tops = [top[:, head * HEAD : (head + 1) * HEAD] for head in range(heads)]
        product = turned.astype(F32) * att_t[block].astype(F32)
        deltas = [
            jnp.sum(product[head * HEAD : (head + 1) * HEAD], axis=0, keepdims=True)
            for head in range(heads)
        ]
        acc_t[...] = jnp.zeros_like(acc_t)

        def tiles(tile, inner):
            seen = visible_tile(first, block, tile, rows)
            for head in range(heads):
                at = slice(head * HEAD, (head + 1) * HEAD)
                query = qkv[0, head, block]
                raw = dot_nt(qkv[1, head, tile], query)
                prob = jnp.where(
                    seen, jnp.exp2(raw * shift - lse[block, head : head + 1]), 0.0
                )
                grad_prob = dot_nt(qkv[2, head, tile], tops[head])
                grad_score = (prob * (grad_prob - deltas[head])).astype(BF16)
                scores[tile, :, head * 256 + 128 : head * 256 + 128 + HEAD] += dot_nn(
                    prob.astype(BF16), tops[head]
                )
                scores[tile, :, head * 256 : head * 256 + HEAD] += dot_nn(grad_score, query)
                acc_t[at] += dot_nn(keys_t[tile, at], grad_score)
            return inner

        lax.fori_loop(0, block + 1, tiles, 0)
        projected[0, block] = (acc_t[...].T * scaling).astype(BF16)
        return carry

    lax.fori_loop(0, MEMBERS, block_back, 0)

    if wa_grads.shape[1] == width:
        blocks = [att_t[member] for member in range(MEMBERS)]

        def proj_grads(number, carry):
            at = pl.ds(pl.multiple_of(number * span, span), span)
            total = dot_nn(blocks[0], grad_all[0, :, at])
            for member in range(1, MEMBERS):
                total += dot_nn(blocks[member], grad_all[member, :, at])
            wa_grads[:, at] = total.astype(BF16)
            return carry

        lax.fori_loop(0, width // span, proj_grads, 0)
    else:

        def proj_grads(number, carry):
            at = pl.ds(pl.multiple_of(number * features, features), features)
            total = dot_nn(att_t[0], grad_all[0, :, at])
            for member in range(1, MEMBERS):
                total += dot_nn(att_t[member], grad_all[member, :, at])
            wa_grads[at] = total.astype(BF16)
            return carry

        lax.fori_loop(0, width // features, proj_grads, 0)
    advance(sum_proj)

    def settle_heads(block, carry):
        for head in range(heads):
            at = slice(head * HEAD, (head + 1) * HEAD)
            grad_keys = scores[block, :, head * 256 : head * 256 + HEAD] * scaling
            projected[1, block, :, at] = grad_keys.astype(BF16)
            grad_values = scores[block, :, head * 256 + 128 : head * 256 + 128 + HEAD]
            projected[2, block, :, at] = grad_values.astype(BF16)
        return carry

    lax.fori_loop(0, MEMBERS, settle_heads, 0)

    def finish_output(at):
        out_keep[at] = (resid[at] + scatter2.total(at)).astype(BF16)

    advance(*sum_out)

    def qkv_grads(kind, carry):
        to = pl.ds(pl.multiple_of(kind * width, width), width)
        left = normed[...].reshape(frame_count, width)
        right = projected[kind].reshape(frame_count, features)
        attn_grads[to] = dot_tn(left, right).astype(BF16)
        return carry

    for kind in range(3):
        lax.fori_loop(kind, kind + 1, qkv_grads, 0)
        done = (kind + 1) * count // 3
        advance(*sum_qkv[kind * count // 3 : done])
    scatter4 = Scatter(wire, place, part, near, joined, far_in, chunks)

    def inputs_back(step, carry):
        block = place.member(*swap_order(3 - step))

        total = dot_nt(projected[0, block], wq_m[0])
        total += dot_nt(projected[1, block], wq_m[1])
        total += dot_nt(projected[2, block], wq_m[2])
        part[block] = total.astype(BF16)

        @pl.when(step == 0)
        def _():
            scatter4.send_corner()

        @pl.when(step == 1)
        def _():
            scatter4.send_far()

        @pl.when(step == 2)
        def _():
            scatter4.send_near()

        return carry

    lax.fori_loop(0, MEMBERS, inputs_back, 0)

    scatter2.finish(finish_output)
    out_trade = wire.copy(out_keep, out_in, place.trade())
    when_swapped(out_trade.start)
    advance(sum_proj, *sum_out)
    advance(*sum_qkv[:2], *sum_qkv[2:], *sum_in)

    def finish_frames(at):
        grad = scatter4.total(at)
        values = x_keep[at].astype(F32)
        scale = lax.rsqrt(jnp.mean(values * values, axis=-1, keepdims=True) + EPSILON)
        gain_sum[1:2] += jnp.sum(grad * values * scale, axis=0, keepdims=True)
        scaled = grad * gain
        mean = jnp.mean(scaled * values, axis=-1, keepdims=True)
        total = grad_resid[at] + scale * scaled - values * (scale * scale * scale) * mean
        grad_frames[at] = total
        moved[at] = total.astype(BF16)

    frames_trades = []
    for number in range(chunks):
        at = pl.ds(number * half, half)
        frames_trades.append(wire.copy(moved.at[at], moved_in.at[at], place.trade()))

    scatter4.finish(finish_frames, lambda number: when_swapped(frames_trades[number].start))

    partners = [place.sibling(), place.across(), {"pair": 1 - place.pair}]
    partners += [place.column(bit) for bit in range(bits)]
    gain_trades = [
        wire.copy(gain_sum.at[pl.ds(8 * number, 8)], gain_got.at[number], partner)
        for number, partner in enumerate(partners)
    ]

    def gain_step(number):
        gain_trades[number].wait_recv()
        here = slice(8 * number, 8 * number + 8)
        gain_sum[8 * number + 8 : 8 * number + 16] = gain_sum[here] + gain_got[number]
        if number + 1 < len(gain_trades):
            gain_trades[number + 1].start()

    gain_trades[0].start()
    gain_chain = Steps([functools.partial(gain_step, n) for n in range(len(partners))])
    sums = sum_qkv + [sum_proj] + sum_in + sum_out
    early, late = sum_qkv[:2], sum_qkv[2:]
    advance(*early, sum_proj, *sum_out, *late, *sum_in, gain_chain)
    advance(*early, gain_chain, sum_proj, *late, gain_chain, *sum_in)
    advance(*early, sum_proj, *late, gain_chain)
    advance_all([gain_chain] + sums)
    gains_out[...] = gain_sum[8 * len(partners) : 8 * len(partners) + 8]

    @when_swapped
    def _():
        out_trade.wait_recv()
        output[...] = out_in[...]
        for one in frames_trades:
            one.wait_recv()
        grad_frames[...] = moved_in[...].astype(F32)
        for one in x_trades + frames_trades + [dy_trade, out_trade]:
            one.wait_send()
        for one in weights:
            one.drain()

    @when_stays
    def _():
        output[...] = out_keep[...]

    for one in (gather_dy, gather_n, gather_g, scatter2, scatter4):
        one.drain()
    first_trade.wait_send()
    for one in gain_trades:
        one.wait_send()
    for one in sums:
        one.finish()


def layer_call(bits, x_own, dy_own, lengths, gain_attn, gain_mlp, wq, wa, wi, wo):
    rows, width = x_own.shape
    features = wa.shape[0]
    heads = features // HEAD
    units = wi.shape[1]
    frames = MEMBERS * rows
    steps = 3 + bits
    members = (MEMBERS, rows, width)
    wa_shape = wa.shape if (features >> bits) % 16 == 0 else (width, features)
    block = pl.BlockSpec(memory_space=pltpu.VMEM)
    whole = pl.BlockSpec(memory_space=pl.ANY)
    outputs = [
        ((rows, width), BF16, block),
        ((rows, width), F32, block),
        ((width, units), BF16, whole),
        ((units, width), BF16, whole),
        ((3 * width, features), BF16, whole),
        (wa_shape, BF16, whole),
        ((8, width), F32, block),
    ]
    scratch = [
        (wq.shape, BF16),
        (wa.shape, BF16),
        (wi.shape, BF16),
        (wo.shape, BF16),
        (members, BF16),
        ((rows, width), BF16),
        (members, BF16),
        (members, BF16),
        (members, BF16),
        ((MEMBERS, rows, units), BF16),
        ((MEMBERS, rows, units), BF16),
        ((3, heads, MEMBERS, rows, HEAD), BF16),
        ((MEMBERS, features, rows), BF16),
        ((MEMBERS, features, rows), BF16),
        ((MEMBERS, features, rows), BF16),
        ((features, rows), F32),
        ((MEMBERS, 8, rows), F32),
        ((8, frames), jnp.int32),
        ((2, 8, frames), jnp.int32),
        ((MEMBERS, rows, max(heads * max(rows, 256), units)), F32),
    ]
    scatter = [(members, BF16), ((2, rows, width), BF16), ((rows, width), BF16),
               ((rows, width), BF16)]
    scratch += scatter * 2
    scratch += [
        ((rows, width), F32),
        ((rows, width), F32),
        ((width + units, width), BF16),
        ((width + units, width), BF16),
        ((3 * width, features), BF16),
        ((3 * width, features), BF16),
        (wa_shape, BF16),
        (wa_shape, BF16),
        ((3, MEMBERS, rows, features), BF16),
        ((8 * steps + 8, width), F32),
        ((steps, 8, width), F32),
    ]
    scratch += [((rows, width), BF16)] * 4
    count = 120 + 9 * (3 * bits + 2)
    return pl.pallas_call(
        functools.partial(layer_kernel, lengths.shape[1], bits),
        out_shape=[jax.ShapeDtypeStruct(shape, kind) for shape, kind, _ in outputs],
        in_specs=[whole, whole, pl.BlockSpec(memory_space=pltpu.SMEM), block, block]
        + [whole] * 4,
        out_specs=[spec for _, _, spec in outputs],
        scratch_shapes=[pltpu.VMEM(shape, kind) for shape, kind in scratch]
        + [
            pltpu.SemaphoreType.DMA((count,)),
            pltpu.SemaphoreType.DMA((count,)),
            pltpu.SemaphoreType.DMA((20,)),
        ],
        compiler_params=pltpu.CompilerParams(
            collective_id=0, has_side_effects=True, vmem_limit_bytes=VMEM_LIMIT
        ),
        name="layer",
    )(x_own, dy_own, lengths, gain_attn, gain_mlp, wq, wa, wi, wo)


def widen_kernel(*refs):
    count = (len(refs) - 3) // 2
    for source, target in zip(refs[:count], refs[count + 1 :]):
        target[...] = source[...].astype(target.dtype)
    for row, target in enumerate(refs[-2:]):
        target[...] = refs[count][row : row + 1]


def widen_call(arrays, kinds, gains, steps):
    specs = [
        pl.BlockSpec((array.shape[0] // steps, array.shape[1]), lambda step: (step, 0))
        for array in arrays
    ]
    moved = sum(array.size * (array.dtype.itemsize + 4) for array in arrays)
    return pl.pallas_call(
        widen_kernel,
        grid=(steps,),
        out_shape=[
            jax.ShapeDtypeStruct(array.shape, kind) for array, kind in zip(arrays, kinds)
        ]
        + [jax.ShapeDtypeStruct((1, gains.shape[1]), gains.dtype)] * 2,
        in_specs=specs + [pl.BlockSpec(gains.shape, lambda step: (0, 0))],
        out_specs=specs + [pl.BlockSpec((1, gains.shape[1]), lambda step: (0, 0))] * 2,
        cost_estimate=pl.CostEstimate(flops=0, bytes_accessed=moved, transcendentals=0),
        compiler_params=pltpu.CompilerParams(vmem_limit_bytes=VMEM_LIMIT),
        name="widen",
    )(*arrays, gains)


def per_device(bits, frames, lengths, wq, wa, wi, wo, gain_attn, gain_mlp, cotangent):
    width = frames.shape[1]
    features = wa.shape[0]
    output, grad_frames, in_sums, out_sums, qkv_sums, wa_sums, gains = layer_call(
        bits, frames, cotangent, lengths, gain_attn.reshape(1, width),
        gain_mlp.reshape(1, width), wq, wa, wi, wo,
    )
    output, grad_frames, in_sums, out_sums, qkv_sums, wa_sums, mlp_gain, attn_gain = widen_call(
        (output, grad_frames, in_sums, out_sums, qkv_sums, wa_sums),
        (output.dtype,) + (F32,) * 5, gains, WIDEN_STEPS,
    )
    if wa_sums.shape != wa.shape:
        turned = wa_sums.reshape(width // features, features, features)
        wa_sums = jnp.transpose(turned, (1, 0, 2)).reshape(features, width)
    return (
        output,
        grad_frames,
        qkv_sums.reshape(3, width, features),
        wa_sums,
        in_sums,
        out_sums,
        attn_gain.reshape(width),
        mlp_gain.reshape(width),
    )


def solution(mesh):
    batches = mesh.shape["dp"]
    bits = (batches // 2).bit_length() - 1
    inner = Mesh(mesh.devices.reshape(batches // 2, 2, 2, 2), AXES)
    dp, mp = ("col", "core"), ("pair", "zz")
    rows = P(dp + mp, None)
    weights = (P(None, None, mp), P(mp, None), P(None, mp), P(mp, None))
    return jax.shard_map(
        functools.partial(per_device, bits),
        mesh=inner,
        in_specs=(rows, P(dp, None)) + weights + (P(), P(), rows),
        out_specs=(rows, rows) + weights + (P(), P()),
        check_vma=False,
    )
```
